32 devices in a mesh: fsdp: 16 (over z, x, core), rep: 2 (over y).
Axes of the slice: x: 2, y: 2, z: 4, core: 2. Of those that a mesh axis runs over, the one named last changes fastest.
Arguments:
- tokens: bfloat16 [32768, 768], P(('fsdp', 'rep')), may hold values from -6 to 6
- w_qkv: bfloat16 [1769472], P('fsdp'), may hold values from -0.21875 to 0.21875
- w_out: bfloat16 [589824], P('fsdp'), may hold values from -0.875 to 0.875
- w_fc1: bfloat16 [2359296], P('fsdp'), may hold values from -0.21875 to 0.21875
- w_fc2: bfloat16 [2359296], P('fsdp'), may hold values from -0.109375 to 0.109375
- gains: bfloat16 [1536], P('fsdp'), may hold values from 0.099609375 to 1.8984375
- biases: bfloat16 [7680], P('fsdp'), may hold values from -3 to 3
- segment: int32 [32768], P(('fsdp', 'rep')), may hold values from 0 to 40, as said below
- cotangent: bfloat16 [32768, 768], P(('fsdp', 'rep')), may hold values from -6 to 6
Outputs:
- output: bfloat16 [32768, 768], P(('fsdp', 'rep'))
- grad_tokens: float32 [32768, 768], P(('fsdp', 'rep'))
- grad_qkv: float32 [1769472], P('fsdp')
- grad_out: float32 [589824], P('fsdp')
- grad_fc1: float32 [2359296], P('fsdp')
- grad_fc2: float32 [2359296], P('fsdp')
- grad_gains: float32 [1536], P('fsdp')
- grad_biases: float32 [7680], P('fsdp')
The draws below stay inside these ranges and needn't reach their ends.
Inputs may be any that keep to these rules, and one draw needn't show every extreme that they name: Within the 1024 tokens of one device, segment numbers start at 0, never fall and rise by at most one from token to token, so every image lies whole on one device. Every image but the last of a device has 25, 64 or 900 tokens; the last image of each device may be cut short by the device's end to as few as 1 token and is still a segment of its own. Some device holds an image of exactly 900 tokens, and some device holds only images of 25 tokens apart from its cut last one.
All inputs are finite; a program needn't handle non-finite values.
Results may differ from the reference program's by a relative error of at most 0.013.
Values may be sent and summed in bfloat16 or wider, within the bound.
No kernel may reach another device: no remote copies, remote signals or barrier semaphores. Data moves between devices by JAX's collectives and lax.ppermute only.
A program may use at most 192 MiB of HBM per device.

```python
import jax
import jax.numpy as jnp
from jax import lax

D = 768
H = 12
HD = 64
FF = 3072
TOK_DEV = 1024
MAXLEN = 900
IMG_A = 64
IMG_B = 25
TOKENS = 32768


def draw_segment(key, part):
    device_count = TOKENS // TOK_DEV
    candidates = TOK_DEV // IMG_B + 1
    key_pick, key_heavy, key_forced, key_light = jax.random.split(jax.random.fold_in(key, 17), 4)
    devices = jnp.arange(device_count, dtype=jnp.int32)
    forced = jax.random.randint(key_forced, (), 0, device_count)
    light = (forced + 1 + jax.random.randint(key_light, (), 0, device_count - 1)) % device_count
    picked = jax.random.randint(key_pick, (device_count, candidates), 0, 2)
    picked = jnp.where((devices == light)[:, None], 1, picked)
    lengths = jnp.where(picked == 0, IMG_A, IMG_B).astype(jnp.int32)
    heavy = jax.random.randint(key_heavy, (device_count,), 0, 8) == 0
    heavy = jnp.logical_or(heavy, devices == forced)
    heavy = jnp.logical_and(heavy, devices != light)
    first = jnp.where(heavy, MAXLEN, lengths[:, 0]).astype(jnp.int32)
    lengths = jnp.concatenate([first[:, None], lengths[:, 1:]], axis=1)
    ends = jnp.cumsum(lengths, axis=1)
    positions = jnp.arange(TOK_DEV, dtype=jnp.int32)
    passed = (ends[:, None, :] <= positions[None, :, None]).astype(jnp.int32)
    numbers = jnp.sum(passed, axis=-1)
    return numbers.reshape(-1).astype(jnp.int32)


def steps_of(rng, shape, shards, smallest, high):
    loudness, own = 1.0, jax.random.fold_in(rng, 6)
    for axis_at, parts in shards:
        draws = jnp.exp(jax.random.uniform(jax.random.fold_in(own, axis_at), (parts,), jnp.float32, smallest / len(shards), high / len(shards)))
        loudness = loudness * jnp.repeat(draws, shape[axis_at] // parts).reshape([-1 if axis == axis_at else 1 for axis in range(len(shape))])
    return loudness


def noise(stream_key, extent, width, bound, cuts=(), kind=jnp.bfloat16):
    level = steps_of(stream_key, extent, cuts, -0.22, 0.18) if cuts else 1.0
    entries = jax.random.normal(stream_key, extent, jnp.float32) * width * level
    return jnp.minimum(jnp.maximum(entries, -bound), bound).astype(kind)


def setup_inputs(seed: int = 0) -> dict:
    keys = jax.random.split(jax.random.key(seed), 10)
    tokens = noise(keys[0], (TOKENS, D), 1.0, 6.0, ((0, 32),))
    w_qkv = noise(keys[1], (3 * D * D,), D ** -0.5, 0.21875, ((0, 16),))
    w_out = noise(keys[2], (D * D,), (D // 16) ** -0.5, 0.875, ((0, 16),))
    w_fc1 = noise(keys[3], (D * FF,), D ** -0.5, 0.21875, ((0, 16),))
    w_fc2 = noise(keys[4], (FF * D,), FF ** -0.5, 0.109375, ((0, 16),))
    gains = jnp.clip(1.0 + 0.18 * jax.random.normal(keys[5], (2 * D,), jnp.float32), 0.099609375, 1.8984375).astype(jnp.bfloat16)
    biases = noise(keys[6], (6 * D + FF,), 0.5, 3.0, ((0, 16),))
    segment = draw_segment(jax.random.fold_in(keys[9], 71), 0)
    cotangent = noise(keys[8], (TOKENS, D), 1.0, 6.0, ((0, 32),))
    return {"tokens": tokens, "w_qkv": w_qkv, "w_out": w_out, "w_fc1": w_fc1, "w_fc2": w_fc2, "gains": gains, "biases": biases, "segment": segment, "cotangent": cotangent}


epsilon_norm = 1e-06
score_scale = 0.125
masked_low = -1e+30
highest = lax.Precision.HIGHEST

@jax.custom_vjp
def low(v):
    return lax.optimization_barrier(v.astype(jnp.bfloat16)).astype(jnp.float32)

@jax.custom_vjp
def low_back(v):
    return v

def low_keep(v):
    return (low(v), None)

def low_pass(kept, grad):
    return (grad,)

def back_keep(v):
    return (v, None)

def back_low(kept, grad):
    return (low(grad),)
low.defvjp(low_keep, low_pass)
low_back.defvjp(back_keep, back_low)

def normalize(values, gain, shift):
    center = values - lax.optimization_barrier(jnp.mean(values, axis=-1, keepdims=True))
    spread = lax.optimization_barrier(jnp.mean(center * center, axis=-1, keepdims=True))
    return center * lax.rsqrt(spread + epsilon_norm) * gain + shift

def gelu_exact(values):
    return jax.nn.gelu(values, approximate=False)

def unpack(gains, biases):
    return (gains[:D], gains[D:], biases[:D], biases[D:2 * D], biases[2 * D:3 * D], biases[3 * D:4 * D], biases[4 * D:5 * D], biases[5 * D:5 * D + FF], biases[5 * D + FF:])

def block_forward(tokens_blk, segment_blk, weight_qkv, weight_out, weight_up, weight_down, gains, biases):
    gain_one, gain_two, shift_one, bias_query, bias_value, bias_out, shift_two, bias_up, bias_down = unpack(gains, biases)
    row_count = tokens_blk.shape[0]
    normed = low(normalize(tokens_blk, gain_one, shift_one))
    projected = jnp.dot(normed, weight_qkv, precision=highest)
    queries = low(low_back(projected[:, :D] + bias_query))
    keys_all = low(low_back(projected[:, D:2 * D]))
    values_all = low(low_back(projected[:, 2 * D:] + bias_value))
    query_heads = queries.reshape(row_count, H, HD)
    key_heads = keys_all.reshape(row_count, H, HD)
    value_heads = values_all.reshape(row_count, H, HD)
    scores = jnp.einsum('qhd,khd->hqk', query_heads, key_heads, precision=highest) * score_scale
    scores = low_back(scores)
    same_image = segment_blk[:, None] == segment_blk[None, :]
    scores = jnp.where(same_image[None], scores, masked_low)
    probs = low(jax.nn.softmax(scores, axis=-1))
    attended = jnp.einsum('hqk,khd->qhd', probs, value_heads, precision=highest).reshape(row_count, D)
    attended = low(low_back(attended))
    branch = low_back(jnp.dot(attended, weight_out, precision=highest) + bias_out)
    middle = tokens_blk + branch
    normed_two = low(normalize(middle, gain_two, shift_two))
    hidden_pre = low_back(jnp.dot(normed_two, weight_up, precision=highest) + bias_up)
    activated = low(gelu_exact(hidden_pre))
    mixed = low_back(jnp.dot(activated, weight_down, precision=highest) + bias_down)
    return middle + mixed

def reference(tokens, w_qkv, w_out, w_fc1, w_fc2, gains, biases, segment, cotangent):
    segment_blocks = segment.reshape(-1, TOK_DEV)

    def forward(tokens_in, flat_qkv, flat_out, flat_up, flat_down, gains_in, biases_in):
        weight_qkv = flat_qkv.reshape(D, 3 * D)
        weight_out = flat_out.reshape(D, D)
        weight_up = flat_up.reshape(D, FF)
        weight_down = flat_down.reshape(FF, D)

        def one_block(pair):
            return block_forward(pair[0], pair[1], weight_qkv, weight_out, weight_up, weight_down, gains_in, biases_in)
        result = lax.map(jax.checkpoint(one_block), (tokens_in.reshape(-1, TOK_DEV, D), segment_blocks))
        return result.reshape(-1, D)
    output, pullback = jax.vjp(forward, tokens.astype(jnp.float32), w_qkv.astype(jnp.float32), w_out.astype(jnp.float32), w_fc1.astype(jnp.float32), w_fc2.astype(jnp.float32), gains.astype(jnp.float32), biases.astype(jnp.float32))
    grads = pullback(cotangent.astype(jnp.float32))
    return (output.astype(jnp.bfloat16), grads[0], grads[1], grads[2], grads[3], grads[4], grads[5], grads[6])
```

```python
import functools

import jax
import jax.numpy as jnp
from jax import lax
from jax.experimental import pallas as pl
from jax.experimental.pallas import tpu as pltpu
from jax.sharding import Mesh
from jax.sharding import PartitionSpec as P

D = 768
H = 12
HD = 64
FF = 3072
B16 = jnp.bfloat16
F32 = jnp.float32

epsilon_norm = 1e-06
score_scale = 0.125
masked_low = -1e30

FWD_GROUPS = (6, 6)
NZ, NX = 4, 2
ROWS = D // 16
ROWS2 = FF // 16
FSDP = ("z", "x", "core")


def mm(a, b, ca, cb):
    return lax.dot_general(a, b, (((ca,), (cb,)), ((), ())), preferred_element_type=F32)


def params(mib=56):
    return pltpu.CompilerParams(
        dimension_semantics=("arbitrary",), vmem_limit_bytes=mib * 1024 * 1024
    )


def cost(flops, nbytes, trans=0):
    return pl.CostEstimate(flops=int(flops), bytes_accessed=int(nbytes), transcendentals=int(trans))


def shape(dims, dtype):
    return jax.ShapeDtypeStruct(dims, dtype)


def layer_norm(values, gain, shift):
    center = values - jnp.mean(values, axis=-1, keepdims=True)
    spread = jnp.mean(center * center, axis=-1, keepdims=True)
    return center * lax.rsqrt(spread + epsilon_norm) * gain + shift


def layer_norm_back(values, gain, grad):
    center = values - jnp.mean(values, axis=-1, keepdims=True)
    spread = jnp.mean(center * center, axis=-1, keepdims=True)
    inverse = lax.rsqrt(spread + epsilon_norm)
    hat = center * inverse
    grad_hat = grad * gain
    grad_values = inverse * (
        grad_hat
        - jnp.mean(grad_hat, axis=-1, keepdims=True)
        - hat * jnp.mean(grad_hat * hat, axis=-1, keepdims=True)
    )
    return grad_values, jnp.sum(grad * hat, axis=0, keepdims=True), jnp.sum(grad, axis=0, keepdims=True)


def erf(x):
    x = jnp.clip(x, -3.7439211627767994, 3.7439211627767994)
    z = x * x
    top = 0.00022905065861350646
    for c in (0.0034082910107109506, 0.050955695062380861, 0.18520832239976145, 1.128379143519084):
        top = top * z + c
    low = -1.1791602954361697e-7
    for c in (
        0.000023547966471313185,
        0.0010179625278914885,
        0.014070470171167667,
        0.11098505178285362,
        0.49746925110067538,
        1.0,
    ):
        low = low * z + c
    return x * top / low


def block_of(tab, t):
    return tab[t]


def assemble(tab, mine, theirs, dest, rows):
    core = tab[8]
    for t in range(NZ * NX):
        base = tab[t] * 2
        dest[pl.ds(pl.multiple_of((base + core) * rows, 16), rows), :] = mine[t]
        dest[pl.ds(pl.multiple_of((base + 1 - core) * rows, 16), rows), :] = theirs[t]


def scatter(tab, source, own, send, rows):
    core = tab[8]
    for t in range(NZ * NX):
        base = tab[t] * 2
        own[t] = source[pl.ds(pl.multiple_of((base + core) * rows, 16), rows), :]
        send[t] = source[pl.ds(pl.multiple_of((base + 1 - core) * rows, 16), rows), :]


def qkv_body(first, tab, x_ref, mine, theirs, gain, shift, bias, *rest):
    if first:
        out_ref, h_ref, w_s = rest

        @pl.when(pl.program_id(0) == 0)
        def _():
            h_ref[...] = layer_norm(x_ref[...].astype(F32), gain[...], shift[...]).astype(B16)

        h = h_ref
    else:
        out_ref, w_s = rest
        h = x_ref
    assemble(tab, mine, theirs, w_s, ROWS)
    out_ref[0] = (mm(h[...], w_s[...], 1, 0) + bias[0]).astype(B16)


def qkv_call(first, tab, x, mine, theirs, gain, shift, bias):
    tokens = x.shape[0]
    width = mine.shape[2] // 3
    full = pl.BlockSpec((tokens, D), lambda j, t: (0, 0))
    row = pl.BlockSpec((1, D), lambda j, t: (0, 0))
    piece = pl.BlockSpec((8, ROWS, width), lambda j, t: (0, 0, j))
    outs = [shape((3, tokens, width), B16)]
    out_specs = [pl.BlockSpec((1, tokens, width), lambda j, t: (j, 0, 0))]
    if first:
        outs.append(shape((tokens, D), B16))
        out_specs.append(full)
    return pl.pallas_call(
        functools.partial(qkv_body, first),
        grid_spec=pltpu.PrefetchScalarGridSpec(
            num_scalar_prefetch=1,
            grid=(3,),
            in_specs=[full, piece, piece, row, row, pl.BlockSpec((1, 1, width), lambda j, t: (j, 0, 0))],
            out_specs=out_specs,
            scratch_shapes=[pltpu.VMEM((D, width), B16)],
        ),
        out_shape=outs,
        compiler_params=params(),
        cost_estimate=cost(6 * tokens * D * width, 8 * tokens * D),
        name="qkv_first" if first else "qkv_next",
    )(tab, x, mine, theirs, gain, shift, bias)


def make_mask(seg_ref, mask):
    @pl.when(pl.program_id(0) == 0)
    def _():
        row = seg_ref[...].astype(F32)
        mask[...] = jnp.where(row.T == row, 0.0, masked_low)


def attend_body(rows, q_ref, k_ref, v_ref, seg_ref, o_ref, lse_ref, mask):
    make_mask(seg_ref, mask)
    tokens = q_ref.shape[1]
    for h in range(2):
        cols = slice(h * HD, (h + 1) * HD)
        k = k_ref[0, :, cols]
        v = v_ref[0, :, cols]
        for b in range(tokens // rows):
            r = slice(b * rows, (b + 1) * rows)
            q = q_ref[0, r, cols] * jnp.asarray(score_scale, B16)
            s = mm(q, k, 1, 1) + mask[r, :]
            top = jnp.max(s, axis=-1, keepdims=True)
            p = jnp.exp(s - top)
            total = jnp.sum(p, axis=-1, keepdims=True)
            a = (p * (1.0 / total)).astype(B16)
            o_ref[r, cols] = mm(a, v, 1, 0).astype(B16)
            lse_ref[0, h : h + 1, r] = (top + jnp.log(total)).T


def attend_call(qkv, seg):
    _, tokens, width = qkv.shape
    pairs = width // 128
    head = lambda j: pl.BlockSpec((1, tokens, 128), lambda i: (j, 0, i))
    return pl.pallas_call(
        functools.partial(attend_body, min(512, tokens)),
        grid=(pairs,),
        in_specs=[head(0), head(1), head(2), pl.BlockSpec((1, tokens), lambda i: (0, 0))],
        out_specs=[
            pl.BlockSpec((tokens, 128), lambda i: (0, i)),
            pl.BlockSpec((1, 2, tokens), lambda i: (i, 0, 0)),
        ],
        out_shape=[shape((tokens, width), B16), shape((pairs, 2, tokens), F32)],
        scratch_shapes=[pltpu.VMEM((tokens, tokens), F32)],
        compiler_params=params(),
        cost_estimate=cost(pairs * 16 * 128 * tokens * tokens, 8 * tokens * width, pairs * 2 * tokens * tokens),
        name="attend",
    )(qkv, qkv, qkv, seg)


def up_body(split, tab, oa_ref, ob_ref, x_ref, mine, theirs, bo, gain, shift, c1, x1_ref, h2_ref, act_ref, slope_ref, wo, w1):
    @pl.when(pl.program_id(0) == 0)
    def _():
        core = tab[8]
        for t in range(NZ * NX):
            base = tab[t] * 2
            at = pl.ds(pl.multiple_of((base + core) * ROWS, 16), ROWS)
            wo[at, :] = mine[t, :, :D]
            w1[at, :] = mine[t, :, D:]
            at = pl.ds(pl.multiple_of((base + 1 - core) * ROWS, 16), ROWS)
            wo[at, :] = theirs[t, :, :D]
            w1[at, :] = theirs[t, :, D:]

    x1 = (
        x_ref[...].astype(F32)
        + (mm(oa_ref[...], wo[:split, :], 1, 0) + mm(ob_ref[...], wo[split:, :], 1, 0))
        + bo[...]
    )
    x1_ref[...] = x1
    h2 = layer_norm(x1, gain[...], shift[...]).astype(B16)
    h2_ref[...] = h2
    tile = 512
    for f in range(FF // tile):
        cols = slice(f * tile, (f + 1) * tile)
        u = mm(h2, w1[:, cols], 1, 0) + c1[:, cols]
        cdf = 0.5 + 0.5 * erf(u * 0.7071067811865476)
        act_ref[:, cols] = (u * cdf).astype(B16)
        slope_ref[:, cols] = (cdf + u * (jnp.exp(u * u * -0.5) * 0.3989422804014327)).astype(B16)


def up_call(tab, oa, ob, x, mine, theirs, bo, gain, shift, c1):
    tokens = x.shape[0]
    rows = min(256, tokens)
    split = oa.shape[1]
    block = lambda w: pl.BlockSpec((rows, w), lambda i, t: (i, 0))
    row = lambda w: pl.BlockSpec((1, w), lambda i, t: (0, 0))
    piece = pl.BlockSpec((8, ROWS, D + FF), lambda i, t: (0, 0, 0), pipeline_mode=pl.Buffered(1))
    return pl.pallas_call(
        functools.partial(up_body, split),
        grid_spec=pltpu.PrefetchScalarGridSpec(
            num_scalar_prefetch=1,
            grid=(tokens // rows,),
            in_specs=[block(split), block(D - split), block(D), piece, piece, row(D), row(D), row(D), row(FF)],
            out_specs=[block(D), block(D), block(FF), block(FF)],
            scratch_shapes=[pltpu.VMEM((D, D), B16), pltpu.VMEM((D, FF), B16)],
        ),
        out_shape=[shape((tokens, D), F32), shape((tokens, D), B16), shape((tokens, FF), B16), shape((tokens, FF), B16)],
        compiler_params=params(),
        cost_estimate=cost(2 * tokens * D * (D + FF), 30 * tokens * D, tokens * FF),
        name="up",
    )(tab, oa, ob, x, mine, theirs, bo, gain, shift, c1)


def down_body(tab, act_ref, slope_ref, dy_ref, x1_ref, mine, theirs, c2, out_ref, du_ref, own, send, dc1, dc2, acc, w2, dw2):
    step = pl.program_id(0)
    core = tab[8]

    @pl.when(step == 0)
    def _():
        acc[...] = x1_ref[...] + c2[...]
        dc2[...] = jnp.sum(dy_ref[...].astype(F32), axis=0, keepdims=True)

    for rx in range(NX):
        base = lax.rem(tab[rx * NZ], 2) * 2
        w2[pl.ds(pl.multiple_of((base + core) * ROWS2, 64), ROWS2), :] = mine[rx, 0]
        w2[pl.ds(pl.multiple_of((base + 1 - core) * ROWS2, 64), ROWS2), :] = theirs[rx, 0]
    act = act_ref[...]
    dy = dy_ref[...]
    w = w2[...]
    du = (mm(dy, w, 1, 1) * slope_ref[...].astype(F32)).astype(B16)
    du_ref[...] = du
    dc1[...] = jnp.sum(du.astype(F32), axis=0, keepdims=True)
    acc[...] += mm(act, w, 1, 0)
    dw2[...] = mm(act, dy, 0, 0).astype(B16)
    for rx in range(NX):
        base = lax.rem(tab[rx * NZ], 2) * 2
        own[rx, 0] = dw2[pl.ds(pl.multiple_of((base + core) * ROWS2, 64), ROWS2), :]
        send[rx, 0] = dw2[pl.ds(pl.multiple_of((base + 1 - core) * ROWS2, 64), ROWS2), :]

    @pl.when(step == NZ - 1)
    def _():
        out_ref[...] = acc[...].astype(B16)


def down_call(tab, act, slope, dy, x1, mine, theirs, c2):
    tokens = dy.shape[0]
    width = FF // NZ
    full = pl.BlockSpec((tokens, D), lambda i, t: (0, 0))
    ff = pl.BlockSpec((tokens, width), lambda i, t: (0, t[i] // 2))
    piece = pl.BlockSpec((NX, 1, ROWS2, D), lambda i, t: (0, i, 0, 0))
    row = pl.BlockSpec((1, D), lambda i, t: (0, 0))
    pieces = shape((NX, NZ, ROWS2, D), B16)
    return pl.pallas_call(
        down_body,
        grid_spec=pltpu.PrefetchScalarGridSpec(
            num_scalar_prefetch=1,
            grid=(NZ,),
            in_specs=[ff, ff, full, full, piece, piece, row],
            out_specs=[full, ff, piece, piece, pl.BlockSpec((1, width), lambda i, t: (0, t[i] // 2)), row],
            scratch_shapes=[pltpu.VMEM((tokens, D), F32), pltpu.VMEM((width, D), B16), pltpu.VMEM((width, D), B16)],
        ),
        out_shape=[
            shape((tokens, D), B16),
            shape((tokens, FF), B16),
            pieces,
            pieces,
            shape((1, FF), F32),
            shape((1, D), F32),
        ],
        compiler_params=params(),
        cost_estimate=cost(6 * tokens * D * FF, 40 * tokens * D),
        name="down",
    )(tab, act, slope, dy, x1, mine.reshape(NX, NZ, ROWS2, D), theirs.reshape(NX, NZ, ROWS2, D), c2)


def middle_body(split, tab, h2_ref, du_ref, dy_ref, x1_ref, oa_ref, ob_ref, mine, theirs, gain, dx_ref, do_ref, own, send, dvec, acc, w_s, dw):
    step = pl.program_id(0)

    @pl.when(step == 0)
    def _():
        acc[...] = jnp.zeros_like(acc)

    assemble(tab, mine, theirs, w_s, ROWS)

    @pl.when(step < NZ)
    def _():
        du = du_ref[...]
        dw[...] = mm(h2_ref[...], du, 0, 0).astype(B16)
        acc[...] += mm(du, w_s[...], 1, 1)

    @pl.when(step == NZ)
    def _():
        grad, dgain, dshift = layer_norm_back(x1_ref[...], gain[...], acc[...])
        dx = dy_ref[...].astype(F32) + grad
        dx_ref[...] = dx
        da = dx.astype(B16)
        dvec[0:1, :] = dgain
        dvec[1:2, :] = dshift
        dvec[2:3, :] = jnp.sum(da.astype(F32), axis=0, keepdims=True)
        do_ref[...] = mm(da, w_s[...], 1, 1).astype(B16)
        dw[:split, :] = mm(oa_ref[...], da, 0, 0).astype(B16)
        dw[split:, :] = mm(ob_ref[...], da, 0, 0).astype(B16)

    scatter(tab, dw, own, send, ROWS)


def middle_call(tab, h2, du, dy, x1, oa, ob, mine, theirs, gain):
    tokens = dy.shape[0]
    split = oa.shape[1]
    full = lambda w: pl.BlockSpec((tokens, w), lambda i, t: (0, 0), pipeline_mode=pl.Buffered(1))
    out_full = pl.BlockSpec((tokens, D), lambda i, t: (0, 0))
    piece = pl.BlockSpec((8, ROWS, D), lambda i, t: (0, 0, lax.rem(i + 1, NZ + 1)))
    pieces = shape((8, ROWS, D + FF), B16)
    return pl.pallas_call(
        functools.partial(middle_body, split),
        grid_spec=pltpu.PrefetchScalarGridSpec(
            num_scalar_prefetch=1,
            grid=(NZ + 1,),
            in_specs=[
                full(D),
                pl.BlockSpec((tokens, D), lambda i, t: (0, jnp.minimum(i, NZ - 1))),
                full(D),
                full(D),
                full(split),
                full(D - split),
                piece,
                piece,
                pl.BlockSpec((1, D), lambda i, t: (0, 0)),
            ],
            out_specs=[out_full, out_full, piece, piece, pl.BlockSpec((8, D), lambda i, t: (0, 0))],
            scratch_shapes=[pltpu.VMEM((tokens, D), F32), pltpu.VMEM((D, D), B16), pltpu.VMEM((D, D), B16)],
        ),
        out_shape=[shape((tokens, D), F32), shape((tokens, D), B16), pieces, pieces, shape((8, D), F32)],
        compiler_params=params(),
        cost_estimate=cost(4 * tokens * D * (D + FF), 40 * tokens * D),
        name="middle",
    )(tab, h2, du, dy, x1, oa, ob, mine, theirs, gain)


def attend_back_body(rows, q_ref, k_ref, v_ref, do_ref, o_ref, lse_ref, seg_ref, out_ref, mask):
    make_mask(seg_ref, mask)
    tokens = q_ref.shape[1]
    for h in range(2):
        cols = slice(h * HD, (h + 1) * HD)
        k = k_ref[0, :, cols]
        v = v_ref[0, :, cols]
        dk = jnp.zeros((HD, tokens), F32)
        dv = jnp.zeros((HD, tokens), F32)
        for b in range(tokens // rows):
            r = slice(b * rows, (b + 1) * rows)
            q = q_ref[0, r, cols] * jnp.asarray(score_scale, B16)
            do = do_ref[r, cols]
            centre = jnp.sum(do.astype(F32) * o_ref[r, cols].astype(F32), axis=1, keepdims=True)
            s = mm(q, k, 1, 1) + mask[r, :]
            p = jnp.exp(s - lse_ref[0, h : h + 1, r].T)
            da = mm(do, v, 1, 1)
            ds = (p * (da - centre)).astype(B16)
            dv = dv + mm(do.T, p.astype(B16), 1, 0)
            dk = dk + mm(q.T, ds, 1, 0)
            out_ref[0, r, cols] = (mm(ds, k, 1, 0) * score_scale).astype(B16)
        out_ref[1, :, cols] = dk.T.astype(B16)
        out_ref[2, :, cols] = dv.T.astype(B16)


def attend_back_call(qkv, do, o, lse, seg, first_pair):
    _, tokens, width = qkv.shape
    pairs = width // 128
    head = lambda j: pl.BlockSpec((1, tokens, 128), lambda i: (j, 0, i))
    return pl.pallas_call(
        functools.partial(attend_back_body, min(512, tokens)),
        grid=(pairs,),
        in_specs=[
            head(0),
            head(1),
            head(2),
            pl.BlockSpec((tokens, 128), lambda i: (0, i + first_pair)),
            pl.BlockSpec((tokens, 128), lambda i: (0, i)),
            pl.BlockSpec((1, 2, tokens), lambda i: (i, 0, 0)),
            pl.BlockSpec((1, tokens), lambda i: (0, 0)),
        ],
        out_specs=pl.BlockSpec((3, tokens, 128), lambda i: (0, 0, i)),
        out_shape=shape((3, tokens, width), B16),
        scratch_shapes=[pltpu.VMEM((tokens, tokens), F32)],
        compiler_params=params(),
        cost_estimate=cost(pairs * 40 * 128 * tokens * tokens, 16 * tokens * width, pairs * 2 * tokens * tokens),
        name="attend_back",
    )(qkv, qkv, qkv, do, o, lse, seg)


def weight_body(tab, h_ref, d_ref, own, send, dbias, dw):
    d = d_ref[0]
    dbias[0] = jnp.sum(d.astype(F32), axis=0, keepdims=True)
    dw[...] = mm(h_ref[...], d, 0, 0).astype(B16)
    scatter(tab, dw, own, send, ROWS)


def weight_call(tab, h1, dqkv):
    _, tokens, width = dqkv.shape
    piece = pl.BlockSpec((8, ROWS, width), lambda j, t: (0, 0, j))
    pieces = shape((8, ROWS, 3 * width), B16)
    return pl.pallas_call(
        weight_body,
        grid_spec=pltpu.PrefetchScalarGridSpec(
            num_scalar_prefetch=1,
            grid=(3,),
            in_specs=[
                pl.BlockSpec((tokens, D), lambda j, t: (0, 0)),
                pl.BlockSpec((1, tokens, width), lambda j, t: (j, 0, 0)),
            ],
            out_specs=[piece, piece, pl.BlockSpec((1, 1, width), lambda j, t: (j, 0, 0))],
            scratch_shapes=[pltpu.VMEM((D, width), B16)],
        ),
        out_shape=[pieces, pieces, shape((3, 1, width), F32)],
        compiler_params=params(),
        cost_estimate=cost(6 * tokens * D * width, 12 * tokens * width),
        name="qkv_weight",
    )(tab, h1, dqkv)


def input_body(tab, da_ref, db_ref, x_ref, dx_ref, ma, ta, mb, tb, gain, out_ref, dvec, wa, wb):
    step = pl.program_id(0)

    @pl.when(step == 0)
    def _():
        assemble(tab, ma, ta, wa, ROWS)
        assemble(tab, mb, tb, wb, ROWS)
        dvec[...] = jnp.zeros_like(dvec)

    dh = None
    for d_ref, w in ((da_ref, wa), (db_ref, wb)):
        width = d_ref.shape[2]
        for j in range(3):
            term = mm(d_ref[j], w[:, j * width : (j + 1) * width], 1, 1)
            dh = term if dh is None else dh + term
    grad, dgain, dshift = layer_norm_back(x_ref[...].astype(F32), gain[...], dh)
    out_ref[...] = dx_ref[...] + grad
    dvec[0:1, :] += dgain
    dvec[1:2, :] += dshift


def input_call(tab, da, db, x, dx, ma, ta, mb, tb, gain):
    tokens = x.shape[0]
    rows = min(256, tokens)
    wa, wb = da.shape[2], db.shape[2]
    grads = lambda w: pl.BlockSpec((3, rows, w), lambda i, t: (0, i, 0))
    block = pl.BlockSpec((rows, D), lambda i, t: (i, 0))
    piece = lambda w: pl.BlockSpec((8, ROWS, 3 * w), lambda i, t: (0, 0, 0), pipeline_mode=pl.Buffered(1))
    return pl.pallas_call(
        input_body,
        grid_spec=pltpu.PrefetchScalarGridSpec(
            num_scalar_prefetch=1,
            grid=(tokens // rows,),
            in_specs=[
                grads(wa),
                grads(wb),
                block,
                block,
                piece(wa),
                piece(wa),
                piece(wb),
                piece(wb),
                pl.BlockSpec((1, D), lambda i, t: (0, 0)),
            ],
            out_specs=[block, pl.BlockSpec((8, D), lambda i, t: (0, 0))],
            scratch_shapes=[pltpu.VMEM((D, 3 * wa), B16), pltpu.VMEM((D, 3 * wb), B16)],
        ),
        out_shape=[shape((tokens, D), F32), shape((8, D), F32)],
        compiler_params=params(),
        cost_estimate=cost(6 * tokens * D * D, 20 * tokens * D),
        name="input_grad",
    )(tab, da, db, x, dx, ma, ta, mb, tb, gain)


def add_core_body(a, b, keep, send):
    keep[0] = (a[0, 0].astype(F32) + b[0, 0].astype(F32)).astype(B16)
    send[0] = (a[1, 0].astype(F32) + b[1, 0].astype(F32)).astype(B16)


def add_core(own, received):
    _, r, w = own.shape
    both = pl.BlockSpec((NX, 1, r, w), lambda i: (0, i, 0, 0))
    one = pl.BlockSpec((1, r, w), lambda i: (i, 0, 0))
    return pl.pallas_call(
        add_core_body,
        grid=(NZ,),
        in_specs=[both, both],
        out_specs=[one, one],
        out_shape=[shape((NZ, r, w), B16)] * 2,
        compiler_params=params(),
        cost_estimate=cost(8 * r * w, 48 * r * w),
        name="add_core",
    )(own.reshape(NX, NZ, r, w), received.reshape(NX, NZ, r, w))


def add_x_body(a, b, *outs):
    for i, out in enumerate(outs):
        out[...] = (a[i].astype(F32) + b[i].astype(F32)).astype(B16)


def add_x(keep, received):
    _, r, w = keep.shape
    return pl.pallas_call(
        add_x_body,
        out_shape=[shape((r, w), B16)] * NZ,
        compiler_params=pltpu.CompilerParams(vmem_limit_bytes=32 * 1024 * 1024),
        cost_estimate=cost(4 * r * w, 24 * r * w),
        name="add_x",
    )(keep, received)


def add_z_body(a, b, c, d, out):
    out[...] = ((a[...].astype(F32) + b[...].astype(F32)) + (c[...].astype(F32) + d[...].astype(F32))).astype(B16)


def add_z(parts):
    return pl.pallas_call(
        add_z_body,
        out_shape=shape(parts[0].shape, B16),
        compiler_params=pltpu.CompilerParams(vmem_limit_bytes=32 * 1024 * 1024),
        cost_estimate=cost(4 * parts[0].size, 10 * parts[0].size),
        name="add_z",
    )(*parts)


def flip(value, axis, size, by):
    return lax.ppermute(value, axis, [(i, i ^ by) for i in range(size)])


def gather_blocks(shard):
    along = jnp.stack([shard] + [flip(shard, "z", NZ, by) for by in range(1, NZ)])
    mine = jnp.concatenate([along, flip(along, "x", NX, 1)])
    return mine, flip(mine, "core", 2, 1)


def reduce_blocks(own, send):
    keep, out = add_core(own, flip(send, "core", 2, 1))
    parts = add_x(keep, flip(out, "x", NX, 1))
    total = add_z([parts[0]] + [flip(parts[by], "z", NZ, by) for by in range(1, NZ)])
    return total.astype(F32) + flip(total, "rep", 2, 1).astype(F32)


def gather_any(shard):
    whole = lax.all_gather(shard, FSDP, axis=0, tiled=True)
    blocks = whole.reshape(NZ, NX, 2, -1, whole.shape[1]).transpose(2, 1, 0, 3, 4)
    blocks = blocks.reshape(2, NZ * NX, -1, whole.shape[1])
    return blocks[0], blocks[1]


def reduce_any(own, send):
    blocks = jnp.stack([own, send]).reshape(2, NX, NZ, *own.shape[1:]).transpose(2, 1, 0, 3, 4)
    whole = blocks.reshape(-1, own.shape[2])
    part = lax.psum_scatter(whole, FSDP, scatter_dimension=0, tiled=True)
    return lax.psum(part, "rep").astype(F32)


def shards(tokens, w_qkv, w_out, w_fc1, w_fc2, gains, biases, segment, cotangent):
    nz, nx = lax.axis_size("z"), lax.axis_size("x")
    count = nz * nx * 2
    grid = (nz, nx, lax.axis_size("core"), lax.axis_size("rep")) == (NZ, NX, 2, 2)
    gather, reduce = (gather_blocks, reduce_blocks) if grid else (gather_any, reduce_any)
    if grid:
        mz, mx, core = lax.axis_index("z"), lax.axis_index("x"), lax.axis_index("core")
    else:
        mz, mx, core = 0, 0, 0
    tab = jnp.stack(
        [jnp.asarray((mz ^ rz) * NX + (mx ^ rx), jnp.int32) for rx in range(NX) for rz in range(NZ)]
        + [jnp.asarray(core, jnp.int32)]
    )
    seg = segment.reshape(1, -1)

    shard_qkv = w_qkv.reshape(-1, 3 * D)
    bounds = []
    at = 0
    for heads in FWD_GROUPS:
        bounds.append((at * HD, (at + heads) * HD))
        at += heads
    qkv_shards = [
        jnp.concatenate([shard_qkv[:, part * D + a : part * D + b] for part in range(3)], axis=1)
        for a, b in bounds
    ]
    qkv_pieces = [gather(s) for s in qkv_shards]
    vec = jnp.concatenate([gains, biases])
    vec = lax.all_to_all(
        jnp.broadcast_to(vec[None], (count, vec.shape[0])), FSDP, split_axis=0, concat_axis=0, tiled=True
    ).astype(F32)
    ngain = gains.shape[0]
    gains_all = vec[:, :ngain].reshape(1, -1)
    biases_all = vec[:, ngain:].reshape(1, -1)
    gain_one, gain_two = gains_all[:, :D], gains_all[:, D:]
    shift_one, bias_q, bias_v, bias_o, shift_two = [biases_all[:, i * D : (i + 1) * D] for i in range(5)]
    bias_up, bias_down = biases_all[:, 5 * D : 5 * D + FF], biases_all[:, 5 * D + FF :]
    shard_up = jnp.concatenate([w_out.reshape(-1, D), w_fc1.reshape(-1, FF)], axis=1)
    up_mine, up_theirs = gather(shard_up)
    down_mine, down_theirs = gather(w_fc2.reshape(-1, D))

    qkv, outs, lses = [], [], []
    h1 = None
    for g, (a, b) in enumerate(bounds):
        bias = jnp.stack([bias_q[:, a:b], jnp.zeros((1, b - a), F32), bias_v[:, a:b]])
        mine, theirs = qkv_pieces[g]
        if g == 0:
            proj, h1 = qkv_call(True, tab, tokens, mine, theirs, gain_one, shift_one, bias)
        else:
            (proj,) = qkv_call(False, tab, h1, mine, theirs, gain_one, shift_one, bias)
        o, lse = attend_call(proj, seg)
        qkv.append(proj)
        outs.append(o)
        lses.append(lse)
    x1, h2, act, slope = up_call(
        tab, outs[0], outs[1], tokens, up_mine, up_theirs, bias_o, gain_two, shift_two, bias_up
    )
    output, du, own2, send2, dc1, dc2 = down_call(
        tab, act, slope, cotangent, x1, down_mine, down_theirs, bias_down
    )
    grad_fc2 = reduce(own2.reshape(8, ROWS2, D), send2.reshape(8, ROWS2, D))
    dx1, do, own1, send1, dmid = middle_call(
        tab, h2, du, cotangent, x1, outs[0], outs[1], up_mine, up_theirs, gain_two
    )
    grad_up = reduce(own1, send1)
    dqkv, grads, dbias = [], [], []
    for g, (a, b) in enumerate(bounds):
        d = attend_back_call(qkv[g], do, outs[g], lses[g], seg, a // 128)
        own, send, db = weight_call(tab, h1, d)
        grads.append(reduce(own, send))
        dqkv.append(d)
        dbias.append(db)
    grad_tokens, din = input_call(
        tab, dqkv[0], dqkv[1], tokens, dx1, *qkv_pieces[0], *qkv_pieces[1], gain_one
    )
    dgains = jnp.concatenate([din[0], dmid[0]])
    dbiases = jnp.concatenate(
        [
            din[1],
            jnp.concatenate([db[0, 0] for db in dbias]),
            jnp.concatenate([db[2, 0] for db in dbias]),
            dmid[2],
            dmid[1],
            dc1[0],
            dc2[0],
        ]
    )
    small = jnp.concatenate([dgains.reshape(count, -1), dbiases.reshape(count, -1)], axis=1)
    reps = lax.axis_size("rep")
    small = jnp.broadcast_to(small[:, None], (count, reps, small.shape[1])).reshape(count * reps, -1)
    small = lax.all_to_all(small, FSDP + ("rep",), split_axis=0, concat_axis=0, tiled=True)
    small = jnp.sum(small, axis=0)
    widths = [b - a for a, b in bounds]
    grad_qkv = jnp.concatenate(
        [g[:, part * w : (part + 1) * w] for part in range(3) for g, w in zip(grads, widths)], axis=1
    )
    return (
        output,
        grad_tokens,
        grad_qkv.reshape(-1),
        grad_up[:, :D].reshape(-1),
        grad_up[:, D:].reshape(-1),
        grad_fc2.reshape(-1),
        small[:ngain],
        small[ngain:],
    )


def solution(mesh):
    count, reps = mesh.shape["fsdp"], mesh.shape["rep"]
    inner = Mesh(mesh.devices.reshape(count // 4, 2, 2, reps), FSDP + ("rep",))
    rows = P(FSDP + ("rep",), None)
    flat = P(FSDP)
    return jax.shard_map(
        shards,
        mesh=inner,
        in_specs=(rows, flat, flat, flat, flat, flat, flat, P(FSDP + ("rep",)), rows),
        out_specs=(rows, rows, flat, flat, flat, flat, flat, flat),
        check_vma=False,
    )
```

```python
import functools

import jax
import jax.numpy as jnp
from jax import lax
from jax.experimental import pallas as pl
from jax.experimental.pallas import tpu as pltpu
from jax.sharding import Mesh
from jax.sharding import PartitionSpec as P

D = 768
H = 12
HD = 64
FF = 3072
B16 = jnp.bfloat16
F32 = jnp.float32

epsilon_norm = 1e-06
score_scale = 0.125
masked_low = -1e30

FWD_GROUPS = (4, 8)
NZ, NX = 4, 2
ROWS = D // 16
ROWS2 = FF // 16
FSDP = ("z", "x", "core")


def mm(a, b, ca, cb):
    return lax.dot_general(a, b, (((ca,), (cb,)), ((), ())), preferred_element_type=F32)


def params(mib=56):
    return pltpu.CompilerParams(
        dimension_semantics=("arbitrary",), vmem_limit_bytes=mib * 1024 * 1024
    )


def cost(flops, nbytes, trans=0):
    return pl.CostEstimate(flops=int(flops), bytes_accessed=int(nbytes), transcendentals=int(trans))


def shape(dims, dtype):
    return jax.ShapeDtypeStruct(dims, dtype)


def layer_norm(values, gain, shift):
    center = values - jnp.mean(values, axis=-1, keepdims=True)
    spread = jnp.mean(center * center, axis=-1, keepdims=True)
    return center * lax.rsqrt(spread + epsilon_norm) * gain + shift


def layer_norm_back(values, gain, grad):
    center = values - jnp.mean(values, axis=-1, keepdims=True)
    spread = jnp.mean(center * center, axis=-1, keepdims=True)
    inverse = lax.rsqrt(spread + epsilon_norm)
    hat = center * inverse
    grad_hat = grad * gain
    grad_values = inverse * (
        grad_hat
        - jnp.mean(grad_hat, axis=-1, keepdims=True)
        - hat * jnp.mean(grad_hat * hat, axis=-1, keepdims=True)
    )
    return grad_values, jnp.sum(grad * hat, axis=0, keepdims=True), jnp.sum(grad, axis=0, keepdims=True)


def erf(x):
    x = jnp.clip(x, -3.7439211627767994, 3.7439211627767994)
    z = x * x
    top = 0.00022905065861350646
    for c in (0.0034082910107109506, 0.050955695062380861, 0.18520832239976145, 1.128379143519084):
        top = top * z + c
    low = -1.1791602954361697e-7
    for c in (
        0.000023547966471313185,
        0.0010179625278914885,
        0.014070470171167667,
        0.11098505178285362,
        0.49746925110067538,
        1.0,
    ):
        low = low * z + c
    return x * top / low


def places(tab, rows):
    core = tab[8]
    for t in range(NZ * NX):
        base = tab[t] * 2
        yield (
            t,
            pl.ds(pl.multiple_of((base + core) * rows, 16), rows),
            pl.ds(pl.multiple_of((base + 1 - core) * rows, 16), rows),
        )


def assemble(tab, parts, dest):
    for t, here, there in places(tab, ROWS):
        rx, rz = divmod(t, NZ)
        dest[here, :] = parts[rx][rz]
        dest[there, :] = parts[2 + rx][rz]


def scatter(tab, source, own, send):
    for t, here, there in places(tab, ROWS):
        own[t] = source[here, :]
        send[t] = source[there, :]


def qkv_body(first, tab, x_ref, p0, p1, p2, p3, gain, shift, bias, *rest):
    if first:
        out_ref, h_ref, w_s = rest

        @pl.when(pl.program_id(0) == 0)
        def _():
            h_ref[...] = layer_norm(x_ref[...].astype(F32), gain[...], shift[...]).astype(B16)

        h = h_ref
    else:
        out_ref, w_s = rest
        h = x_ref
    assemble(tab, (p0, p1, p2, p3), w_s)
    out_ref[0] = (mm(h[...], w_s[...], 1, 0) + bias[0]).astype(B16)


def qkv_call(first, tab, x, parts, gain, shift, bias):
    tokens = x.shape[0]
    width = parts[0].shape[2] // 3
    full = pl.BlockSpec((tokens, D), lambda j, t: (0, 0))
    row = pl.BlockSpec((1, D), lambda j, t: (0, 0))
    piece = pl.BlockSpec((NZ, ROWS, width), lambda j, t: (0, 0, j))
    outs = [shape((3, tokens, width), B16)]
    out_specs = [pl.BlockSpec((1, tokens, width), lambda j, t: (j, 0, 0))]
    if first:
        outs.append(shape((tokens, D), B16))
        out_specs.append(full)
    return pl.pallas_call(
        functools.partial(qkv_body, first),
        grid_spec=pltpu.PrefetchScalarGridSpec(
            num_scalar_prefetch=1,
            grid=(3,),
            in_specs=[full, piece, piece, piece, piece, row, row, pl.BlockSpec((1, 1, width), lambda j, t: (j, 0, 0))],
            out_specs=out_specs,
            scratch_shapes=[pltpu.VMEM((D, width), B16)],
        ),
        out_shape=outs,
        compiler_params=params(),
        cost_estimate=cost(6 * tokens * D * width, 8 * tokens * D),
        name="qkv_first" if first else "qkv_next",
    )(tab, x, *parts, gain, shift, bias)


def make_mask(seg_ref, mask):
    @pl.when(pl.program_id(0) == 0)
    def _():
        row = seg_ref[...].astype(F32)
        mask[...] = jnp.where(row.T == row, 0.0, masked_low)


def attend_body(rows, q_ref, k_ref, v_ref, seg_ref, o_ref, lse_ref, mask):
    make_mask(seg_ref, mask)
    tokens = q_ref.shape[1]
    for h in range(2):
        cols = slice(h * HD, (h + 1) * HD)
        k = k_ref[0, :, cols]
        v = v_ref[0, :, cols]
        for b in range(tokens // rows):
            r = slice(b * rows, (b + 1) * rows)
            q = q_ref[0, r, cols] * jnp.asarray(score_scale, B16)
            s = mm(q, k, 1, 1) + mask[r, :]
            top = jnp.max(s, axis=-1, keepdims=True)
            p = jnp.exp(s - top)
            total = jnp.sum(p, axis=-1, keepdims=True)
            a = (p * (1.0 / total)).astype(B16)
            o_ref[r, cols] = mm(a, v, 1, 0).astype(B16)
            lse_ref[0, h : h + 1, r] = (top + jnp.log(total)).T


def attend_call(qkv, seg, start=0, pairs=None):
    _, tokens, width = qkv.shape
    pairs = pairs or width // 128
    width = pairs * 128
    head = lambda j: pl.BlockSpec((1, tokens, 128), lambda i: (j, 0, i + start))
    return pl.pallas_call(
        functools.partial(attend_body, min(512, tokens)),
        grid=(pairs,),
        in_specs=[head(0), head(1), head(2), pl.BlockSpec((1, tokens), lambda i: (0, 0))],
        out_specs=[
            pl.BlockSpec((tokens, 128), lambda i: (0, i)),
            pl.BlockSpec((1, 2, tokens), lambda i: (i, 0, 0)),
        ],
        out_shape=[shape((tokens, width), B16), shape((pairs, 2, tokens), F32)],
        scratch_shapes=[pltpu.VMEM((tokens, tokens), F32)],
        compiler_params=params(),
        cost_estimate=cost(pairs * 16 * 128 * tokens * tokens, 8 * tokens * width, pairs * 2 * tokens * tokens),
        name="attend",
    )(qkv, qkv, qkv, seg)


HALF = FF // 2


def gelu_tiles(h2, w1, c1, act_ref, slope_ref):
    tile = 512
    for f in range(HALF // tile):
        cols = slice(f * tile, (f + 1) * tile)
        u = mm(h2, w1[:, cols], 1, 0) + c1[:, cols]
        cdf = 0.5 + 0.5 * erf(u * 0.7071067811865476)
        act_ref[:, cols] = (u * cdf).astype(B16)
        slope_ref[:, cols] = (cdf + u * (jnp.exp(u * u * -0.5) * 0.3989422804014327)).astype(B16)


def up_body(count, tab, *refs):
    outs, (x_ref, p0, p1, p2, p3, bo, gain, shift, c1) = refs[:count], refs[count : count + 9]
    x1_ref, h2_ref, act_ref, slope_ref, w_s = refs[count + 9 :]

    @pl.when(pl.program_id(0) == 0)
    def _():
        assemble(tab, (p0, p1, p2, p3), w_s)

    x1 = x_ref[...].astype(F32) + bo[...]
    at = 0
    for o in outs:
        x1 = x1 + mm(o[...], w_s[at : at + o.shape[1], HALF:], 1, 0)
        at += o.shape[1]
    x1_ref[...] = x1
    h2 = layer_norm(x1, gain[...], shift[...]).astype(B16)
    h2_ref[...] = h2
    gelu_tiles(h2, w_s, c1, act_ref, slope_ref)


def up_call(tab, outs, x, parts, bo, gain, shift, c1):
    tokens = x.shape[0]
    rows = min(256, tokens)
    block = lambda w: pl.BlockSpec((rows, w), lambda i, t: (i, 0))
    row = lambda w: pl.BlockSpec((1, w), lambda i, t: (0, 0))
    piece = pl.BlockSpec((NZ, ROWS, HALF + D), lambda i, t: (0, 0, 0), pipeline_mode=pl.Buffered(1))
    return pl.pallas_call(
        functools.partial(up_body, len(outs)),
        grid_spec=pltpu.PrefetchScalarGridSpec(
            num_scalar_prefetch=1,
            grid=(tokens // rows,),
            in_specs=[block(o.shape[1]) for o in outs]
            + [block(D)]
            + [piece] * 4
            + [row(D), row(D), row(D), row(HALF)],
            out_specs=[block(D), block(D), block(HALF), block(HALF)],
            scratch_shapes=[pltpu.VMEM((D, HALF + D), B16)],
        ),
        out_shape=[shape((tokens, D), F32), shape((tokens, D), B16), shape((tokens, FF), B16), shape((tokens, FF), B16)],
        compiler_params=params(),
        cost_estimate=cost(2 * tokens * D * (D + HALF), 20 * tokens * D, tokens * HALF),
        name="up_first",
    )(tab, *outs, x, *parts, bo, gain, shift, c1)


def up_next_body(tab, h2_ref, p0, p1, p2, p3, c1, act_in, slope_in, act_ref, slope_ref, w_s):
    @pl.when(pl.program_id(0) == 0)
    def _():
        assemble(tab, (p0, p1, p2, p3), w_s)

    gelu_tiles(h2_ref[...], w_s, c1, act_ref, slope_ref)


def up_next_call(tab, h2, parts, c1, act, slope):
    tokens = h2.shape[0]
    rows = min(256, tokens)
    half = pl.BlockSpec((rows, HALF), lambda i, t: (i, 1))
    piece = pl.BlockSpec((NZ, ROWS, HALF), lambda i, t: (0, 0, 0), pipeline_mode=pl.Buffered(1))
    return pl.pallas_call(
        up_next_body,
        grid_spec=pltpu.PrefetchScalarGridSpec(
            num_scalar_prefetch=1,
            grid=(tokens // rows,),
            in_specs=[
                pl.BlockSpec((rows, D), lambda i, t: (i, 0)),
                piece,
                piece,
                piece,
                piece,
                pl.BlockSpec((1, HALF), lambda i, t: (0, 1)),
                pl.BlockSpec(memory_space=pl.ANY),
                pl.BlockSpec(memory_space=pl.ANY),
            ],
            out_specs=[half, half],
            scratch_shapes=[pltpu.VMEM((D, HALF), B16)],
        ),
        out_shape=[shape((tokens, FF), B16), shape((tokens, FF), B16)],
        input_output_aliases={7: 0, 8: 1},
        compiler_params=params(),
        cost_estimate=cost(2 * tokens * D * HALF, 10 * tokens * D, tokens * HALF),
        name="up_next",
    )(tab, h2, *parts, c1, act, slope)


def down_body(tab, act_ref, slope_ref, dy_ref, x1_ref, p0, p1, p2, p3, c2, out_ref, du_ref, own, send, dc1, dc2, acc, w2, dw2):
    step = pl.program_id(0)
    core = tab[8]

    @pl.when(step == 0)
    def _():
        acc[...] = x1_ref[...] + c2[...]
        dc2[...] = jnp.sum(dy_ref[...].astype(F32), axis=0, keepdims=True)

    for rx in range(NX):
        base = lax.rem(tab[rx * NZ], 2) * 2
        w2[pl.ds(pl.multiple_of((base + core) * ROWS2, 64), ROWS2), :] = (p0, p1)[rx][0]
        w2[pl.ds(pl.multiple_of((base + 1 - core) * ROWS2, 64), ROWS2), :] = (p2, p3)[rx][0]
    act = act_ref[...]
    dy = dy_ref[...]
    w = w2[...]
    du = (mm(dy, w, 1, 1) * slope_ref[...].astype(F32)).astype(B16)
    du_ref[...] = du
    dc1[...] = jnp.sum(du.astype(F32), axis=0, keepdims=True)
    acc[...] += mm(act, w, 1, 0)
    dw2[...] = mm(act, dy, 0, 0).astype(B16)
    for rx in range(NX):
        base = lax.rem(tab[rx * NZ], 2) * 2
        own[rx, 0] = dw2[pl.ds(pl.multiple_of((base + core) * ROWS2, 64), ROWS2), :]
        send[rx, 0] = dw2[pl.ds(pl.multiple_of((base + 1 - core) * ROWS2, 64), ROWS2), :]

    @pl.when(step == NZ - 1)
    def _():
        out_ref[...] = acc[...].astype(B16)


def down_call(tab, act, slope, dy, x1, parts, c2):
    tokens = dy.shape[0]
    width = FF // NZ
    full = pl.BlockSpec((tokens, D), lambda i, t: (0, 0))
    ff = pl.BlockSpec((tokens, width), lambda i, t: (0, t[i] // 2))
    piece = pl.BlockSpec((NX, 1, ROWS2, D), lambda i, t: (0, i, 0, 0))
    part = pl.BlockSpec((1, ROWS2, D), lambda i, t: (i, 0, 0))
    row = pl.BlockSpec((1, D), lambda i, t: (0, 0))
    pieces = shape((NX, NZ, ROWS2, D), B16)
    return pl.pallas_call(
        down_body,
        grid_spec=pltpu.PrefetchScalarGridSpec(
            num_scalar_prefetch=1,
            grid=(NZ,),
            in_specs=[ff, ff, full, full, part, part, part, part, row],
            out_specs=[full, ff, piece, piece, pl.BlockSpec((1, width), lambda i, t: (0, t[i] // 2)), row],
            scratch_shapes=[pltpu.VMEM((tokens, D), F32), pltpu.VMEM((width, D), B16), pltpu.VMEM((width, D), B16)],
        ),
        out_shape=[
            shape((tokens, D), B16),
            shape((tokens, FF), B16),
            pieces,
            pieces,
            shape((1, FF), F32),
            shape((1, D), F32),
        ],
        compiler_params=params(),
        cost_estimate=cost(6 * tokens * D * FF, 40 * tokens * D),
        name="down",
    )(tab, act, slope, dy, x1, *parts, c2)


def hidden_body(tab, h2_ref, du_ref, a0, a1, a2, a3, b0, b1, b2, b3, acc, own, send, w_s, dw):
    step = pl.program_id(0)

    @pl.when(step == 0)
    def _():
        acc[...] = jnp.zeros_like(acc)

    @pl.when(step < 2)
    def _():
        assemble(tab, (a0, a1, a2, a3), w_s)

    @pl.when(step >= 2)
    def _():
        assemble(tab, (b0, b1, b2, b3), w_s)

    du = du_ref[...]
    dw[...] = mm(h2_ref[...], du, 0, 0).astype(B16)
    acc[...] += mm(du, w_s[...], 1, 1)
    scatter(tab, dw, own, send)


def hidden_call(tab, h2, du, first, second):
    tokens = h2.shape[0]
    full = pl.BlockSpec((tokens, D), lambda i, t: (0, 0), pipeline_mode=pl.Buffered(1))
    piece = pl.BlockSpec((8, ROWS, D), lambda i, t: (0, 0, i))
    part_a = pl.BlockSpec((NZ, ROWS, D), lambda i, t: (0, 0, jnp.minimum(i, 1)))
    part_b = pl.BlockSpec((NZ, ROWS, D), lambda i, t: (0, 0, jnp.maximum(i - 2, 0)))
    pieces = shape((8, ROWS, FF), B16)
    return pl.pallas_call(
        hidden_body,
        grid_spec=pltpu.PrefetchScalarGridSpec(
            num_scalar_prefetch=1,
            grid=(FF // D,),
            in_specs=[full, pl.BlockSpec((tokens, D), lambda i, t: (0, i))] + [part_a] * 4 + [part_b] * 4,
            out_specs=[pl.BlockSpec((tokens, D), lambda i, t: (0, 0)), piece, piece],
            scratch_shapes=[pltpu.VMEM((D, D), B16), pltpu.VMEM((D, D), B16)],
        ),
        out_shape=[shape((tokens, D), F32), pieces, pieces],
        compiler_params=params(),
        cost_estimate=cost(4 * tokens * D * FF, 20 * tokens * D),
        name="hidden",
    )(tab, h2, du, *first, *second)


def middle_body(count, tab, *refs):
    outs, (dh_ref, dy_ref, x1_ref, p0, p1, p2, p3, gain) = refs[:count], refs[count : count + 8]
    dx_ref, do_ref, own, send, dvec, w_s, dw = refs[count + 8 :]
    assemble(tab, (p0, p1, p2, p3), w_s)
    grad, dgain, dshift = layer_norm_back(x1_ref[...], gain[...], dh_ref[...])
    dx = dy_ref[...].astype(F32) + grad
    dx_ref[...] = dx
    da = dx.astype(B16)
    dvec[0:1, :] = dgain
    dvec[1:2, :] = dshift
    dvec[2:3, :] = jnp.sum(da.astype(F32), axis=0, keepdims=True)
    do_ref[...] = mm(da, w_s[...], 1, 1).astype(B16)
    at = 0
    for o in outs:
        dw[at : at + o.shape[1], :] = mm(o[...], da, 0, 0).astype(B16)
        at += o.shape[1]
    scatter(tab, dw, own, send)


def middle_call(tab, outs, dh, dy, x1, parts, gain, width):
    tokens = dy.shape[0]
    full = lambda w: pl.BlockSpec((tokens, w), lambda i, t: (0, 0))
    part = pl.BlockSpec((NZ, ROWS, D), lambda i, t: (0, 0, HALF // D))
    piece = pl.BlockSpec((8, ROWS, D), lambda i, t: (0, 0, width // D))
    pieces = shape((8, ROWS, width + D), B16)
    return pl.pallas_call(
        functools.partial(middle_body, len(outs)),
        grid_spec=pltpu.PrefetchScalarGridSpec(
            num_scalar_prefetch=1,
            grid=(1,),
            in_specs=[full(o.shape[1]) for o in outs]
            + [full(D), full(D), full(D)]
            + [part] * 4
            + [pl.BlockSpec((1, D), lambda i, t: (0, 0))],
            out_specs=[full(D), full(D), piece, piece, pl.BlockSpec((8, D), lambda i, t: (0, 0))],
            scratch_shapes=[pltpu.VMEM((D, D), B16), pltpu.VMEM((D, D), B16)],
        ),
        out_shape=[shape((tokens, D), F32), shape((tokens, D), B16), pieces, pieces, shape((8, D), F32)],
        compiler_params=params(),
        cost_estimate=cost(4 * tokens * D * D, 20 * tokens * D),
        name="middle",
    )(tab, *outs, dh, dy, x1, *parts, gain)


def attend_back_body(rows, q_ref, k_ref, v_ref, do_ref, o_ref, lse_ref, seg_ref, out_ref, mask):
    make_mask(seg_ref, mask)
    tokens = q_ref.shape[1]
    for h in range(2):
        cols = slice(h * HD, (h + 1) * HD)
        k = k_ref[0, :, cols]
        v = v_ref[0, :, cols]
        dk = jnp.zeros((HD, tokens), F32)
        dv = jnp.zeros((HD, tokens), F32)
        for b in range(tokens // rows):
            r = slice(b * rows, (b + 1) * rows)
            q = q_ref[0, r, cols] * jnp.asarray(score_scale, B16)
            do = do_ref[r, cols]
            centre = jnp.sum(do.astype(F32) * o_ref[r, cols].astype(F32), axis=1, keepdims=True)
            s = mm(q, k, 1, 1) + mask[r, :]
            p = jnp.exp(s - lse_ref[0, h : h + 1, r].T)
            da = mm(do, v, 1, 1)
            ds = (p * (da - centre)).astype(B16)
            dv = dv + mm(do.T, p.astype(B16), 1, 0)
            dk = dk + mm(q.T, ds, 1, 0)
            out_ref[0, r, cols] = (mm(ds, k, 1, 0) * score_scale).astype(B16)
        out_ref[1, :, cols] = dk.T.astype(B16)
        out_ref[2, :, cols] = dv.T.astype(B16)


def attend_back_call(qkv, do, o, lse, seg, first_pair):
    _, tokens, width = qkv.shape
    pairs = width // 128
    head = lambda j: pl.BlockSpec((1, tokens, 128), lambda i: (j, 0, i))
    return pl.pallas_call(
        functools.partial(attend_back_body, min(512, tokens)),
        grid=(pairs,),
        in_specs=[
            head(0),
            head(1),
            head(2),
            pl.BlockSpec((tokens, 128), lambda i: (0, i + first_pair)),
            pl.BlockSpec((tokens, 128), lambda i: (0, i)),
            pl.BlockSpec((1, 2, tokens), lambda i: (i, 0, 0)),
            pl.BlockSpec((1, tokens), lambda i: (0, 0)),
        ],
        out_specs=pl.BlockSpec((3, tokens, 128), lambda i: (0, 0, i)),
        out_shape=shape((3, tokens, width), B16),
        scratch_shapes=[pltpu.VMEM((tokens, tokens), F32)],
        compiler_params=params(),
        cost_estimate=cost(pairs * 40 * 128 * tokens * tokens, 16 * tokens * width, pairs * 2 * tokens * tokens),
        name="attend_back",
    )(qkv, qkv, qkv, do, o, lse, seg)


def weight_body(joined, tab, h_ref, d_ref, *refs):
    own, send, dbias, dw = refs[2 * joined :]
    d = d_ref[0]
    dbias[0] = jnp.sum(d.astype(F32), axis=0, keepdims=True)
    dw[...] = mm(h_ref[...], d, 0, 0).astype(B16)
    scatter(tab, dw, own, send)


def weight_call(tab, h1, dqkv, into=()):
    _, tokens, width = dqkv.shape
    piece = pl.BlockSpec((8, ROWS, width), lambda j, t: (0, 0, j))
    pieces = shape(into[0].shape if into else (8, ROWS, 3 * width), B16)
    return pl.pallas_call(
        functools.partial(weight_body, bool(into)),
        grid_spec=pltpu.PrefetchScalarGridSpec(
            num_scalar_prefetch=1,
            grid=(3,),
            in_specs=[
                pl.BlockSpec((tokens, D), lambda j, t: (0, 0)),
                pl.BlockSpec((1, tokens, width), lambda j, t: (j, 0, 0)),
            ]
            + [pl.BlockSpec(memory_space=pl.ANY)] * len(into),
            out_specs=[piece, piece, pl.BlockSpec((1, 1, width), lambda j, t: (j, 0, 0))],
            scratch_shapes=[pltpu.VMEM((D, width), B16)],
        ),
        out_shape=[pieces, pieces, shape((3, 1, width), F32)],
        input_output_aliases={3: 0, 4: 1} if into else {},
        compiler_params=params(),
        cost_estimate=cost(6 * tokens * D * width, 12 * tokens * width),
        name="qkv_weight",
    )(tab, h1, dqkv, *into)


def input_body(tab, da_ref, db_ref, x_ref, dx_ref, a0, a1, a2, a3, b0, b1, b2, b3, gain, out_ref, dvec, wa, wb):
    step = pl.program_id(0)

    @pl.when(step == 0)
    def _():
        assemble(tab, (a0, a1, a2, a3), wa)
        assemble(tab, (b0, b1, b2, b3), wb)
        dvec[...] = jnp.zeros_like(dvec)

    dh = None
    for d_ref, w in ((da_ref, wa), (db_ref, wb)):
        width = d_ref.shape[2]
        for j in range(3):
            term = mm(d_ref[j], w[:, j * width : (j + 1) * width], 1, 1)
            dh = term if dh is None else dh + term
    grad, dgain, dshift = layer_norm_back(x_ref[...].astype(F32), gain[...], dh)
    out_ref[...] = dx_ref[...] + grad
    dvec[0:1, :] += dgain
    dvec[1:2, :] += dshift


def input_call(tab, da, db, x, dx, parts_a, parts_b, gain):
    tokens = x.shape[0]
    rows = min(256, tokens)
    wa, wb = da.shape[2], db.shape[2]
    grads = lambda w: pl.BlockSpec((3, rows, w), lambda i, t: (0, i, 0))
    block = pl.BlockSpec((rows, D), lambda i, t: (i, 0))
    piece = lambda w: pl.BlockSpec((NZ, ROWS, 3 * w), lambda i, t: (0, 0, 0), pipeline_mode=pl.Buffered(1))
    return pl.pallas_call(
        input_body,
        grid_spec=pltpu.PrefetchScalarGridSpec(
            num_scalar_prefetch=1,
            grid=(tokens // rows,),
            in_specs=[
                grads(wa),
                grads(wb),
                block,
                block,
            ]
            + [piece(wa)] * 4
            + [piece(wb)] * 4
            + [
                pl.BlockSpec((1, D), lambda i, t: (0, 0)),
            ],
            out_specs=[block, pl.BlockSpec((8, D), lambda i, t: (0, 0))],
            scratch_shapes=[pltpu.VMEM((D, 3 * wa), B16), pltpu.VMEM((D, 3 * wb), B16)],
        ),
        out_shape=[shape((tokens, D), F32), shape((8, D), F32)],
        compiler_params=params(),
        cost_estimate=cost(6 * tokens * D * D, 20 * tokens * D),
        name="input_grad",
    )(tab, da, db, x, dx, *parts_a, *parts_b, gain)


def small_params():
    return pltpu.CompilerParams(vmem_limit_bytes=40 * 1024 * 1024)


def add(a, b):
    return (a.astype(F32) + b.astype(F32)).astype(B16)


def stack_body(*refs):
    for i, ref in enumerate(refs[:-1]):
        refs[-1][i] = ref[...]


def stack(parts):
    return pl.pallas_call(
        stack_body,
        out_shape=shape((len(parts), *parts[0].shape), parts[0].dtype),
        compiler_params=small_params(),
        cost_estimate=cost(0, 16 * parts[0].size),
        name="stack",
    )(*parts)


def split_body(a, b, keep, send):
    keep[0] = add(a[0, 0], b[0, 0])
    send[0] = add(a[1, 0], b[1, 0])


def add_split(own, received):
    _, r, w = own.shape
    both = pl.BlockSpec((NX, 1, r, w), lambda i: (0, i, 0, 0))
    one = pl.BlockSpec((1, r, w), lambda i: (i, 0, 0))
    return pl.pallas_call(
        split_body,
        grid=(NZ,),
        in_specs=[both, both],
        out_specs=[one, one],
        out_shape=[shape((NZ, r, w), B16)] * 2,
        compiler_params=params(),
        cost_estimate=cost(8 * r * w, 48 * r * w),
        name="add_split",
    )(own.reshape(NX, NZ, r, w), received.reshape(NX, NZ, r, w))


def halves_body(tab, a, b, keep, send):
    rep = tab[9]
    keep[0] = add(a[0, rep], b[0, rep])
    send[0] = add(a[0, 1 - rep], b[0, 1 - rep])


def add_halves(tab, own, received):
    n, r, w = own.shape
    both = pl.BlockSpec((1, 2, r // 2, w), lambda i, t: (i, 0, 0, 0))
    one = pl.BlockSpec((1, r // 2, w), lambda i, t: (i, 0, 0))
    return pl.pallas_call(
        halves_body,
        grid_spec=pltpu.PrefetchScalarGridSpec(
            num_scalar_prefetch=1, grid=(n,), in_specs=[both, both], out_specs=[one, one]
        ),
        out_shape=[shape((n, r // 2, w), B16)] * 2,
        compiler_params=params(),
        cost_estimate=cost(8 * r * w, 48 * r * w),
        name="add_halves",
    )(tab, own.reshape(n, 2, r // 2, w), received.reshape(n, 2, r // 2, w))


def parts_body(a, b, *outs):
    for i, out in enumerate(outs):
        out[...] = add(a[i], b[i])


def add_parts(keep, received):
    n, r, w = keep.shape
    return pl.pallas_call(
        parts_body,
        out_shape=[shape((r, w), B16)] * n,
        compiler_params=small_params(),
        cost_estimate=cost(4 * r * w, 24 * r * w),
        name="add_parts",
    )(keep, received)


def four_body(a, b, c, d, out):
    out[...] = ((a[...].astype(F32) + b[...].astype(F32)) + (c[...].astype(F32) + d[...].astype(F32))).astype(B16)


def add_four(parts):
    return pl.pallas_call(
        four_body,
        out_shape=shape(parts[0].shape, B16),
        compiler_params=small_params(),
        cost_estimate=cost(4 * parts[0].size, 10 * parts[0].size),
        name="add_four",
    )(*parts)


def tie(*trees):
    flat, tree = jax.tree.flatten(trees)
    return jax.tree.unflatten(tree, lax.optimization_barrier(flat))


def flip(value, axis, size, by):
    return lax.ppermute(value, axis, [(i, i ^ by) for i in range(size)])


def along_z(value):
    return [flip(value, "z", NZ, by) for by in range(1, NZ)]


def swap_z(parts):
    return [flip(parts[by], "z", NZ, by) for by in range(1, NZ)]


def along_x(value):
    return flip(value, "x", NX, 1)


def across(value):
    return flip(value, "core", 2, 1)


def along_rep(value):
    return flip(value, "rep", 2, 1)


def bounds_of():
    out, at = [], 0
    for heads in FWD_GROUPS:
        out.append((at * HD, (at + heads) * HD))
        at += heads
    return out


def weight_shards(w_qkv, w_out, w_fc1, w_fc2):
    shard_qkv = w_qkv.reshape(-1, 3 * D)
    shard_up = w_fc1.reshape(-1, FF)
    return [
        jnp.concatenate([shard_qkv[:, part * D + a : part * D + b] for part in range(3)], axis=1)
        for a, b in bounds_of()
    ] + [
        jnp.concatenate([shard_up[:, :HALF], w_out.reshape(-1, D)], axis=1),
        shard_up[:, HALF:],
        w_fc2.reshape(-1, D),
    ]


def gather_vectors(gains, biases):
    count = 1
    for axis in FSDP:
        count *= lax.axis_size(axis)
    vec = jnp.concatenate([gains, biases])
    vec = lax.all_to_all(
        jnp.broadcast_to(vec[None], (count, vec.shape[0])), FSDP, split_axis=0, concat_axis=0, tiled=True
    ).astype(F32)
    n = gains.shape[0]
    return vec[:, :n].reshape(1, -1), vec[:, n:].reshape(1, -1)


def reduce_small(dgains, dbiases):
    count, reps = 1, lax.axis_size("rep")
    for axis in FSDP:
        count *= lax.axis_size(axis)
    small = jnp.concatenate([dgains.reshape(count, -1), dbiases.reshape(count, -1)], axis=1)
    small = jnp.broadcast_to(small[:, None], (count, reps, small.shape[1])).reshape(count * reps, -1)
    small = lax.all_to_all(small, FSDP + ("rep",), split_axis=0, concat_axis=0, tiled=True)
    small = jnp.sum(small, axis=0)
    n = dgains.shape[0] // count
    return small[:n], small[n:]


def name_vectors(gains_all, biases_all):
    gain_one, gain_two = gains_all[:, :D], gains_all[:, D:]
    shift_one, bias_q, bias_v, bias_o, shift_two = [biases_all[:, i * D : (i + 1) * D] for i in range(5)]
    bias_up, bias_down = biases_all[:, 5 * D : 5 * D + FF], biases_all[:, 5 * D + FF :]
    qkv_bias = [
        jnp.stack([bias_q[:, a:b], jnp.zeros((1, b - a), F32), bias_v[:, a:b]]) for a, b in bounds_of()
    ]
    return gain_one, gain_two, shift_one, shift_two, qkv_bias, bias_o, bias_up, bias_down


def small_gradients(din, dmid, dbias, dc1, dc2):
    dgains = jnp.concatenate([din[0], dmid[0]])
    dbiases = jnp.concatenate(
        [
            din[1],
            jnp.concatenate([db[0, 0] for db in dbias]),
            jnp.concatenate([db[2, 0] for db in dbias]),
            dmid[2],
            dmid[1],
            dc1[0],
            dc2[0],
        ]
    )
    return dgains, dbiases


def join_qkv(grads):
    widths = [b - a for a, b in bounds_of()]
    return jnp.concatenate(
        [g[:, part * w : (part + 1) * w] for part in range(3) for g, w in zip(grads, widths)], axis=1
    ).reshape(-1)


GROUP_ONE = 3 * HD * FWD_GROUPS[1]


def shards(tokens, w_qkv, w_out, w_fc1, w_fc2, gains, biases, segment, cotangent):
    mz, mx, core = lax.axis_index("z"), lax.axis_index("x"), lax.axis_index("core")
    rep = lax.axis_index("rep")
    tab = jnp.stack(
        [((mz ^ rz) * NX + (mx ^ rx)).astype(jnp.int32) for rx in range(NX) for rz in range(NZ)]
        + [core.astype(jnp.int32), rep.astype(jnp.int32)]
    )
    seg = segment.reshape(1, -1)
    pairs = [(b - a) // 128 for a, b in bounds_of()]
    s0, s1, s2, s3, s4 = weight_shards(w_qkv, w_out, w_fc1, w_fc2)

    z0 = along_z(s0)
    vec = gather_vectors(gains, biases)
    z0, vec, s1 = tie(z0, vec, s1)
    gain_one, gain_two, shift_one, shift_two, qkv_bias, bias_o, bias_up, bias_down = name_vectors(*vec)
    a0 = stack([s0, *z0])
    x0, c0 = along_x(a0), across(a0)
    z1 = along_z(s1)
    x0, c0, s2 = tie(x0, c0, s2)
    w0 = (a0, x0, c0, across(x0))
    qkv0, h1 = qkv_call(True, tab, tokens, w0, gain_one, shift_one, qkv_bias[0])
    qkv0, z1, s2, s3 = tie(qkv0, z1, s2, s3)
    a1 = stack([s1, *z1])
    x1_, c1_ = along_x(a1), across(a1)
    z2 = along_z(s2)
    o0, lse0 = attend_call(qkv0, seg)
    o0, x1_, c1_, s3, s4, h1 = tie(o0, x1_, c1_, s3, s4, h1)
    z3 = along_z(s3)
    w1 = (a1, x1_, c1_, across(x1_))
    (qkv1,) = qkv_call(False, tab, h1, w1, gain_one, shift_one, qkv_bias[1])
    qkv1, z2, s4 = tie(qkv1, z2, s4)
    a2 = stack([s2, *z2])
    x2, c2 = along_x(a2), across(a2)
    z4 = along_z(s4)
    half = pairs[1] // 2
    o1, lse1 = attend_call(qkv1, seg, 0, half)
    o1, z3, qkv1 = tie(o1, z3, qkv1)
    a3 = stack([s3, *z3])
    x3, c3 = along_x(a3), across(a3)
    o2, lse2 = attend_call(qkv1, seg, half, half)
    o2, x2, c2 = tie(o2, x2, c2)
    w2 = (a2, x2, c2, across(x2))
    x1, h2, act, slope = up_call(tab, [o0, o1, o2], tokens, w2, bias_o, gain_two, shift_two, bias_up)
    h2, act, slope, x3, c3, z4 = tie(h2, act, slope, x3, c3, z4)
    a4 = stack([s4, *z4])
    x4, c4 = along_x(a4), across(a4)
    w3 = (a3, x3, c3, across(x3))
    act, slope = up_next_call(tab, h2, w3, bias_up, act, slope)
    act, slope, x4, c4 = tie(act, slope, x4, c4)
    w4 = (a4, x4, c4, across(x4))

    output, du, own2, send2, dc1, dc2 = down_call(tab, act, slope, cotangent, x1, w4, bias_down)
    own2, send2 = own2.reshape(8, ROWS2, D), send2.reshape(8, ROWS2, D)
    du, send2 = tie(du, send2)
    r2 = across(send2)
    dh, own1, send1 = hidden_call(tab, h2, du, w2, w3)
    dh, r2, send1 = tie(dh, r2, send1)
    keep2, give2 = add_halves(tab, own2, r2)
    r2 = along_rep(give2)
    r1 = across(send1)
    dx1, do, own_o, send_o, dmid = middle_call(tab, [o0, o1, o2], dh, cotangent, x1, w2, gain_two, GROUP_ONE)
    do, r1 = tie(do, r1)
    keep1, give1 = add_split(own1, r1)
    r1 = along_x(give1)
    d1 = attend_back_call(qkv1, do, jnp.concatenate([o1, o2], axis=1), jnp.concatenate([lse1, lse2]), seg, pairs[0])
    d1, r1, r2 = tie(d1, r1, r2)
    keep2, give2 = add_split(keep2, r2)
    parts1 = add_parts(keep1, r1)
    r2 = along_x(give2)
    r1 = swap_z(parts1)
    own_q, send_q, db1 = weight_call(tab, h1, d1, (own_o, send_o))
    send_q, own_q, r2, r1, do = tie(send_q, own_q, r2, r1, do)
    rq = across(send_q)
    parts2 = add_parts(keep2, r2)
    total1 = add_four([parts1[0], *r1])
    r2 = swap_z(parts2)
    y1 = along_rep(total1)
    d0 = attend_back_call(qkv0, do, o0, lse0, seg, 0)
    d0, rq, r2, y1 = tie(d0, rq, r2, y1)
    keepq, giveq = add_split(own_q, rq)
    rq = along_x(giveq)
    total2 = add_four([parts2[0], *r2])
    y2 = along_rep(total2)
    own_p, send_p, db0 = weight_call(tab, h1, d0)
    send_p, rq, y2 = tie(send_p, rq, y2)
    rp = across(send_p)
    partsq = add_parts(keepq, rq)
    rq = swap_z(partsq)
    rp, own_p = tie(rp, own_p)
    keepp, givep = add_split(own_p, rp)
    givep, dx1 = tie(givep, dx1)
    rp = along_x(givep)
    grad_tokens, din = input_call(tab, d0, d1, tokens, dx1, w0, w1, gain_one)
    din, rp, rq = tie(din, rp, rq)
    partsp = add_parts(keepp, rp)
    rp = swap_z(partsp)
    totalq = add_four([partsq[0], *rq])
    yq = along_rep(totalq)
    small = reduce_small(*small_gradients(din, dmid, (db0, db1), dc1, dc2))
    totalp = add_four([partsp[0], *rp])
    yp = along_rep(totalp)

    grad1 = total1.astype(F32) + y1.astype(F32)
    pair = jnp.where(rep == 0, jnp.concatenate([total2, y2]), jnp.concatenate([y2, total2]))
    gradq = totalq.astype(F32) + yq.astype(F32)
    gradp = totalp.astype(F32) + yp.astype(F32)
    return (
        output,
        grad_tokens,
        join_qkv([gradp, gradq[:, :GROUP_ONE]]),
        gradq[:, GROUP_ONE:].reshape(-1),
        grad1.reshape(-1),
        pair.astype(F32).reshape(-1),
        *small,
    )


def gather_any(shard):
    whole = lax.all_gather(shard, FSDP, axis=0, tiled=True)
    blocks = whole.reshape(NZ, NX, 2, -1, whole.shape[1]).transpose(2, 1, 0, 3, 4)
    return blocks[0, 0], blocks[0, 1], blocks[1, 0], blocks[1, 1]


def reduce_any(own, send):
    blocks = jnp.stack([own, send]).reshape(2, NX, NZ, *own.shape[1:]).transpose(2, 1, 0, 3, 4)
    whole = blocks.reshape(-1, own.shape[2])
    part = lax.psum_scatter(whole, FSDP, scatter_dimension=0, tiled=True)
    return lax.psum(part, "rep").astype(F32)


def shards_any(tokens, w_qkv, w_out, w_fc1, w_fc2, gains, biases, segment, cotangent):
    tab = jnp.asarray([rz * NX + rx for rx in range(NX) for rz in range(NZ)] + [0, 0], jnp.int32)
    seg = segment.reshape(1, -1)
    pairs = [(b - a) // 128 for a, b in bounds_of()]
    w0, w1, w2, w3, w4 = [gather_any(s) for s in weight_shards(w_qkv, w_out, w_fc1, w_fc2)]
    gain_one, gain_two, shift_one, shift_two, qkv_bias, bias_o, bias_up, bias_down = name_vectors(
        *gather_vectors(gains, biases)
    )
    qkv0, h1 = qkv_call(True, tab, tokens, w0, gain_one, shift_one, qkv_bias[0])
    (qkv1,) = qkv_call(False, tab, h1, w1, gain_one, shift_one, qkv_bias[1])
    o0, lse0 = attend_call(qkv0, seg)
    o1, lse1 = attend_call(qkv1, seg)
    x1, h2, act, slope = up_call(tab, [o0, o1], tokens, w2, bias_o, gain_two, shift_two, bias_up)
    act, slope = up_next_call(tab, h2, w3, bias_up, act, slope)
    output, du, own2, send2, dc1, dc2 = down_call(tab, act, slope, cotangent, x1, w4, bias_down)
    dh, own1, send1 = hidden_call(tab, h2, du, w2, w3)
    dx1, do, own_o, send_o, dmid = middle_call(tab, [o0, o1], dh, cotangent, x1, w2, gain_two, GROUP_ONE)
    d1 = attend_back_call(qkv1, do, o1, lse1, seg, pairs[0])
    d0 = attend_back_call(qkv0, do, o0, lse0, seg, 0)
    own_q, send_q, db1 = weight_call(tab, h1, d1, (own_o, send_o))
    own_p, send_p, db0 = weight_call(tab, h1, d0)
    grad_tokens, din = input_call(tab, d0, d1, tokens, dx1, w0, w1, gain_one)
    gradq = reduce_any(own_q, send_q)
    return (
        output,
        grad_tokens,
        join_qkv([reduce_any(own_p, send_p), gradq[:, :GROUP_ONE]]),
        gradq[:, GROUP_ONE:].reshape(-1),
        reduce_any(own1, send1).reshape(-1),
        reduce_any(own2.reshape(8, ROWS2, D), send2.reshape(8, ROWS2, D)).reshape(-1),
        *reduce_small(*small_gradients(din, dmid, (db0, db1), dc1, dc2)),
    )


def solution(mesh):
    count, reps = mesh.shape["fsdp"], mesh.shape["rep"]
    inner = Mesh(mesh.devices.reshape(count // 4, 2, 2, reps), FSDP + ("rep",))
    rows = P(FSDP + ("rep",), None)
    flat = P(FSDP)
    return jax.shard_map(
        shards if (count, reps) == (2 * NZ * NX, 2) else shards_any,
        mesh=inner,
        in_specs=(rows, flat, flat, flat, flat, flat, flat, P(FSDP + ("rep",)), rows),
        out_specs=(rows, rows, flat, flat, flat, flat, flat, flat),
        check_vma=False,
    )
```

```python
import functools

import jax
import jax.numpy as jnp
from jax import lax
from jax.experimental import pallas as pl
from jax.experimental.pallas import tpu as pltpu
from jax.sharding import Mesh
from jax.sharding import PartitionSpec as P

D = 768
H = 12
HD = 64
FF = 3072
B16 = jnp.bfloat16
F32 = jnp.float32

epsilon_norm = 1e-06
score_scale = 0.125
masked_low = -1e30

FWD_GROUPS = (4, 8)
NZ, NX = 4, 2
ROWS = D // 16
ROWS2 = FF // 16
FSDP = ("z", "x", "core")


def mm(a, b, ca, cb):
    return lax.dot_general(a, b, (((ca,), (cb,)), ((), ())), preferred_element_type=F32)


def params(mib=56):
    return pltpu.CompilerParams(
        dimension_semantics=("arbitrary",), vmem_limit_bytes=mib * 1024 * 1024
    )


def cost(flops, nbytes, trans=0):
    return pl.CostEstimate(flops=int(flops), bytes_accessed=int(nbytes), transcendentals=int(trans))


def shape(dims, dtype):
    return jax.ShapeDtypeStruct(dims, dtype)


def layer_norm(values, gain, shift):
    center = values - jnp.mean(values, axis=-1, keepdims=True)
    spread = jnp.mean(center * center, axis=-1, keepdims=True)
    return center * lax.rsqrt(spread + epsilon_norm) * gain + shift


def layer_norm_back(values, gain, grad):
    center = values - jnp.mean(values, axis=-1, keepdims=True)
    spread = jnp.mean(center * center, axis=-1, keepdims=True)
    inverse = lax.rsqrt(spread + epsilon_norm)
    hat = center * inverse
    grad_hat = grad * gain
    grad_values = inverse * (
        grad_hat
        - jnp.mean(grad_hat, axis=-1, keepdims=True)
        - hat * jnp.mean(grad_hat * hat, axis=-1, keepdims=True)
    )
    return grad_values, jnp.sum(grad * hat, axis=0, keepdims=True), jnp.sum(grad, axis=0, keepdims=True)


def erf(x):
    x = jnp.clip(x, -3.7439211627767994, 3.7439211627767994)
    z = x * x
    top = 0.00022905065861350646
    for c in (0.0034082910107109506, 0.050955695062380861, 0.18520832239976145, 1.128379143519084):
        top = top * z + c
    low = -1.1791602954361697e-7
    for c in (
        0.000023547966471313185,
        0.0010179625278914885,
        0.014070470171167667,
        0.11098505178285362,
        0.49746925110067538,
        1.0,
    ):
        low = low * z + c
    return x * top / low


def places(tab, rows):
    core = tab[8]
    for t in range(NZ * NX):
        base = tab[t] * 2
        yield (
            t,
            pl.ds(pl.multiple_of((base + core) * rows, 16), rows),
            pl.ds(pl.multiple_of((base + 1 - core) * rows, 16), rows),
        )


def assemble(tab, parts, dest):
    for t, here, there in places(tab, ROWS):
        rx, rz = divmod(t, NZ)
        dest[here, :] = parts[rx][rz]
        dest[there, :] = parts[2 + rx][rz]


def scatter(tab, source, own, send):
    for t, here, there in places(tab, ROWS):
        own[t] = source[here, :]
        send[t] = source[there, :]


def qkv_body(first, tab, x_ref, p0, p1, p2, p3, gain, shift, bias, *rest):
    if first:
        out_ref, h_ref, w_s = rest

        @pl.when(pl.program_id(0) == 0)
        def _():
            h_ref[...] = layer_norm(x_ref[...].astype(F32), gain[...], shift[...]).astype(B16)

        h = h_ref
    else:
        out_ref, w_s = rest
        h = x_ref
    assemble(tab, (p0, p1, p2, p3), w_s)
    out_ref[0] = (mm(h[...], w_s[...], 1, 0) + bias[0]).astype(B16)


def qkv_call(first, tab, x, parts, gain, shift, bias):
    tokens = x.shape[0]
    width = parts[0].shape[2] // 3
    full = pl.BlockSpec((tokens, D), lambda j, t: (0, 0))
    row = pl.BlockSpec((1, D), lambda j, t: (0, 0))
    piece = pl.BlockSpec((NZ, ROWS, width), lambda j, t: (0, 0, j))
    outs = [shape((3, tokens, width), B16)]
    out_specs = [pl.BlockSpec((1, tokens, width), lambda j, t: (j, 0, 0))]
    if first:
        outs.append(shape((tokens, D), B16))
        out_specs.append(full)
    return pl.pallas_call(
        functools.partial(qkv_body, first),
        grid_spec=pltpu.PrefetchScalarGridSpec(
            num_scalar_prefetch=1,
            grid=(3,),
            in_specs=[full, piece, piece, piece, piece, row, row, pl.BlockSpec((1, 1, width), lambda j, t: (j, 0, 0))],
            out_specs=out_specs,
            scratch_shapes=[pltpu.VMEM((D, width), B16)],
        ),
        out_shape=outs,
        compiler_params=params(),
        cost_estimate=cost(6 * tokens * D * width, 8 * tokens * D),
        name="qkv_first" if first else "qkv_next",
    )(tab, x, *parts, gain, shift, bias)


def make_mask(seg_ref, mask):
    @pl.when(pl.program_id(0) == 0)
    def _():
        row = seg_ref[...].astype(F32)
        mask[...] = jnp.where(row.T == row, 0.0, masked_low)


def attend_body(rows, q_ref, k_ref, v_ref, seg_ref, o_ref, lse_ref, mask):
    make_mask(seg_ref, mask)
    tokens = q_ref.shape[1]
    for h in range(2):
        cols = slice(h * HD, (h + 1) * HD)
        k = k_ref[0, :, cols]
        v = v_ref[0, :, cols]
        for b in range(tokens // rows):
            r = slice(b * rows, (b + 1) * rows)
            q = q_ref[0, r, cols] * jnp.asarray(score_scale, B16)
            s = mm(q, k, 1, 1) + mask[r, :]
            top = jnp.max(s, axis=-1, keepdims=True)
            p = jnp.exp(s - top)
            total = jnp.sum(p, axis=-1, keepdims=True)
            a = (p * (1.0 / total)).astype(B16)
            o_ref[r, cols] = mm(a, v, 1, 0).astype(B16)
            lse_ref[0, h : h + 1, r] = (top + jnp.log(total)).T


def attend_call(qkv, seg, start=0, pairs=None):
    _, tokens, width = qkv.shape
    pairs = pairs or width // 128
    width = pairs * 128
    head = lambda j: pl.BlockSpec((1, tokens, 128), lambda i: (j, 0, i + start))
    return pl.pallas_call(
        functools.partial(attend_body, min(512, tokens)),
        grid=(pairs,),
        in_specs=[head(0), head(1), head(2), pl.BlockSpec((1, tokens), lambda i: (0, 0))],
        out_specs=[
            pl.BlockSpec((tokens, 128), lambda i: (0, i)),
            pl.BlockSpec((1, 2, tokens), lambda i: (i, 0, 0)),
        ],
        out_shape=[shape((tokens, width), B16), shape((pairs, 2, tokens), F32)],
        scratch_shapes=[pltpu.VMEM((tokens, tokens), F32)],
        compiler_params=params(),
        cost_estimate=cost(pairs * 16 * 128 * tokens * tokens, 8 * tokens * width, pairs * 2 * tokens * tokens),
        name="attend",
    )(qkv, qkv, qkv, seg)


BULK = ROWS2 + 4 * ROWS + ROWS
N16 = 16
SPARE = 16


def up_body(count, *refs):
    outs, (x_ref, wo_ref, wa, wb, wc, wd, bo, gain, shift, c1) = refs[:count], refs[count : count + 10]
    x1_ref, h2_ref, act_ref, slope_ref = refs[count + 10 :]
    x1 = x_ref[...].astype(F32) + bo[...]
    wo = wo_ref[...].reshape(D, D)
    at = 0
    for o in outs:
        x1 = x1 + mm(o[...], wo[at : at + o.shape[1], :], 1, 0)
        at += o.shape[1]
    x1_ref[...] = x1
    h2 = layer_norm(x1, gain[...], shift[...]).astype(B16)
    h2_ref[...] = h2
    tile = D // 2
    for f in range(FF // tile):
        cols = slice(f * tile, (f + 1) * tile)
        w = (wa, wb, wc, wd)[f // 2][:, :, (f % 2) * tile : (f % 2 + 1) * tile].reshape(D, tile)
        u = mm(h2, w, 1, 0) + c1[:, cols]
        cdf = 0.5 + 0.5 * erf(u * 0.7071067811865476)
        act_ref[:, cols] = (u * cdf).astype(B16)
        slope_ref[:, cols] = (cdf + u * (jnp.exp(u * u * -0.5) * 0.3989422804014327)).astype(B16)


def bulk_block(j):
    return pl.BlockSpec((N16, ROWS, D), lambda i: (0, j, 0), pipeline_mode=pl.Buffered(1))


def up_call(outs, x, bulk, bo, gain, shift, c1):
    tokens = x.shape[0]
    rows = min(256, tokens)
    block = lambda w: pl.BlockSpec((rows, w), lambda i: (i, 0))
    row = lambda w: pl.BlockSpec((1, w), lambda i: (0, 0))
    return pl.pallas_call(
        functools.partial(up_body, len(outs)),
        grid=(tokens // rows,),
        in_specs=[block(o.shape[1]) for o in outs]
        + [block(D)]
        + [bulk_block(j) for j in (8, 4, 5, 6, 7)]
        + [row(D), row(D), row(D), row(FF)],
        out_specs=[block(D), block(D), block(FF), block(FF)],
        out_shape=[shape((tokens, D), F32), shape((tokens, D), B16), shape((tokens, FF), B16), shape((tokens, FF), B16)],
        compiler_params=params(),
        cost_estimate=cost(2 * tokens * D * (D + FF), 30 * tokens * D, tokens * FF),
        name="up",
    )(*outs, x, bulk, bulk, bulk, bulk, bulk, bo, gain, shift, c1)


def down_body(act_ref, slope_ref, dy_ref, x1_ref, w_ref, c2, out_ref, du_ref, dw_ref, dc1, dc2, acc):
    step = pl.program_id(0)

    @pl.when(step == 0)
    def _():
        acc[...] = x1_ref[...] + c2[...]
        dc2[...] = jnp.sum(dy_ref[...].astype(F32), axis=0, keepdims=True)

    act = act_ref[...]
    dy = dy_ref[...]
    w = w_ref[...].reshape(D, D)
    du = (mm(dy, w, 1, 1) * slope_ref[...].astype(F32)).astype(B16)
    du_ref[...] = du
    dc1[...] = jnp.sum(du.astype(F32), axis=0, keepdims=True)
    acc[...] += mm(act, w, 1, 0)
    dw_ref[...] = mm(act, dy, 0, 0).astype(B16)

    @pl.when(step == FF // D - 1)
    def _():
        out_ref[...] = acc[...].astype(B16)


def down_call(act, slope, dy, x1, bulk, c2):
    tokens = dy.shape[0]
    full = pl.BlockSpec((tokens, D), lambda i: (0, 0))
    ff = pl.BlockSpec((tokens, D), lambda i: (0, i))
    piece = pl.BlockSpec((N16 // 4, ROWS2, D), lambda i: (i, 0, 0))
    row = pl.BlockSpec((1, D), lambda i: (0, 0))
    return pl.pallas_call(
        down_body,
        grid=(FF // D,),
        in_specs=[ff, ff, full, full, piece, row],
        out_specs=[full, ff, pl.BlockSpec((D, D), lambda i: (i, 0)), pl.BlockSpec((1, D), lambda i: (0, i)), row],
        out_shape=[
            shape((tokens, D), B16),
            shape((tokens, FF), B16),
            shape((FF, D), B16),
            shape((1, FF), F32),
            shape((1, D), F32),
        ],
        scratch_shapes=[pltpu.VMEM((tokens, D), F32)],
        compiler_params=params(),
        cost_estimate=cost(6 * tokens * D * FF, 40 * tokens * D),
        name="down",
    )(act, slope, dy, x1, bulk, c2)


def hidden_body(tab, h2_ref, du_ref, w_ref, acc, own, send, dw):
    @pl.when(pl.program_id(0) == 0)
    def _():
        acc[...] = jnp.zeros_like(acc)

    du = du_ref[...]
    dw[...] = mm(h2_ref[...], du, 0, 0).astype(B16)
    acc[...] += mm(du, w_ref[...].reshape(D, D), 1, 1)
    scatter(tab, dw, own, send)


def hidden_call(tab, h2, du, bulk):
    tokens = h2.shape[0]
    full = pl.BlockSpec((tokens, D), lambda i, t: (0, 0), pipeline_mode=pl.Buffered(1))
    piece = pl.BlockSpec((8, ROWS, D), lambda i, t: (0, 0, i))
    pieces = shape((8, ROWS, FF), B16)
    return pl.pallas_call(
        hidden_body,
        grid_spec=pltpu.PrefetchScalarGridSpec(
            num_scalar_prefetch=1,
            grid=(FF // D,),
            in_specs=[
                full,
                pl.BlockSpec((tokens, D), lambda i, t: (0, i)),
                pl.BlockSpec((N16, ROWS, D), lambda i, t: (0, 4 + i, 0)),
            ],
            out_specs=[pl.BlockSpec((tokens, D), lambda i, t: (0, 0)), piece, piece],
            scratch_shapes=[pltpu.VMEM((D, D), B16)],
        ),
        out_shape=[shape((tokens, D), F32), pieces, pieces],
        compiler_params=params(),
        cost_estimate=cost(4 * tokens * D * FF, 20 * tokens * D),
        name="hidden",
    )(tab, h2, du, bulk)


def middle_body(count, *refs):
    outs, (dh_ref, dy_ref, x1_ref, w_ref, gain) = refs[:count], refs[count : count + 5]
    dx_ref, do_ref, dw_ref, dvec = refs[count + 5 :]
    grad, dgain, dshift = layer_norm_back(x1_ref[...], gain[...], dh_ref[...])
    dx = dy_ref[...].astype(F32) + grad
    dx_ref[...] = dx
    da = dx.astype(B16)
    dvec[0:1, :] = dgain
    dvec[1:2, :] = dshift
    dvec[2:3, :] = jnp.sum(da.astype(F32), axis=0, keepdims=True)
    do_ref[...] = mm(da, w_ref[...].reshape(D, D), 1, 1).astype(B16)
    at = 0
    for o in outs:
        dw_ref[at : at + o.shape[1], :] = mm(o[...], da, 0, 0).astype(B16)
        at += o.shape[1]


def middle_call(outs, dh, dy, x1, bulk, gain):
    tokens = dy.shape[0]
    full = lambda w: pl.BlockSpec((tokens, w), lambda i: (0, 0))
    return pl.pallas_call(
        functools.partial(middle_body, len(outs)),
        grid=(1,),
        in_specs=[full(o.shape[1]) for o in outs]
        + [full(D), full(D), full(D)]
        + [pl.BlockSpec((N16, ROWS, D), lambda i: (0, 8, 0))]
        + [pl.BlockSpec((1, D), lambda i: (0, 0))],
        out_specs=[full(D), full(D), pl.BlockSpec((D, D), lambda i: (0, 0)), pl.BlockSpec((8, D), lambda i: (0, 0))],
        out_shape=[shape((tokens, D), F32), shape((tokens, D), B16), shape((D, D), B16), shape((8, D), F32)],
        compiler_params=params(),
        cost_estimate=cost(4 * tokens * D * D, 20 * tokens * D),
        name="middle",
    )(*outs, dh, dy, x1, bulk, gain)


def attend_back_body(rows, q_ref, k_ref, v_ref, do_ref, o_ref, lse_ref, seg_ref, out_ref, mask):
    make_mask(seg_ref, mask)
    tokens = q_ref.shape[1]
    for h in range(2):
        cols = slice(h * HD, (h + 1) * HD)
        k = k_ref[0, :, cols]
        v = v_ref[0, :, cols]
        dk = jnp.zeros((HD, tokens), F32)
        dv = jnp.zeros((HD, tokens), F32)
        for b in range(tokens // rows):
            r = slice(b * rows, (b + 1) * rows)
            q = q_ref[0, r, cols] * jnp.asarray(score_scale, B16)
            do = do_ref[r, cols]
            centre = jnp.sum(do.astype(F32) * o_ref[r, cols].astype(F32), axis=1, keepdims=True)
            s = mm(q, k, 1, 1) + mask[r, :]
            p = jnp.exp(s - lse_ref[0, h : h + 1, r].T)
            da = mm(do, v, 1, 1)
            ds = (p * (da - centre)).astype(B16)
            dv = dv + mm(do.T, p.astype(B16), 1, 0)
            dk = dk + mm(q.T, ds, 1, 0)
            out_ref[0, r, cols] = (mm(ds, k, 1, 0) * score_scale).astype(B16)
        out_ref[1, :, cols] = dk.T.astype(B16)
        out_ref[2, :, cols] = dv.T.astype(B16)


def attend_back_call(qkv, do, o, lse, seg, first_pair):
    _, tokens, width = qkv.shape
    pairs = width // 128
    head = lambda j: pl.BlockSpec((1, tokens, 128), lambda i: (j, 0, i))
    return pl.pallas_call(
        functools.partial(attend_back_body, min(512, tokens)),
        grid=(pairs,),
        in_specs=[
            head(0),
            head(1),
            head(2),
            pl.BlockSpec((tokens, 128), lambda i: (0, i + first_pair)),
            pl.BlockSpec((tokens, 128), lambda i: (0, i)),
            pl.BlockSpec((1, 2, tokens), lambda i: (i, 0, 0)),
            pl.BlockSpec((1, tokens), lambda i: (0, 0)),
        ],
        out_specs=pl.BlockSpec((3, tokens, 128), lambda i: (0, 0, i)),
        out_shape=shape((3, tokens, width), B16),
        scratch_shapes=[pltpu.VMEM((tokens, tokens), F32)],
        compiler_params=params(),
        cost_estimate=cost(pairs * 40 * 128 * tokens * tokens, 16 * tokens * width, pairs * 2 * tokens * tokens),
        name="attend_back",
    )(qkv, qkv, qkv, do, o, lse, seg)


def weight_body(tab, h_ref, d_ref, own, send, dbias, dw):
    d = d_ref[0]
    dbias[0] = jnp.sum(d.astype(F32), axis=0, keepdims=True)
    dw[...] = mm(h_ref[...], d, 0, 0).astype(B16)
    scatter(tab, dw, own, send)


def weight_call(tab, h1, dqkv):
    _, tokens, width = dqkv.shape
    piece = pl.BlockSpec((8, ROWS, width), lambda j, t: (0, 0, j))
    pieces = shape((8, ROWS, 3 * width), B16)
    return pl.pallas_call(
        weight_body,
        grid_spec=pltpu.PrefetchScalarGridSpec(
            num_scalar_prefetch=1,
            grid=(3,),
            in_specs=[
                pl.BlockSpec((tokens, D), lambda j, t: (0, 0)),
                pl.BlockSpec((1, tokens, width), lambda j, t: (j, 0, 0)),
            ],
            out_specs=[piece, piece, pl.BlockSpec((1, 1, width), lambda j, t: (j, 0, 0))],
            scratch_shapes=[pltpu.VMEM((D, width), B16)],
        ),
        out_shape=[pieces, pieces, shape((3, 1, width), F32)],
        compiler_params=params(),
        cost_estimate=cost(6 * tokens * D * width, 12 * tokens * width),
        name="qkv_weight",
    )(tab, h1, dqkv)


def input_body(tab, da_ref, db_ref, x_ref, dx_ref, a0, a1, a2, a3, b0, b1, b2, b3, gain, *refs):
    out_ref, dvec, wa, wb = refs[-4:]
    step = pl.program_id(0)

    @pl.when(step == 0)
    def _():
        assemble(tab, (a0, a1, a2, a3), wa)
        assemble(tab, (b0, b1, b2, b3), wb)
        dvec[...] = jnp.zeros_like(dvec)

    dh = None
    for d_ref, w in ((da_ref, wa), (db_ref, wb)):
        width = d_ref.shape[2]
        for j in range(3):
            term = mm(d_ref[j], w[:, j * width : (j + 1) * width], 1, 1)
            dh = term if dh is None else dh + term
    grad, dgain, dshift = layer_norm_back(x_ref[...].astype(F32), gain[...], dh)
    out_ref[...] = dx_ref[...] + grad
    dvec[0:1, :] += dgain
    dvec[1:2, :] += dshift


def input_call(tab, da, db, x, dx, parts_a, parts_b, gain, start, steps, into=()):
    tokens = x.shape[0]
    rows = tokens // 4
    wa, wb = da.shape[2], db.shape[2]
    grads = lambda w: pl.BlockSpec((3, rows, w), lambda i, t: (0, i + start, 0))
    block = pl.BlockSpec((rows, D), lambda i, t: (i + start, 0))
    piece = lambda w: pl.BlockSpec((NZ, ROWS, 3 * w), lambda i, t: (0, 0, 0), pipeline_mode=pl.Buffered(1))
    return pl.pallas_call(
        input_body,
        grid_spec=pltpu.PrefetchScalarGridSpec(
            num_scalar_prefetch=1,
            grid=(steps,),
            in_specs=[grads(wa), grads(wb), block, block]
            + [piece(wa)] * 4
            + [piece(wb)] * 4
            + [pl.BlockSpec((1, D), lambda i, t: (0, 0))]
            + [pl.BlockSpec(memory_space=pl.ANY)] * len(into),
            out_specs=[block, pl.BlockSpec((8, D), lambda i, t: (0, 0))],
            scratch_shapes=[pltpu.VMEM((D, 3 * wa), B16), pltpu.VMEM((D, 3 * wb), B16)],
        ),
        out_shape=[shape((tokens, D), F32), shape((8, D), F32)],
        input_output_aliases={14: 0} if into else {},
        compiler_params=params(),
        cost_estimate=cost(6 * steps * rows * D * D, 20 * steps * rows * D),
        name="input_grad",
    )(tab, da, db, x, dx, *parts_a, *parts_b, gain, *into)


def small_params():
    return pltpu.CompilerParams(vmem_limit_bytes=40 * 1024 * 1024)


def add(a, b):
    return a + b


def stack_body(*refs):
    for i, ref in enumerate(refs[:-1]):
        refs[-1][i] = ref[...]


def stack(parts):
    return pl.pallas_call(
        stack_body,
        out_shape=shape((len(parts), *parts[0].shape), parts[0].dtype),
        compiler_params=small_params(),
        cost_estimate=cost(0, 16 * parts[0].size),
        name="stack",
    )(*parts)


def split_body(a, b, keep, send):
    keep[0] = add(a[0, 0], b[0, 0])
    send[0] = add(a[1, 0], b[1, 0])


def add_split(own, received):
    _, r, w = own.shape
    both = pl.BlockSpec((NX, 1, r, w), lambda i: (0, i, 0, 0))
    one = pl.BlockSpec((1, r, w), lambda i: (i, 0, 0))
    return pl.pallas_call(
        split_body,
        grid=(NZ,),
        in_specs=[both, both],
        out_specs=[one, one],
        out_shape=[shape((NZ, r, w), B16)] * 2,
        compiler_params=params(),
        cost_estimate=cost(8 * r * w, 48 * r * w),
        name="add_split",
    )(own.reshape(NX, NZ, r, w), received.reshape(NX, NZ, r, w))


def halves_body(tab, a0, b0, a1, b1, keep, send):
    keep[...] = add(a0[...], b0[...])
    send[...] = add(a1[...], b1[...])


def add_halves(tab, own, received):
    n, r, w = own.shape
    mine = pl.BlockSpec((2, r, w // 2), lambda i, t: (i, 0, t[9]))
    other = pl.BlockSpec((2, r, w // 2), lambda i, t: (i, 0, 1 - t[9]))
    one = pl.BlockSpec((2, r, w // 2), lambda i, t: (i, 0, 0))
    return pl.pallas_call(
        halves_body,
        grid_spec=pltpu.PrefetchScalarGridSpec(
            num_scalar_prefetch=1, grid=(n // 2,), in_specs=[mine, mine, other, other], out_specs=[one, one]
        ),
        out_shape=[shape((n, r, w // 2), B16)] * 2,
        compiler_params=params(),
        cost_estimate=cost(8 * r * w, 48 * r * w),
        name="add_halves",
    )(tab, own, received, own, received)


def vectors_body(tab, p0, p1, p2, p3, out):
    parts = (p0, p1, p2, p3)
    core = tab[8]
    for t in range(NZ * NX):
        rx, rz = divmod(t, NZ)
        base = tab[t] * 2
        out[pl.ds(base + core, 1), :] = parts[rx][rz, 0:1, :].astype(F32)
        out[pl.ds(base + 1 - core, 1), :] = parts[2 + rx][rz, 0:1, :].astype(F32)


def read_vectors(tab, parts):
    width = parts[0].shape[2]
    part = pl.BlockSpec((NZ, SPARE, width), lambda i, t: (0, ROWS // SPARE, 0))
    return pl.pallas_call(
        vectors_body,
        grid_spec=pltpu.PrefetchScalarGridSpec(
            num_scalar_prefetch=1,
            grid=(1,),
            in_specs=[part] * 4,
            out_specs=pl.BlockSpec((N16, width), lambda i, t: (0, 0)),
        ),
        out_shape=shape((N16, width), F32),
        name="vectors",
    )(tab, *parts)


def parts_body(a, b, *outs):
    for i, out in enumerate(outs):
        out[...] = add(a[i], b[i])


def add_parts(keep, received):
    n, r, w = keep.shape
    return pl.pallas_call(
        parts_body,
        out_shape=[shape((r, w), B16)] * n,
        compiler_params=small_params(),
        cost_estimate=cost(4 * r * w, 24 * r * w),
        name="add_parts",
    )(keep, received)


def four_body(a, b, c, d, out):
    out[...] = ((a[...].astype(F32) + b[...].astype(F32)) + (c[...].astype(F32) + d[...].astype(F32))).astype(B16)


def add_four(parts):
    return pl.pallas_call(
        four_body,
        out_shape=shape(parts[0].shape, B16),
        compiler_params=small_params(),
        cost_estimate=cost(4 * parts[0].size, 10 * parts[0].size),
        name="add_four",
    )(*parts)


def tie(*trees):
    flat, tree = jax.tree.flatten(trees)
    return jax.tree.unflatten(tree, lax.optimization_barrier(flat))


def flip(value, axis, size, by):
    return lax.ppermute(value, axis, [(i, i ^ by) for i in range(size)])


def along_z(value):
    return [flip(value, "z", NZ, by) for by in range(1, NZ)]


def swap_z(parts):
    return [flip(parts[by], "z", NZ, by) for by in range(1, NZ)]


def along_x(value):
    return flip(value, "x", NX, 1)


def across(value):
    return flip(value, "core", 2, 1)


def along_rep(value):
    return flip(value, "rep", 2, 1)


def bounds_of():
    out, at = [], 0
    for heads in FWD_GROUPS:
        out.append((at * HD, (at + heads) * HD))
        at += heads
    return out


def qkv_shards(w_qkv):
    shard = w_qkv.reshape(-1, 3 * D)
    return [jnp.concatenate([shard[:, part * D + a : part * D + b] for part in range(3)], axis=1) for a, b in bounds_of()]


def column_blocks(w):
    return [w[:, j * D : (j + 1) * D] for j in range(w.shape[1] // D)]


def gather_vectors(gains, biases):
    count = 1
    for axis in FSDP:
        count *= lax.axis_size(axis)
    vec = jnp.concatenate([gains, biases])
    vec = lax.all_to_all(
        jnp.broadcast_to(vec[None], (count, vec.shape[0])), FSDP, split_axis=0, concat_axis=0, tiled=True
    ).astype(F32)
    n = gains.shape[0]
    return vec[:, :n].reshape(1, -1), vec[:, n:].reshape(1, -1)


def reduce_small(dgains, dbiases):
    count, reps = 1, lax.axis_size("rep")
    for axis in FSDP:
        count *= lax.axis_size(axis)
    small = jnp.concatenate([dgains.reshape(count, -1), dbiases.reshape(count, -1)], axis=1)
    small = jnp.broadcast_to(small[:, None], (count, reps, small.shape[1])).reshape(count * reps, -1)
    small = lax.all_to_all(small, FSDP + ("rep",), split_axis=0, concat_axis=0, tiled=True)
    small = jnp.sum(small, axis=0)
    n = dgains.shape[0] // count
    return small[:n], small[n:]


def name_vectors(gains_all, biases_all):
    gain_one, gain_two = gains_all[:, :D], gains_all[:, D:]
    shift_one, bias_q, bias_v, bias_o, shift_two = [biases_all[:, i * D : (i + 1) * D] for i in range(5)]
    bias_up, bias_down = biases_all[:, 5 * D : 5 * D + FF], biases_all[:, 5 * D + FF :]
    qkv_bias = [
        jnp.stack([bias_q[:, a:b], jnp.zeros((1, b - a), F32), bias_v[:, a:b]]) for a, b in bounds_of()
    ]
    return gain_one, gain_two, shift_one, shift_two, qkv_bias, bias_o, bias_up, bias_down


def small_gradients(din, dmid, dbias, dc1, dc2):
    dgains = jnp.concatenate([din[0], dmid[0]])
    dbiases = jnp.concatenate(
        [
            din[1],
            jnp.concatenate([db[0, 0] for db in dbias]),
            jnp.concatenate([db[2, 0] for db in dbias]),
            dmid[2],
            dmid[1],
            dc1[0],
            dc2[0],
        ]
    )
    return dgains, dbiases


def join_qkv(grads):
    widths = [b - a for a, b in bounds_of()]
    return jnp.concatenate(
        [g[:, part * w : (part + 1) * w] for part in range(3) for g, w in zip(grads, widths)], axis=1
    ).reshape(-1)


def shards(tokens, w_qkv, w_out, w_fc1, w_fc2, gains, biases, segment, cotangent):
    mz, mx, core = lax.axis_index("z"), lax.axis_index("x"), lax.axis_index("core")
    rep = lax.axis_index("rep")
    tab = jnp.stack(
        [((mz ^ rz) * NX + (mx ^ rx)).astype(jnp.int32) for rx in range(NX) for rz in range(NZ)]
        + [core.astype(jnp.int32), rep.astype(jnp.int32)]
    )
    seg = segment.reshape(1, -1)
    pairs = [(b - a) // 128 for a, b in bounds_of()]
    s0, s1 = qkv_shards(w_qkv)
    vec = jnp.concatenate([gains, biases]).reshape(1, -1)
    s0 = jnp.concatenate([s0, jnp.pad(vec, ((0, SPARE - 1), (0, s0.shape[1] - vec.shape[1])))])
    bulk = jnp.concatenate([w_fc2.reshape(ROWS2, D), *column_blocks(w_fc1.reshape(ROWS, FF)), w_out.reshape(ROWS, D)])
    bulk = lax.dynamic_slice_in_dim(bulk, rep * (BULK // 2), BULK // 2)
    bulk = lax.all_gather(bulk, FSDP + ("rep",), axis=0, tiled=False).reshape(N16, BULK, D)

    z0 = along_z(s0)
    z0, s1 = tie(z0, s1)
    a0 = stack([s0, *z0])
    x0, c0 = along_x(a0), across(a0)
    z1 = along_z(s1)
    x0, c0 = tie(x0, c0)
    w0 = (a0, x0, c0, across(x0))
    vec = read_vectors(tab, w0)
    ngain = gains.shape[0]
    gain_one, gain_two, shift_one, shift_two, qkv_bias, bias_o, bias_up, bias_down = name_vectors(
        vec[:, :ngain].reshape(1, -1), vec[:, ngain : ngain + biases.shape[0]].reshape(1, -1)
    )
    qkv0, h1 = qkv_call(True, tab, tokens, w0, gain_one, shift_one, qkv_bias[0])
    qkv0, z1 = tie(qkv0, z1)
    a1 = stack([s1, *z1])
    x1, c1 = along_x(a1), across(a1)
    o0, lse0 = attend_call(qkv0, seg)
    o0, x1, c1, h1 = tie(o0, x1, c1, h1)
    w1 = (a1, x1, c1, across(x1))
    (qkv1,) = qkv_call(False, tab, h1, w1, gain_one, shift_one, qkv_bias[1])
    o1, lse1 = attend_call(qkv1, seg)
    outs = [o0, o1]
    x1, h2, act, slope = up_call(outs, tokens, bulk, bias_o, gain_two, shift_two, bias_up)

    output, du, dw2, dc1, dc2 = down_call(act, slope, cotangent, x1, bulk, bias_down)
    r2 = lax.psum_scatter(dw2, FSDP, scatter_dimension=0, tiled=True)
    dh, own1, send1 = hidden_call(tab, h2, du, bulk)
    r1 = across(send1)
    dx1, do, dwo, dmid = middle_call(outs, dh, cotangent, x1, bulk, gain_two)
    ro = lax.psum_scatter(dwo, FSDP, scatter_dimension=0, tiled=True)
    do, r1 = tie(do, r1)
    keep, give = add_halves(tab, own1, r1)
    do, give = tie(do, give)
    r1 = along_rep(give)
    d1 = attend_back_call(qkv1, do, o1, lse1, seg, pairs[0])
    d1, r1 = tie(d1, r1)
    own_q, send_q, db1 = weight_call(tab, h1, d1)
    keep, give = add_split(keep, r1)
    send_q, give, do = tie(send_q, give, do)
    rq = across(send_q)
    r1 = along_x(give)
    d0 = attend_back_call(qkv0, do, o0, lse0, seg, 0)
    d0, rq, r1 = tie(d0, rq, r1)
    keepq, giveq = add_split(own_q, rq)
    parts1 = add_parts(keep, r1)
    giveq, parts1, d0 = tie(giveq, parts1, d0)
    rq = along_x(giveq)
    r1 = swap_z(parts1)
    own_p, send_p, db0 = weight_call(tab, h1, d0)
    send_p, dx1 = tie(send_p, dx1)
    rp = across(send_p)
    tokens_rows = dx1.shape[0] // 4
    grad_tokens, din0 = input_call(tab, d0, d1, tokens, dx1, w0, w1, gain_one, 0, 2)
    grad_tokens, rp, rq, r1 = tie(grad_tokens, rp, rq, r1)
    keepp, givep = add_split(own_p, rp)
    partsq = add_parts(keepq, rq)
    total1 = add_four([parts1[0], *r1])
    givep, partsq, total1, grad_tokens = tie(givep, partsq, total1, grad_tokens)
    rp = along_x(givep)
    rq = swap_z(partsq)
    y1 = along_rep(total1)
    grad_tokens, din1 = input_call(tab, d0, d1, tokens, dx1, w0, w1, gain_one, 2, 2, (grad_tokens,))
    din1, rp, rq, y1, r2 = tie(din1, rp, rq, y1, r2)
    partsp = add_parts(keepp, rp)
    rp = swap_z(partsp)
    totalq = add_four([partsq[0], *rq])
    small = reduce_small(*small_gradients(din0 + din1, dmid, (db0, db1), dc1, dc2))
    rest = jnp.concatenate([r2, ro])
    yq, yr = along_rep(totalq), along_rep(rest)
    totalp = add_four([partsp[0], *rp])
    yp = along_rep(totalp)
    gradp = totalp.astype(F32) + yp.astype(F32)
    gradq = totalq.astype(F32) + yq.astype(F32)
    rest = rest.astype(F32) + yr.astype(F32)
    grad1 = jnp.where(rep == 0, jnp.concatenate([total1, y1], axis=1), jnp.concatenate([y1, total1], axis=1))
    return (
        output,
        grad_tokens,
        join_qkv([gradp, gradq]),
        rest[ROWS2:].reshape(-1),
        grad1.astype(F32).reshape(-1),
        rest[:ROWS2].reshape(-1),
        *small,
    )


def gather_any(shard):
    whole = lax.all_gather(shard, FSDP, axis=0, tiled=True)
    blocks = whole.reshape(NZ, NX, 2, -1, whole.shape[1]).transpose(2, 1, 0, 3, 4)
    return blocks[0, 0], blocks[0, 1], blocks[1, 0], blocks[1, 1]


def sum_rows(whole):
    part = lax.psum_scatter(whole, FSDP, scatter_dimension=0, tiled=True)
    return lax.psum(part, "rep").astype(F32)


def reduce_any(own, send):
    blocks = jnp.stack([own, send]).reshape(2, NX, NZ, *own.shape[1:]).transpose(2, 1, 0, 3, 4)
    return sum_rows(blocks.reshape(-1, own.shape[2]))


def shards_any(tokens, w_qkv, w_out, w_fc1, w_fc2, gains, biases, segment, cotangent):
    tab = jnp.asarray([rz * NX + rx for rx in range(NX) for rz in range(NZ)] + [0], jnp.int32)
    seg = segment.reshape(1, -1)
    pairs = [(b - a) // 128 for a, b in bounds_of()]
    w0, w1 = [gather_any(s) for s in qkv_shards(w_qkv)]
    whole = [
        lax.all_gather(w.reshape(-1, n), FSDP, axis=0, tiled=True) for w, n in ((w_fc2, D), (w_fc1, FF), (w_out, D))
    ]
    bulk = jnp.concatenate(
        [b.reshape(N16, -1, D) for w in whole for b in column_blocks(w)], axis=1
    )
    gain_one, gain_two, shift_one, shift_two, qkv_bias, bias_o, bias_up, bias_down = name_vectors(
        *gather_vectors(gains, biases)
    )
    qkv0, h1 = qkv_call(True, tab, tokens, w0, gain_one, shift_one, qkv_bias[0])
    (qkv1,) = qkv_call(False, tab, h1, w1, gain_one, shift_one, qkv_bias[1])
    o0, lse0 = attend_call(qkv0, seg)
    o1, lse1 = attend_call(qkv1, seg)
    outs = [o0, o1]
    x1, h2, act, slope = up_call(outs, tokens, bulk, bias_o, gain_two, shift_two, bias_up)
    output, du, dw2, dc1, dc2 = down_call(act, slope, cotangent, x1, bulk, bias_down)
    dh, own1, send1 = hidden_call(tab, h2, du, bulk)
    dx1, do, dwo, dmid = middle_call(outs, dh, cotangent, x1, bulk, gain_two)
    d1 = attend_back_call(qkv1, do, o1, lse1, seg, pairs[0])
    d0 = attend_back_call(qkv0, do, o0, lse0, seg, 0)
    own_q, send_q, db1 = weight_call(tab, h1, d1)
    own_p, send_p, db0 = weight_call(tab, h1, d0)
    grad_tokens, din = input_call(tab, d0, d1, tokens, dx1, w0, w1, gain_one, 0, 4)
    return (
        output,
        grad_tokens,
        join_qkv([reduce_any(own_p, send_p), reduce_any(own_q, send_q)]),
        sum_rows(dwo).reshape(-1),
        reduce_any(own1, send1).reshape(-1),
        sum_rows(dw2).reshape(-1),
        *reduce_small(*small_gradients(din, dmid, (db0, db1), dc1, dc2)),
    )


def solution(mesh):
    count, reps = mesh.shape["fsdp"], mesh.shape["rep"]
    inner = Mesh(mesh.devices.reshape(count // 4, 2, 2, reps), FSDP + ("rep",))
    rows = P(FSDP + ("rep",), None)
    flat = P(FSDP)
    return jax.shard_map(
        shards if (count, reps) == (2 * NZ * NX, 2) else shards_any,
        mesh=inner,
        in_specs=(rows, flat, flat, flat, flat, flat, flat, P(FSDP + ("rep",)), rows),
        out_specs=(rows, rows, flat, flat, flat, flat, flat, flat),
        check_vma=False,
    )
```

```python
import functools

import jax
import jax.numpy as jnp
from jax import lax
from jax.experimental import pallas as pl
from jax.experimental.pallas import tpu as pltpu
from jax.sharding import Mesh
from jax.sharding import PartitionSpec as P

D = 768
H = 12
HD = 64
FF = 3072
B16 = jnp.bfloat16
F32 = jnp.float32

epsilon_norm = 1e-06
score_scale = 0.125
masked_low = -1e30

FWD_GROUPS = (4, 8)
NZ, NX = 4, 2
ROWS = D // 16
ROWS2 = FF // 16
FSDP = ("z", "x", "core")


def mm(a, b, ca, cb):
    return lax.dot_general(a, b, (((ca,), (cb,)), ((), ())), preferred_element_type=F32)


def params(mib=56):
    return pltpu.CompilerParams(
        dimension_semantics=("arbitrary",), vmem_limit_bytes=mib * 1024 * 1024
    )


def cost(flops, nbytes, trans=0):
    return pl.CostEstimate(flops=int(flops), bytes_accessed=int(nbytes), transcendentals=int(trans))


def shape(dims, dtype):
    return jax.ShapeDtypeStruct(dims, dtype)


def layer_norm(values, gain, shift):
    center = values - jnp.mean(values, axis=-1, keepdims=True)
    spread = jnp.mean(center * center, axis=-1, keepdims=True)
    return center * lax.rsqrt(spread + epsilon_norm) * gain + shift


def layer_norm_back(values, gain, grad):
    center = values - jnp.mean(values, axis=-1, keepdims=True)
    spread = jnp.mean(center * center, axis=-1, keepdims=True)
    inverse = lax.rsqrt(spread + epsilon_norm)
    hat = center * inverse
    grad_hat = grad * gain
    grad_values = inverse * (
        grad_hat
        - jnp.mean(grad_hat, axis=-1, keepdims=True)
        - hat * jnp.mean(grad_hat * hat, axis=-1, keepdims=True)
    )
    return grad_values, jnp.sum(grad * hat, axis=0, keepdims=True), jnp.sum(grad, axis=0, keepdims=True)


def normal(u):
    bell = jnp.exp(u * u * -0.5)
    t = 1.0 / (1.0 + 0.2316418882663604 * jnp.abs(u))
    top = 0.5307027145
    for c in (-0.7265760135, 0.7107068705, -0.142248368, 0.127414796):
        top = top * t + c
    tail = top * t * bell
    return jnp.where(u < 0.0, tail, 1.0 - tail), bell * 0.3989422804014327


def places(tab, rows):
    core = tab[8]
    for t in range(NZ * NX):
        base = tab[t] * 2
        yield (
            t,
            pl.ds(pl.multiple_of((base + core) * rows, 16), rows),
            pl.ds(pl.multiple_of((base + 1 - core) * rows, 16), rows),
        )


def assemble(tab, parts, dest):
    for t, here, there in places(tab, ROWS):
        rx, rz = divmod(t, NZ)
        dest[here, :] = parts[rx][rz]
        dest[there, :] = parts[2 + rx][rz]


def scatter(tab, source, own, send):
    for t, here, there in places(tab, ROWS):
        own[t] = source[here, :]
        send[t] = source[there, :]


def vector(j):
    return pl.BlockSpec((1, D), lambda *_: (0, j))


def qkv_body(first, at, tab, x_ref, p0, p1, p2, p3, gain, biases, *rest):
    step = pl.program_id(0)
    if first:
        out_ref, h_ref, w_s = rest

        @pl.when(step == 0)
        def _():
            h_ref[...] = layer_norm(x_ref[...].astype(F32), gain[...], biases[:, :D]).astype(B16)

        h = h_ref
    else:
        out_ref, w_s = rest
        h = x_ref
    assemble(tab, (p0, p1, p2, p3), w_s)
    bias = [biases[:, part * D + at : part * D + at + w_s.shape[1]] for part in (1, 2)]
    bias = jnp.where(step == 0, bias[0], jnp.where(step == 2, bias[1], 0.0))
    out_ref[0] = (mm(h[...], w_s[...], 1, 0) + bias).astype(B16)


def qkv_call(first, at, tab, x, parts, gains, biases):
    tokens = x.shape[0]
    width = parts[0].shape[2] // 3
    full = pl.BlockSpec((tokens, D), lambda j, t: (0, 0))
    piece = pl.BlockSpec((NZ, ROWS, width), lambda j, t: (0, 0, j))
    outs = [shape((3, tokens, width), B16)]
    out_specs = [pl.BlockSpec((1, tokens, width), lambda j, t: (j, 0, 0))]
    if first:
        outs.append(shape((tokens, D), B16))
        out_specs.append(full)
    return pl.pallas_call(
        functools.partial(qkv_body, first, at),
        grid_spec=pltpu.PrefetchScalarGridSpec(
            num_scalar_prefetch=1,
            grid=(3,),
            in_specs=[full, piece, piece, piece, piece, vector(0), pl.BlockSpec(biases.shape, lambda j, t: (0, 0))],
            out_specs=out_specs,
            scratch_shapes=[pltpu.VMEM((D, width), B16)],
        ),
        out_shape=outs,
        compiler_params=params(),
        cost_estimate=cost(6 * tokens * D * width, 8 * tokens * D),
        name="qkv_first" if first else "qkv_next",
    )(tab, x, *parts, gains, biases)


def make_mask(seg_ref, mask):
    @pl.when(pl.program_id(0) == 0)
    def _():
        row = seg_ref[...].astype(F32)
        mask[...] = jnp.where(row.T == row, 0.0, masked_low)


def attend_body(rows, q_ref, k_ref, v_ref, seg_ref, o_ref, lse_ref, mask):
    make_mask(seg_ref, mask)
    tokens = q_ref.shape[1]
    for h in range(2):
        cols = slice(h * HD, (h + 1) * HD)
        k = k_ref[0, :, cols]
        v = v_ref[0, :, cols]
        for b in range(tokens // rows):
            r = slice(b * rows, (b + 1) * rows)
            q = q_ref[0, r, cols] * jnp.asarray(score_scale, B16)
            s = mm(q, k, 1, 1) + mask[r, :]
            top = jnp.max(s, axis=-1, keepdims=True)
            p = jnp.exp(s - top)
            total = jnp.sum(p, axis=-1, keepdims=True)
            o_ref[r, cols] = (mm(p.astype(B16), v, 1, 0) * (1.0 / total)).astype(B16)
            lse_ref[0, h : h + 1, r] = (top + jnp.log(total)).T


def attend_call(qkv, seg, start=0, pairs=None):
    _, tokens, width = qkv.shape
    pairs = pairs or width // 128
    width = pairs * 128
    head = lambda j: pl.BlockSpec((1, tokens, 128), lambda i: (j, 0, i + start))
    return pl.pallas_call(
        functools.partial(attend_body, min(512, tokens)),
        grid=(pairs,),
        in_specs=[head(0), head(1), head(2), pl.BlockSpec((1, tokens), lambda i: (0, 0))],
        out_specs=[
            pl.BlockSpec((tokens, 128), lambda i: (0, i)),
            pl.BlockSpec((1, 2, tokens), lambda i: (i, 0, 0)),
        ],
        out_shape=[shape((tokens, width), B16), shape((pairs, 2, tokens), F32)],
        scratch_shapes=[pltpu.VMEM((tokens, tokens), F32)],
        compiler_params=params(),
        cost_estimate=cost(pairs * 16 * 128 * tokens * tokens, 8 * tokens * width, pairs * 2 * tokens * tokens),
        name="attend",
    )(qkv, qkv, qkv, seg)


BULK = ROWS2 + 4 * ROWS + ROWS
N16 = 16
SPARE = 16


def up_body(count, *refs):
    outs, (x_ref, wo_ref, wa, wb, wc, wd, gain, biases) = refs[:count], refs[count : count + 8]
    x1_ref, h2_ref, act_ref, slope_ref = refs[count + 8 :]
    x1 = x_ref[...].astype(F32) + biases[:, 3 * D : 4 * D]
    wo = wo_ref[...].reshape(D, D)
    at = 0
    for o in outs:
        x1 = x1 + mm(o[...], wo[at : at + o.shape[1], :], 1, 0)
        at += o.shape[1]
    x1_ref[...] = x1
    h2 = layer_norm(x1, gain[...], biases[:, 4 * D : 5 * D]).astype(B16)
    h2_ref[...] = h2
    tile = D // 2
    for f in range(FF // tile):
        cols = slice(f * tile, (f + 1) * tile)
        w = (wa, wb, wc, wd)[f // 2][:, :, (f % 2) * tile : (f % 2 + 1) * tile].reshape(D, tile)
        u = mm(h2, w, 1, 0) + biases[:, 5 * D + f * tile : 5 * D + (f + 1) * tile]
        cdf, density = normal(u)
        act_ref[:, cols] = (u * cdf).astype(B16)
        slope_ref[:, cols] = (cdf + u * density).astype(B16)


def bulk_block(j):
    return pl.BlockSpec((N16, ROWS, D), lambda i: (0, j, 0), pipeline_mode=pl.Buffered(1))


def up_call(outs, x, bulk, gains, biases):
    tokens = x.shape[0]
    rows = min(256, tokens)
    block = lambda w: pl.BlockSpec((rows, w), lambda i: (i, 0))
    return pl.pallas_call(
        functools.partial(up_body, len(outs)),
        grid=(tokens // rows,),
        in_specs=[block(o.shape[1]) for o in outs]
        + [block(D)]
        + [bulk_block(j) for j in (8, 4, 5, 6, 7)]
        + [vector(1), pl.BlockSpec(biases.shape, lambda i: (0, 0))],
        out_specs=[block(D), block(D), block(FF), block(FF)],
        out_shape=[shape((tokens, D), F32), shape((tokens, D), B16), shape((tokens, FF), B16), shape((tokens, FF), B16)],
        compiler_params=params(),
        cost_estimate=cost(2 * tokens * D * (D + FF), 30 * tokens * D, tokens * FF),
        name="up",
    )(*outs, x, bulk, bulk, bulk, bulk, bulk, gains, biases)


def down_body(act_ref, slope_ref, dy_ref, w_ref, du_ref, dw_ref, dc1, dc2):
    @pl.when(pl.program_id(0) == 0)
    def _():
        dc2[...] = jnp.sum(dy_ref[...].astype(F32), axis=0, keepdims=True)

    dy = dy_ref[...]
    du = (mm(dy, w_ref[...].reshape(D, D), 1, 1) * slope_ref[...].astype(F32)).astype(B16)
    du_ref[...] = du
    dc1[...] = jnp.sum(du.astype(F32), axis=0, keepdims=True)
    dw_ref[...] = mm(act_ref[...], dy, 0, 0).astype(B16)


def down_call(act, slope, dy, bulk):
    tokens = dy.shape[0]
    ff = pl.BlockSpec((tokens, D), lambda i: (0, i))
    return pl.pallas_call(
        down_body,
        grid=(FF // D,),
        in_specs=[
            ff,
            ff,
            pl.BlockSpec((tokens, D), lambda i: (0, 0)),
            pl.BlockSpec((N16 // 4, ROWS2, D), lambda i: (i, 0, 0)),
        ],
        out_specs=[
            ff,
            pl.BlockSpec((D, D), lambda i: (i, 0)),
            vector_step(),
            pl.BlockSpec((1, D), lambda i: (0, 0)),
        ],
        out_shape=[shape((tokens, FF), B16), shape((FF, D), B16), shape((1, FF), F32), shape((1, D), F32)],
        compiler_params=params(),
        cost_estimate=cost(4 * tokens * D * FF, 30 * tokens * D),
        name="down",
    )(act, slope, dy, bulk)


def vector_step():
    return pl.BlockSpec((1, D), lambda i: (0, i))


def finish_body(act_ref, x1_ref, w_ref, c2, *refs):
    refs[-1][...] = (x1_ref[...] + c2[...] + mm(act_ref[...], w_ref[...].reshape(FF, D), 1, 0)).astype(B16)


def finish_call(act, x1, bulk, biases, start, steps, into=()):
    tokens = x1.shape[0]
    rows = tokens // 4
    block = lambda w: pl.BlockSpec((rows, w), lambda i: (i + start, 0))
    return pl.pallas_call(
        finish_body,
        grid=(steps,),
        in_specs=[
            block(FF),
            block(D),
            pl.BlockSpec((N16, ROWS2, D), lambda i: (0, 0, 0), pipeline_mode=pl.Buffered(1)),
            vector(9),
        ]
        + [pl.BlockSpec(memory_space=pl.ANY)] * len(into),
        out_specs=block(D),
        out_shape=shape((tokens, D), B16),
        input_output_aliases={4: 0} if into else {},
        compiler_params=params(),
        cost_estimate=cost(2 * steps * rows * D * FF, 20 * steps * rows * D),
        name="finish",
    )(act, x1, bulk, biases, *into)


def hidden_body(tab, h2_ref, du_ref, w_ref, acc, own, send, dw):
    @pl.when(pl.program_id(0) == 0)
    def _():
        acc[...] = jnp.zeros_like(acc)

    du = du_ref[...]
    dw[...] = mm(h2_ref[...], du, 0, 0).astype(B16)
    acc[...] += mm(du, w_ref[...].reshape(D, D), 1, 1)
    scatter(tab, dw, own, send)


def hidden_call(tab, h2, du, bulk):
    tokens = h2.shape[0]
    full = pl.BlockSpec((tokens, D), lambda i, t: (0, 0), pipeline_mode=pl.Buffered(1))
    piece = pl.BlockSpec((8, ROWS, D), lambda i, t: (0, 0, i))
    pieces = shape((8, ROWS, FF), B16)
    return pl.pallas_call(
        hidden_body,
        grid_spec=pltpu.PrefetchScalarGridSpec(
            num_scalar_prefetch=1,
            grid=(FF // D,),
            in_specs=[
                full,
                pl.BlockSpec((tokens, D), lambda i, t: (0, i)),
                pl.BlockSpec((N16, ROWS, D), lambda i, t: (0, 4 + i, 0)),
            ],
            out_specs=[pl.BlockSpec((tokens, D), lambda i, t: (0, 0)), piece, piece],
            scratch_shapes=[pltpu.VMEM((D, D), B16)],
        ),
        out_shape=[shape((tokens, D), F32), pieces, pieces],
        compiler_params=params(),
        cost_estimate=cost(4 * tokens * D * FF, 20 * tokens * D),
        name="hidden",
    )(tab, h2, du, bulk)


def middle_body(count, *refs):
    outs, (dh_ref, dy_ref, x1_ref, w_ref, gain) = refs[:count], refs[count : count + 5]
    dx_ref, do_ref, dw_ref, dvec = refs[count + 5 :]
    grad, dgain, dshift = layer_norm_back(x1_ref[...], gain[...], dh_ref[...])
    dx = dy_ref[...].astype(F32) + grad
    dx_ref[...] = dx
    da = dx.astype(B16)
    dvec[0:1, :] = dgain
    dvec[1:2, :] = dshift
    dvec[2:3, :] = jnp.sum(da.astype(F32), axis=0, keepdims=True)
    do_ref[...] = mm(da, w_ref[...].reshape(D, D), 1, 1).astype(B16)
    at = 0
    for o in outs:
        dw_ref[at : at + o.shape[1], :] = mm(o[...], da, 0, 0).astype(B16)
        at += o.shape[1]


def middle_call(outs, dh, dy, x1, bulk, gains):
    tokens = dy.shape[0]
    full = lambda w: pl.BlockSpec((tokens, w), lambda i: (0, 0))
    return pl.pallas_call(
        functools.partial(middle_body, len(outs)),
        grid=(1,),
        in_specs=[full(o.shape[1]) for o in outs]
        + [full(D), full(D), full(D)]
        + [pl.BlockSpec((N16, ROWS, D), lambda i: (0, 8, 0)), vector(1)],
        out_specs=[full(D), full(D), pl.BlockSpec((D, D), lambda i: (0, 0)), pl.BlockSpec((8, D), lambda i: (0, 0))],
        out_shape=[shape((tokens, D), F32), shape((tokens, D), B16), shape((D, D), B16), shape((8, D), F32)],
        compiler_params=params(),
        cost_estimate=cost(4 * tokens * D * D, 20 * tokens * D),
        name="middle",
    )(*outs, dh, dy, x1, bulk, gains)


def attend_back_body(rows, q_ref, k_ref, v_ref, do_ref, o_ref, lse_ref, seg_ref, out_ref, mask):
    make_mask(seg_ref, mask)
    tokens = q_ref.shape[1]
    for h in range(2):
        cols = slice(h * HD, (h + 1) * HD)
        k = k_ref[0, :, cols]
        v = v_ref[0, :, cols]
        dk = jnp.zeros((HD, tokens), F32)
        dv = jnp.zeros((HD, tokens), F32)
        for b in range(tokens // rows):
            r = slice(b * rows, (b + 1) * rows)
            q = q_ref[0, r, cols] * jnp.asarray(score_scale, B16)
            do = do_ref[r, cols]
            centre = jnp.sum(do.astype(F32) * o_ref[r, cols].astype(F32), axis=1, keepdims=True)
            s = mm(q, k, 1, 1) + mask[r, :]
            p = jnp.exp(s - lse_ref[0, h : h + 1, r].T)
            da = mm(do, v, 1, 1)
            ds = (p * (da - centre)).astype(B16)
            dv = dv + mm(do.T, p.astype(B16), 1, 0)
            dk = dk + mm(q.T, ds, 1, 0)
            out_ref[0, r, cols] = (mm(ds, k, 1, 0) * score_scale).astype(B16)
        out_ref[1, :, cols] = dk.T.astype(B16)
        out_ref[2, :, cols] = dv.T.astype(B16)


def attend_back_call(qkv, do, o, lse, seg, first_pair):
    _, tokens, width = qkv.shape
    pairs = width // 128
    head = lambda j: pl.BlockSpec((1, tokens, 128), lambda i: (j, 0, i))
    return pl.pallas_call(
        functools.partial(attend_back_body, min(512, tokens)),
        grid=(pairs,),
        in_specs=[
            head(0),
            head(1),
            head(2),
            pl.BlockSpec((tokens, 128), lambda i: (0, i + first_pair)),
            pl.BlockSpec((tokens, 128), lambda i: (0, i)),
            pl.BlockSpec((1, 2, tokens), lambda i: (i, 0, 0)),
            pl.BlockSpec((1, tokens), lambda i: (0, 0)),
        ],
        out_specs=pl.BlockSpec((3, tokens, 128), lambda i: (0, 0, i)),
        out_shape=shape((3, tokens, width), B16),
        scratch_shapes=[pltpu.VMEM((tokens, tokens), F32)],
        compiler_params=params(),
        cost_estimate=cost(pairs * 40 * 128 * tokens * tokens, 16 * tokens * width, pairs * 2 * tokens * tokens),
        name="attend_back",
    )(qkv, qkv, qkv, do, o, lse, seg)


def weight_body(tab, h_ref, d_ref, din0, din1, dmid, dc1, dc2, own, send, dw, line, rows):
    step = pl.program_id(0)

    @pl.when(step == 0)
    def _():
        din = din0[...] + din1[...]
        line[:, :D] = din[0:1]
        line[:, D : 2 * D] = dmid[0:1, :]
        for at, piece in ((2, din[1:2]), (3, din[2:3]), (4, din[3:4]), (5, dmid[2:3, :]), (6, dmid[1:2, :])):
            line[:, at * D : (at + 1) * D] = piece
        line[:, 7 * D : 7 * D + FF] = dc1[...]
        line[:, 7 * D + FF :] = dc2[...]
        rows[...] = jnp.zeros_like(rows)
        gains, biases = 2 * D // N16, (6 * D + FF) // N16
        for c in range(N16):
            rows[c : c + 1, :gains] = line[:, c * gains : (c + 1) * gains]
            rows[c : c + 1, gains : gains + biases] = line[:, 2 * D + c * biases : 2 * D + (c + 1) * biases]

    width = d_ref.shape[2]
    dw[...] = mm(h_ref[...], d_ref[0], 0, 0).astype(B16)
    core = tab[8]
    for t, here, there in places(tab, ROWS):
        own[t, :ROWS, :] = dw[here, :]
        send[t, :ROWS, :] = dw[there, :]
    for t in range(NZ * NX):
        base = tab[t] * 2
        for out, row in ((own, base + core), (send, base + 1 - core)):
            picked = rows[pl.ds(row, 1), pl.ds(pl.multiple_of(step * width, 128), width)]
            out[t, ROWS:, :] = jnp.broadcast_to(picked, (SPARE, width)).astype(B16)


def weight_call(tab, h1, dqkv, din0, din1, dmid, dc1, dc2):
    _, tokens, width = dqkv.shape
    piece = pl.BlockSpec((8, ROWS + SPARE, width), lambda j, t: (0, 0, j))
    pieces = shape((8, ROWS + SPARE, 3 * width), B16)
    whole = lambda v: pl.BlockSpec(v.shape, lambda j, t: (0, 0))
    return pl.pallas_call(
        weight_body,
        grid_spec=pltpu.PrefetchScalarGridSpec(
            num_scalar_prefetch=1,
            grid=(3,),
            in_specs=[
                pl.BlockSpec((tokens, D), lambda j, t: (0, 0)),
                pl.BlockSpec((1, tokens, width), lambda j, t: (j, 0, 0)),
            ]
            + [whole(v) for v in (din0, din1, dmid, dc1, dc2)],
            out_specs=[piece, piece],
            scratch_shapes=[
                pltpu.VMEM((D, width), B16),
                pltpu.VMEM((1, 8 * D + FF), F32),
                pltpu.VMEM((N16, 3 * width), F32),
            ],
        ),
        out_shape=[pieces, pieces],
        compiler_params=params(),
        cost_estimate=cost(6 * tokens * D * width, 12 * tokens * width),
        name="qkv_weight",
    )(tab, h1, dqkv, din0, din1, dmid, dc1, dc2)


def joint_body(h_ref, d_ref, o_ref, dw):
    width = d_ref.shape[2]
    dw[:, :width] = mm(h_ref[...], d_ref[0], 0, 0).astype(B16)
    dw[:, width:] = o_ref[...]


def joint_call(h1, dqkv, dwo):
    _, tokens, width = dqkv.shape
    side = D // 3
    return pl.pallas_call(
        joint_body,
        grid=(3,),
        in_specs=[
            pl.BlockSpec((tokens, D), lambda j: (0, 0)),
            pl.BlockSpec((1, tokens, width), lambda j: (j, 0, 0)),
            pl.BlockSpec((D, side), lambda j: (0, j)),
        ],
        out_specs=pl.BlockSpec((D, width + side), lambda j: (0, j)),
        out_shape=shape((D, 3 * (width + side)), B16),
        compiler_params=params(),
        cost_estimate=cost(6 * tokens * D * width, 12 * tokens * width),
        name="joint_weight",
    )(h1, dqkv, dwo)


def split_joint(total):
    side = D // 3
    parts = jnp.split(total, 3, axis=1)
    width = parts[0].shape[1] - side
    return jnp.concatenate([p[:, :width] for p in parts], axis=1), jnp.concatenate([p[:, width:] for p in parts], axis=1)


def input_body(tab, da_ref, db_ref, x_ref, dx_ref, a0, a1, a2, a3, b0, b1, b2, b3, gain, *refs):
    out_ref, dvec, wa, wb = refs[-4:]
    step = pl.program_id(0)

    @pl.when(step == 0)
    def _():
        assemble(tab, (a0, a1, a2, a3), wa)
        assemble(tab, (b0, b1, b2, b3), wb)
        dvec[...] = jnp.zeros_like(dvec)

    dh, at = None, 0
    for d_ref, w in ((da_ref, wa), (db_ref, wb)):
        width = d_ref.shape[2]
        for j in range(3):
            term = mm(d_ref[j], w[:, j * width : (j + 1) * width], 1, 1)
            dh = term if dh is None else dh + term
        for j, row in ((0, 2), (2, 3)):
            dvec[row : row + 1, at : at + width] += jnp.sum(d_ref[j].astype(F32), axis=0, keepdims=True)
        at += width
    grad, dgain, dshift = layer_norm_back(x_ref[...].astype(F32), gain[...], dh)
    out_ref[...] = dx_ref[...] + grad
    dvec[0:1, :] += dgain
    dvec[1:2, :] += dshift


def input_call(tab, da, db, x, dx, parts_a, parts_b, gain, start, steps, into=()):
    tokens = x.shape[0]
    rows = tokens // 4
    wa, wb = da.shape[2], db.shape[2]
    grads = lambda w: pl.BlockSpec((3, rows, w), lambda i, t: (0, i + start, 0))
    block = pl.BlockSpec((rows, D), lambda i, t: (i + start, 0))
    piece = lambda w: pl.BlockSpec((NZ, ROWS, 3 * w), lambda i, t: (0, 0, 0), pipeline_mode=pl.Buffered(1))
    return pl.pallas_call(
        input_body,
        grid_spec=pltpu.PrefetchScalarGridSpec(
            num_scalar_prefetch=1,
            grid=(steps,),
            in_specs=[grads(wa), grads(wb), block, block]
            + [piece(wa)] * 4
            + [piece(wb)] * 4
            + [vector(0)]
            + [pl.BlockSpec(memory_space=pl.ANY)] * len(into),
            out_specs=[block, pl.BlockSpec((8, D), lambda i, t: (0, 0))],
            scratch_shapes=[pltpu.VMEM((D, 3 * wa), B16), pltpu.VMEM((D, 3 * wb), B16)],
        ),
        out_shape=[shape((tokens, D), F32), shape((8, D), F32)],
        input_output_aliases={14: 0} if into else {},
        compiler_params=params(),
        cost_estimate=cost(6 * steps * rows * D * D, 20 * steps * rows * D),
        name="input_grad",
    )(tab, da, db, x, dx, *parts_a, *parts_b, gain, *into)


def small_params():
    return pltpu.CompilerParams(vmem_limit_bytes=40 * 1024 * 1024)


def add(a, b):
    return a + b


def stack_body(*refs):
    for i, ref in enumerate(refs[:-1]):
        refs[-1][i] = ref[...]


def stack(parts):
    return pl.pallas_call(
        stack_body,
        out_shape=shape((len(parts), *parts[0].shape), parts[0].dtype),
        compiler_params=small_params(),
        cost_estimate=cost(0, 16 * parts[0].size),
        name="stack",
    )(*parts)


def split_body(grid, a, b, keep, send):
    if grid:
        keep[0] = add(a[0, 0], b[0, 0])
        send[0] = add(a[1, 0], b[1, 0])
    else:
        keep[...] = add(a[0], b[0])
        send[...] = add(a[1], b[1])


def add_split(own, received, grid=True):
    _, r, w = own.shape
    both = pl.BlockSpec((NX, 1, r, w), lambda i: (0, i, 0, 0))
    one = pl.BlockSpec((1, r, w), lambda i: (i, 0, 0))
    how = dict(grid=(NZ,), in_specs=[both, both], out_specs=[one, one], compiler_params=params())
    return pl.pallas_call(
        functools.partial(split_body, grid),
        out_shape=[shape((NZ, r, w), B16)] * 2,
        cost_estimate=cost(8 * r * w, 48 * r * w),
        name="add_split",
        **(how if grid else dict(compiler_params=small_params())),
    )(own.reshape(NX, NZ, r, w), received.reshape(NX, NZ, r, w))


def halves_body(tab, a0, b0, a1, b1, keep, send):
    keep[...] = add(a0[...], b0[...])
    send[...] = add(a1[...], b1[...])


def add_halves(tab, own, received):
    n, r, w = own.shape
    mine = pl.BlockSpec((2, r, w // 2), lambda i, t: (i, 0, t[9]))
    other = pl.BlockSpec((2, r, w // 2), lambda i, t: (i, 0, 1 - t[9]))
    one = pl.BlockSpec((2, r, w // 2), lambda i, t: (i, 0, 0))
    return pl.pallas_call(
        halves_body,
        grid_spec=pltpu.PrefetchScalarGridSpec(
            num_scalar_prefetch=1, grid=(n // 2,), in_specs=[mine, mine, other, other], out_specs=[one, one]
        ),
        out_shape=[shape((n, r, w // 2), B16)] * 2,
        compiler_params=params(),
        cost_estimate=cost(8 * r * w, 48 * r * w),
        name="add_halves",
    )(tab, own, received, own, received)


def vectors_body(tab, p0, p1, p2, p3, gains, biases, rows):
    parts = (p0, p1, p2, p3)
    core = tab[8]
    for t in range(NZ * NX):
        rx, rz = divmod(t, NZ)
        base = tab[t] * 2
        rows[pl.ds(base + core, 1), :] = parts[rx][rz, 0:1, :].astype(F32)
        rows[pl.ds(base + 1 - core, 1), :] = parts[2 + rx][rz, 0:1, :].astype(F32)
    at = 0
    for out in (gains, biases):
        n = out.shape[1] // N16
        for c in range(N16):
            out[:, c * n : (c + 1) * n] = rows[c : c + 1, at : at + n]
        at += n


def read_vectors(tab, parts, ngain, nbias):
    width = parts[0].shape[2]
    part = pl.BlockSpec((NZ, SPARE, width), lambda i, t: (0, ROWS // SPARE, 0))
    whole = lambda n: pl.BlockSpec((1, N16 * n), lambda i, t: (0, 0))
    return pl.pallas_call(
        vectors_body,
        grid_spec=pltpu.PrefetchScalarGridSpec(
            num_scalar_prefetch=1,
            grid=(1,),
            in_specs=[part] * 4,
            out_specs=[whole(ngain), whole(nbias)],
            scratch_shapes=[pltpu.VMEM((N16, width), F32)],
        ),
        out_shape=[shape((1, N16 * ngain), F32), shape((1, N16 * nbias), F32)],
        name="vectors",
    )(tab, *parts)


def parts_body(a, b, *outs):
    for i, out in enumerate(outs):
        out[...] = add(a[i], b[i])


def add_parts(keep, received):
    n, r, w = keep.shape
    return pl.pallas_call(
        parts_body,
        out_shape=[shape((r, w), B16)] * n,
        compiler_params=small_params(),
        cost_estimate=cost(4 * r * w, 24 * r * w),
        name="add_parts",
    )(keep, received)


def four_body(a, b, c, d, out):
    out[...] = ((a[...].astype(F32) + b[...].astype(F32)) + (c[...].astype(F32) + d[...].astype(F32))).astype(B16)


def add_four(parts):
    return pl.pallas_call(
        four_body,
        out_shape=shape(parts[0].shape, B16),
        compiler_params=small_params(),
        cost_estimate=cost(4 * parts[0].size, 10 * parts[0].size),
        name="add_four",
    )(*parts)


def tie(*trees):
    flat, tree = jax.tree.flatten(trees)
    return jax.tree.unflatten(tree, lax.optimization_barrier(flat))


def flip(value, axis, size, by):
    return lax.ppermute(value, axis, [(i, i ^ by) for i in range(size)])


def along_z(value):
    return [flip(value, "z", NZ, by) for by in range(1, NZ)]


def swap_z(parts):
    return [flip(parts[by], "z", NZ, by) for by in range(1, NZ)]


def along_x(value):
    return flip(value, "x", NX, 1)


def across(value):
    return flip(value, "core", 2, 1)


def along_rep(value):
    return flip(value, "rep", 2, 1)


def bounds_of():
    out, at = [], 0
    for heads in FWD_GROUPS:
        out.append((at * HD, (at + heads) * HD))
        at += heads
    return out


def qkv_shards(w_qkv):
    shard = w_qkv.reshape(-1, 3 * D)
    return [jnp.concatenate([shard[:, part * D + a : part * D + b] for part in range(3)], axis=1) for a, b in bounds_of()]


def column_blocks(w):
    return [w[:, j * D : (j + 1) * D] for j in range(w.shape[1] // D)]


def gather_vectors(gains, biases):
    count = 1
    for axis in FSDP:
        count *= lax.axis_size(axis)
    vec = jnp.concatenate([gains, biases])
    vec = lax.all_to_all(
        jnp.broadcast_to(vec[None], (count, vec.shape[0])), FSDP, split_axis=0, concat_axis=0, tiled=True
    ).astype(F32)
    n = gains.shape[0]
    return vec[:, :n].reshape(1, -1), vec[:, n:].reshape(1, -1)


def reduce_small(dgains, dbiases):
    count, reps = 1, lax.axis_size("rep")
    for axis in FSDP:
        count *= lax.axis_size(axis)
    small = jnp.concatenate([dgains.reshape(count, -1), dbiases.reshape(count, -1)], axis=1)
    small = jnp.broadcast_to(small[:, None], (count, reps, small.shape[1])).reshape(count * reps, -1)
    small = lax.all_to_all(small, FSDP + ("rep",), split_axis=0, concat_axis=0, tiled=True)
    small = jnp.sum(small, axis=0)
    n = dgains.shape[0] // count
    return small[:n], small[n:]


def small_gradients(din, dmid, dc1, dc2):
    dgains = jnp.concatenate([din[0], dmid[0]])
    dbiases = jnp.concatenate([din[1], din[2], din[3], dmid[2], dmid[1], dc1[0], dc2[0]])
    return dgains, dbiases


def join_qkv(grads):
    widths = [b - a for a, b in bounds_of()]
    return jnp.concatenate(
        [g[:, part * w : (part + 1) * w] for part in range(3) for g, w in zip(grads, widths)], axis=1
    ).reshape(-1)


def shards(tokens, w_qkv, w_out, w_fc1, w_fc2, gains, biases, segment, cotangent):
    mz, mx, core = lax.axis_index("z"), lax.axis_index("x"), lax.axis_index("core")
    rep = lax.axis_index("rep")
    tab = jnp.stack(
        [((mz ^ rz) * NX + (mx ^ rx)).astype(jnp.int32) for rx in range(NX) for rz in range(NZ)]
        + [core.astype(jnp.int32), rep.astype(jnp.int32)]
    )
    seg = segment.reshape(1, -1)
    pairs = [(b - a) // 128 for a, b in bounds_of()]
    starts = [a for a, _ in bounds_of()]
    s0, s1 = qkv_shards(w_qkv)
    vec = jnp.concatenate([gains, biases]).reshape(1, -1)
    s0 = jnp.concatenate([s0, jnp.pad(vec, ((0, SPARE - 1), (0, s0.shape[1] - vec.shape[1])))])
    bulk = jnp.concatenate([w_fc2.reshape(ROWS2, D), *column_blocks(w_fc1.reshape(ROWS, FF)), w_out.reshape(ROWS, D)])
    bulk = lax.dynamic_slice_in_dim(bulk, rep * (BULK // 2), BULK // 2)
    bulk = lax.all_gather(bulk, FSDP + ("rep",), axis=0, tiled=False).reshape(N16, BULK, D)

    z0 = along_z(s0)
    z0, s1 = tie(z0, s1)
    a0 = stack([s0, *z0])
    x0, c0 = along_x(a0), across(a0)
    z1 = along_z(s1)
    x0, c0 = tie(x0, c0)
    w0 = (a0, x0, c0, across(x0))
    gain_all, bias_all = read_vectors(tab, w0, gains.shape[0], biases.shape[0])
    qkv0, h1 = qkv_call(True, starts[0], tab, tokens, w0, gain_all, bias_all)
    qkv0, z1 = tie(qkv0, z1)
    a1 = stack([s1, *z1])
    x1, c1 = along_x(a1), across(a1)
    o0, lse0 = attend_call(qkv0, seg)
    o0, x1, c1, h1 = tie(o0, x1, c1, h1)
    w1 = (a1, x1, c1, across(x1))
    (qkv1,) = qkv_call(False, starts[1], tab, h1, w1, gain_all, bias_all)
    o1, lse1 = attend_call(qkv1, seg)
    outs = [o0, o1]
    x1, h2, act, slope = up_call(outs, tokens, bulk, gain_all, bias_all)

    du, dw2, dc1, dc2 = down_call(act, slope, cotangent, bulk)
    r2 = lax.psum_scatter(dw2, FSDP, scatter_dimension=0, tiled=True)
    dh, own1, send1 = hidden_call(tab, h2, du, bulk)
    r1 = across(send1)
    dx1, do, dwo, dmid = middle_call(outs, dh, cotangent, x1, bulk, gain_all)
    do, r1 = tie(do, r1)
    keep, give = add_halves(tab, own1, r1)
    do, give = tie(do, give)
    r1 = along_rep(give)
    d1 = attend_back_call(qkv1, do, o1, lse1, seg, pairs[0])
    d1, r1 = tie(d1, r1)
    dwq = joint_call(h1, d1, dwo)
    rq = lax.psum_scatter(dwq, FSDP, scatter_dimension=0, tiled=True)
    keep, give = add_split(keep, r1)
    dwq, give, do = tie(dwq, give, do)
    r1 = along_x(give)
    d0 = attend_back_call(qkv0, do, o0, lse0, seg, 0)
    d0, r1 = tie(d0, r1)
    parts1 = add_parts(keep, r1)
    parts1, d0 = tie(parts1, d0)
    r1 = swap_z(parts1)
    grad_tokens, din0 = input_call(tab, d0, d1, tokens, dx1, w0, w1, gain_all, 0, 2)
    grad_tokens, r1, r2 = tie(grad_tokens, r1, r2)
    total1 = add_four([parts1[0], *r1])
    total1, grad_tokens, r2 = tie(total1, grad_tokens, r2)
    y1, y2 = along_rep(total1), along_rep(r2)
    grad_tokens, din1 = input_call(tab, d0, d1, tokens, dx1, w0, w1, gain_all, 2, 2, (grad_tokens,))
    own_p, send_p = weight_call(tab, h1, d0, din0, din1, dmid, dc1, dc2)
    send_p, y1, y2 = tie(send_p, y1, y2)
    rp = across(send_p)
    keepp, givep = add_split(own_p, rp, False)
    givep, act = tie(givep, act)
    rp = along_x(givep)
    output = finish_call(act, x1, bulk, bias_all, 0, 2)
    output, rp = tie(output, rp)
    partsp = add_parts(keepp, rp)
    partsp, output = tie(partsp, output)
    rp = swap_z(partsp)
    output = finish_call(act, x1, bulk, bias_all, 2, 2, (output,))
    output, rp, rq = tie(output, rp, rq)
    totalp = add_four([partsp[0], *rp])
    yp, yq = along_rep(totalp), along_rep(rq)
    gradp = totalp.astype(F32) + yp.astype(F32)
    small = gradp[ROWS, : gains.shape[0] + biases.shape[0]]
    gradq, grado = split_joint(rq.astype(F32) + yq.astype(F32))
    grad1 = jnp.where(rep == 0, jnp.concatenate([total1, y1], axis=1), jnp.concatenate([y1, total1], axis=1))
    return (
        output,
        grad_tokens,
        join_qkv([gradp[:ROWS], gradq]),
        grado.reshape(-1),
        grad1.astype(F32).reshape(-1),
        (r2.astype(F32) + y2.astype(F32)).reshape(-1),
        small[: gains.shape[0]],
        small[gains.shape[0] :],
    )


def gather_any(shard):
    whole = lax.all_gather(shard, FSDP, axis=0, tiled=True)
    blocks = whole.reshape(NZ, NX, 2, -1, whole.shape[1]).transpose(2, 1, 0, 3, 4)
    return blocks[0, 0], blocks[0, 1], blocks[1, 0], blocks[1, 1]


def sum_rows(whole):
    part = lax.psum_scatter(whole, FSDP, scatter_dimension=0, tiled=True)
    return lax.psum(part, "rep").astype(F32)


def reduce_any(own, send):
    blocks = jnp.stack([own, send]).reshape(2, NX, NZ, *own.shape[1:]).transpose(2, 1, 0, 3, 4)
    return sum_rows(blocks.reshape(-1, own.shape[2]))


def shards_any(tokens, w_qkv, w_out, w_fc1, w_fc2, gains, biases, segment, cotangent):
    tab = jnp.asarray([rz * NX + rx for rx in range(NX) for rz in range(NZ)] + [0], jnp.int32)
    seg = segment.reshape(1, -1)
    pairs = [(b - a) // 128 for a, b in bounds_of()]
    w0, w1 = [gather_any(s) for s in qkv_shards(w_qkv)]
    lower, wide, out = [
        lax.all_gather(w.reshape(-1, n), FSDP, axis=0, tiled=True) for w, n in ((w_fc2, D), (w_fc1, FF), (w_out, D))
    ]
    bulk = jnp.concatenate([b.reshape(N16, -1, D) for b in (lower, *column_blocks(wide), out)], axis=1)
    gain_all, bias_all = gather_vectors(gains, biases)
    starts = [a for a, _ in bounds_of()]
    qkv0, h1 = qkv_call(True, starts[0], tab, tokens, w0, gain_all, bias_all)
    (qkv1,) = qkv_call(False, starts[1], tab, h1, w1, gain_all, bias_all)
    o0, lse0 = attend_call(qkv0, seg)
    o1, lse1 = attend_call(qkv1, seg)
    outs = [o0, o1]
    x1, h2, act, slope = up_call(outs, tokens, bulk, gain_all, bias_all)
    output = finish_call(act, x1, bulk, bias_all, 0, 4)
    du, dw2, dc1, dc2 = down_call(act, slope, cotangent, bulk)
    dh, own1, send1 = hidden_call(tab, h2, du, bulk)
    dx1, do, dwo, dmid = middle_call(outs, dh, cotangent, x1, bulk, gain_all)
    d1 = attend_back_call(qkv1, do, o1, lse1, seg, pairs[0])
    d0 = attend_back_call(qkv0, do, o0, lse0, seg, 0)
    dwq = joint_call(h1, d1, dwo)
    grad_tokens, din = input_call(tab, d0, d1, tokens, dx1, w0, w1, gain_all, 0, 4)
    own_p, send_p = [v[:, :ROWS] for v in weight_call(tab, h1, d0, din, jnp.zeros_like(din), dmid, dc1, dc2)]
    gradq, grado = split_joint(sum_rows(dwq))
    return (
        output,
        grad_tokens,
        join_qkv([reduce_any(own_p, send_p), gradq]),
        grado.reshape(-1),
        reduce_any(own1, send1).reshape(-1),
        sum_rows(dw2).reshape(-1),
        *reduce_small(*small_gradients(din, dmid, dc1, dc2)),
    )


def solution(mesh):
    count, reps = mesh.shape["fsdp"], mesh.shape["rep"]
    inner = Mesh(mesh.devices.reshape(count // 4, 2, 2, reps), FSDP + ("rep",))
    rows = P(FSDP + ("rep",), None)
    flat = P(FSDP)
    return jax.shard_map(
        shards if (count, reps) == (2 * NZ * NX, 2) else shards_any,
        mesh=inner,
        in_specs=(rows, flat, flat, flat, flat, flat, flat, P(FSDP + ("rep",)), rows),
        out_specs=(rows, rows, flat, flat, flat, flat, flat, flat),
        check_vma=False,
    )
```

```python
import functools

import jax
import jax.numpy as jnp
from jax import lax
from jax.experimental import pallas as pl
from jax.experimental.pallas import tpu as pltpu
from jax.sharding import Mesh
from jax.sharding import PartitionSpec as P

D = 768
H = 12
HD = 64
FF = 3072
B16 = jnp.bfloat16
F32 = jnp.float32

epsilon_norm = 1e-06
score_scale = 0.125
masked_low = -1e30

FWD_GROUPS = (4, 8)
NZ, NX = 4, 2
ROWS = D // 16
ROWS2 = FF // 16
FSDP = ("z", "x", "core")


def mm(a, b, ca, cb):
    return lax.dot_general(a, b, (((ca,), (cb,)), ((), ())), preferred_element_type=F32)


def params(mib=56):
    return pltpu.CompilerParams(
        dimension_semantics=("arbitrary",), vmem_limit_bytes=mib * 1024 * 1024
    )


def cost(flops, nbytes, trans=0):
    return pl.CostEstimate(flops=int(flops), bytes_accessed=int(nbytes), transcendentals=int(trans))


def shape(dims, dtype):
    return jax.ShapeDtypeStruct(dims, dtype)


def layer_norm(values, gain, shift):
    center = values - jnp.mean(values, axis=-1, keepdims=True)
    spread = jnp.mean(center * center, axis=-1, keepdims=True)
    return center * lax.rsqrt(spread + epsilon_norm) * gain + shift


def layer_norm_back(values, gain, grad):
    center = values - jnp.mean(values, axis=-1, keepdims=True)
    spread = jnp.mean(center * center, axis=-1, keepdims=True)
    inverse = lax.rsqrt(spread + epsilon_norm)
    hat = center * inverse
    grad_hat = grad * gain
    grad_values = inverse * (
        grad_hat
        - jnp.mean(grad_hat, axis=-1, keepdims=True)
        - hat * jnp.mean(grad_hat * hat, axis=-1, keepdims=True)
    )
    return grad_values, jnp.sum(grad * hat, axis=0, keepdims=True), jnp.sum(grad, axis=0, keepdims=True)


def normal(u):
    bell = jnp.exp(u * u * -0.5)
    t = 1.0 / (1.0 + 0.2316418882663604 * jnp.abs(u))
    top = 0.5307027145
    for c in (-0.7265760135, 0.7107068705, -0.142248368, 0.127414796):
        top = top * t + c
    tail = top * t * bell
    return jnp.where(u < 0.0, tail, 1.0 - tail), bell * 0.3989422804014327


def places(tab, rows):
    core = tab[8]
    for t in range(NZ * NX):
        base = tab[t] * 2
        yield (
            t,
            pl.ds(pl.multiple_of((base + core) * rows, 16), rows),
            pl.ds(pl.multiple_of((base + 1 - core) * rows, 16), rows),
        )


def assemble(tab, parts, dest):
    for t, here, there in places(tab, ROWS):
        rx, rz = divmod(t, NZ)
        dest[here, :] = parts[rx][rz]
        dest[there, :] = parts[2 + rx][rz]


def scatter(tab, source, own, send):
    for t, here, there in places(tab, ROWS):
        own[t] = source[here, :]
        send[t] = source[there, :]


def vector(j):
    return pl.BlockSpec((1, D), lambda *_: (0, j))


def qkv_body(first, at, tab, x_ref, p0, p1, p2, p3, gain, biases, *rest):
    step = pl.program_id(0)
    if first:
        out_ref, h_ref, w_s = rest

        @pl.when(step == 0)
        def _():
            def block(r):
                h_ref[r, :] = layer_norm(x_ref[r, :].astype(F32), gain[...], biases[:, :D]).astype(B16)

            each_block(x_ref.shape[0], 256, block)

        h = h_ref
    else:
        out_ref, w_s = rest
        h = x_ref
    assemble(tab, (p0, p1, p2, p3), w_s)
    bias = [biases[:, part * D + at : part * D + at + w_s.shape[1]] for part in (1, 2)]
    bias = jnp.where(step == 0, bias[0], jnp.where(step == 2, bias[1], 0.0))
    out_ref[0] = (mm(h[...], w_s[...], 1, 0) + bias).astype(B16)


def qkv_call(first, at, tab, x, parts, gains, biases):
    tokens = x.shape[0]
    width = parts[0].shape[2] // 3
    full = pl.BlockSpec((tokens, D), lambda j, t: (0, 0))
    piece = pl.BlockSpec((NZ, ROWS, width), lambda j, t: (0, 0, j))
    outs = [shape((3, tokens, width), B16)]
    out_specs = [pl.BlockSpec((1, tokens, width), lambda j, t: (j, 0, 0))]
    if first:
        outs.append(shape((tokens, D), B16))
        out_specs.append(full)
    return pl.pallas_call(
        functools.partial(qkv_body, first, at),
        grid_spec=pltpu.PrefetchScalarGridSpec(
            num_scalar_prefetch=1,
            grid=(3,),
            in_specs=[full, piece, piece, piece, piece, vector(0), pl.BlockSpec(biases.shape, lambda j, t: (0, 0))],
            out_specs=out_specs,
            scratch_shapes=[pltpu.VMEM((D, width), B16)],
        ),
        out_shape=outs,
        compiler_params=params(),
        cost_estimate=cost(6 * tokens * D * width, 8 * tokens * D),
        name="qkv_first" if first else "qkv_next",
    )(tab, x, *parts, gains, biases)


def each_block(count, rows, run):
    rows = min(rows, count)

    def step(b, carry):
        run(pl.ds(pl.multiple_of(b * rows, rows), rows))
        return carry

    lax.fori_loop(0, count // rows, step, 0)


def make_mask(seg_ref, mask):
    @pl.when(pl.program_id(0) == 0)
    def _():
        row = seg_ref[...].astype(F32)

        def block(r):
            mask[r, :] = jnp.where(seg_ref[:, r].astype(F32).T == row, 0.0, masked_low)

        each_block(seg_ref.shape[1], 128, block)


def attend_body(rows, q_ref, k_ref, v_ref, seg_ref, o_ref, lse_ref, mask):
    make_mask(seg_ref, mask)

    def block(r):
        for h in range(2):
            cols = slice(h * HD, (h + 1) * HD)
            q = q_ref[0, r, cols] * jnp.asarray(score_scale, B16)
            s = mm(q, k_ref[0, :, cols], 1, 1) + mask[r, :]
            top = jnp.max(s, axis=-1, keepdims=True)
            p = jnp.exp(s - top)
            total = jnp.sum(p, axis=-1, keepdims=True)
            o_ref[r, cols] = (mm(p.astype(B16), v_ref[0, :, cols], 1, 0) * (1.0 / total)).astype(B16)
            lse_ref[0, h : h + 1, r] = (top + jnp.log(total)).T

    each_block(q_ref.shape[1], rows, block)


def attend_call(qkv, seg, start=0, pairs=None):
    _, tokens, width = qkv.shape
    pairs = pairs or width // 128
    width = pairs * 128
    head = lambda j: pl.BlockSpec((1, tokens, 128), lambda i: (j, 0, i + start))
    return pl.pallas_call(
        functools.partial(attend_body, min(512, tokens)),
        grid=(pairs,),
        in_specs=[head(0), head(1), head(2), pl.BlockSpec((1, tokens), lambda i: (0, 0))],
        out_specs=[
            pl.BlockSpec((tokens, 128), lambda i: (0, i)),
            pl.BlockSpec((1, 2, tokens), lambda i: (i, 0, 0)),
        ],
        out_shape=[shape((tokens, width), B16), shape((pairs, 2, tokens), F32)],
        scratch_shapes=[pltpu.VMEM((tokens, tokens), F32)],
        compiler_params=params(),
        cost_estimate=cost(pairs * 16 * 128 * tokens * tokens, 8 * tokens * width, pairs * 2 * tokens * tokens),
        name="attend",
    )(qkv, qkv, qkv, seg)


BULK = ROWS2 + 4 * ROWS + ROWS
N16 = 16
SPARE = 16
MIDDLE_ROWS = 256


def up_body(count, *refs):
    outs, (x_ref, wo_ref, wa, wb, wc, wd, gain, biases) = refs[:count], refs[count : count + 8]
    x1_ref, h2_ref, act_ref, slope_ref, w_s = refs[count + 8 :]
    tile = w_s.shape[2]

    @pl.when(pl.program_id(0) == 0)
    def _():
        for f in range(FF // tile):
            w_s[f] = (wa, wb, wc, wd)[f // 2][:, :, (f % 2) * tile : (f % 2 + 1) * tile].reshape(D, tile)

    x1 = x_ref[...].astype(F32) + biases[:, 3 * D : 4 * D]
    wo = wo_ref[...].reshape(D, D)
    at = 0
    for o in outs:
        x1 = x1 + mm(o[...], wo[at : at + o.shape[1], :], 1, 0)
        at += o.shape[1]
    x1_ref[...] = x1
    h2_ref[...] = layer_norm(x1, gain[...], biases[:, 4 * D : 5 * D]).astype(B16)

    def pair(g, carry):
        for f in (2 * g, 2 * g + 1):
            cols = pl.ds(pl.multiple_of(f * tile, 128), tile)
            u = mm(h2_ref[...], w_s[f], 1, 0) + biases[:, pl.ds(pl.multiple_of(5 * D + f * tile, 128), tile)]
            cdf, density = normal(u)
            act_ref[:, cols] = (u * cdf).astype(B16)
            slope_ref[:, cols] = (cdf + u * density).astype(B16)
        return carry

    lax.fori_loop(0, FF // tile // 2, pair, 0)


def bulk_block(j):
    return pl.BlockSpec((N16, ROWS, D), lambda i: (0, j, 0), pipeline_mode=pl.Buffered(1))


def up_call(outs, x, bulk, gains, biases):
    tokens = x.shape[0]
    rows = min(256, tokens)
    block = lambda w: pl.BlockSpec((rows, w), lambda i: (i, 0))
    return pl.pallas_call(
        functools.partial(up_body, len(outs)),
        grid=(tokens // rows,),
        in_specs=[block(o.shape[1]) for o in outs]
        + [block(D)]
        + [bulk_block(j) for j in (8, 4, 5, 6, 7)]
        + [vector(1), pl.BlockSpec(biases.shape, lambda i: (0, 0))],
        out_specs=[block(D), block(D), block(FF), block(FF)],
        out_shape=[shape((tokens, D), F32), shape((tokens, D), B16), shape((tokens, FF), B16), shape((tokens, FF), B16)],
        scratch_shapes=[pltpu.VMEM((8, D, FF // 8), B16)],
        compiler_params=params(),
        cost_estimate=cost(2 * tokens * D * (D + FF), 30 * tokens * D, tokens * FF),
        name="up",
    )(*outs, x, bulk, bulk, bulk, bulk, bulk, gains, biases)


def down_body(act_ref, slope_ref, dy_ref, w_ref, du_ref, dw_ref, dc1, dc2):
    @pl.when(pl.program_id(0) == 0)
    def _():
        dc2[...] = jnp.sum(dy_ref[...].astype(F32), axis=0, keepdims=True)

    dc1[...] = jnp.zeros_like(dc1)

    def block(r):
        du = (mm(dy_ref[r, :], w_ref[...].reshape(D, D), 1, 1) * slope_ref[r, :].astype(F32)).astype(B16)
        du_ref[r, :] = du
        dc1[...] += jnp.sum(du.astype(F32), axis=0, keepdims=True)

    each_block(dy_ref.shape[0], 512, block)
    dw_ref[...] = mm(act_ref[...], dy_ref[...], 0, 0).astype(B16)


def down_call(act, slope, dy, bulk):
    tokens = dy.shape[0]
    ff = pl.BlockSpec((tokens, D), lambda i: (0, i))
    return pl.pallas_call(
        down_body,
        grid=(FF // D,),
        in_specs=[
            ff,
            ff,
            pl.BlockSpec((tokens, D), lambda i: (0, 0)),
            pl.BlockSpec((N16 // 4, ROWS2, D), lambda i: (i, 0, 0)),
        ],
        out_specs=[
            ff,
            pl.BlockSpec((D, D), lambda i: (i, 0)),
            vector_step(),
            pl.BlockSpec((1, D), lambda i: (0, 0)),
        ],
        out_shape=[shape((tokens, FF), B16), shape((FF, D), B16), shape((1, FF), F32), shape((1, D), F32)],
        compiler_params=params(),
        cost_estimate=cost(4 * tokens * D * FF, 30 * tokens * D),
        name="down",
    )(act, slope, dy, bulk)


def vector_step():
    return pl.BlockSpec((1, D), lambda i: (0, i))


def finish_body(act_ref, x1_ref, w_ref, c2, *refs):
    refs[-1][...] = (x1_ref[...] + c2[...] + mm(act_ref[...], w_ref[...].reshape(FF, D), 1, 0)).astype(B16)


def finish_call(act, x1, bulk, biases, start, steps, into=()):
    tokens = x1.shape[0]
    rows = tokens // 4
    block = lambda w: pl.BlockSpec((rows, w), lambda i: (i + start, 0))
    return pl.pallas_call(
        finish_body,
        grid=(steps,),
        in_specs=[
            block(FF),
            block(D),
            pl.BlockSpec((N16, ROWS2, D), lambda i: (0, 0, 0), pipeline_mode=pl.Buffered(1)),
            vector(9),
        ]
        + [pl.BlockSpec(memory_space=pl.ANY)] * len(into),
        out_specs=block(D),
        out_shape=shape((tokens, D), B16),
        input_output_aliases={4: 0} if into else {},
        compiler_params=params(),
        cost_estimate=cost(2 * steps * rows * D * FF, 20 * steps * rows * D),
        name="finish",
    )(act, x1, bulk, biases, *into)


def hidden_body(tab, h2_ref, du_ref, w_ref, acc, own, send, dw):
    @pl.when(pl.program_id(0) == 0)
    def _():
        acc[...] = jnp.zeros_like(acc)

    du = du_ref[...]
    dw[...] = mm(h2_ref[...], du, 0, 0).astype(B16)
    acc[...] += mm(du, w_ref[...].reshape(D, D), 1, 1)
    scatter(tab, dw, own, send)


def hidden_call(tab, h2, du, bulk):
    tokens = h2.shape[0]
    full = pl.BlockSpec((tokens, D), lambda i, t: (0, 0), pipeline_mode=pl.Buffered(1))
    piece = pl.BlockSpec((8, ROWS, D), lambda i, t: (0, 0, i))
    pieces = shape((8, ROWS, FF), B16)
    return pl.pallas_call(
        hidden_body,
        grid_spec=pltpu.PrefetchScalarGridSpec(
            num_scalar_prefetch=1,
            grid=(FF // D,),
            in_specs=[
                full,
                pl.BlockSpec((tokens, D), lambda i, t: (0, i)),
                pl.BlockSpec((N16, ROWS, D), lambda i, t: (0, 4 + i, 0)),
            ],
            out_specs=[pl.BlockSpec((tokens, D), lambda i, t: (0, 0)), piece, piece],
            scratch_shapes=[pltpu.VMEM((D, D), B16)],
        ),
        out_shape=[shape((tokens, D), F32), pieces, pieces],
        compiler_params=params(),
        cost_estimate=cost(4 * tokens * D * FF, 20 * tokens * D),
        name="hidden",
    )(tab, h2, du, bulk)


def middle_body(count, *refs):
    outs, (dh_ref, dy_ref, x1_ref, w_ref, gain) = refs[:count], refs[count : count + 5]
    dx_ref, do_ref, dw_ref, dvec, acc = refs[count + 5 :]
    step = pl.program_id(0)

    @pl.when(step == 0)
    def _():
        acc[...] = jnp.zeros_like(acc)
        dvec[...] = jnp.zeros_like(dvec)

    grad, dgain, dshift = layer_norm_back(x1_ref[...], gain[...], dh_ref[...])
    dx = dy_ref[...].astype(F32) + grad
    dx_ref[...] = dx
    da = dx.astype(B16)
    dvec[0:1, :] += dgain
    dvec[1:2, :] += dshift
    dvec[2:3, :] += jnp.sum(da.astype(F32), axis=0, keepdims=True)
    do_ref[...] = mm(da, w_ref[...].reshape(D, D), 1, 1).astype(B16)
    at = 0
    for o in outs:
        acc[at : at + o.shape[1], :] += mm(o[...], da, 0, 0)
        at += o.shape[1]

    @pl.when(step == pl.num_programs(0) - 1)
    def _():
        dw_ref[...] = acc[...].astype(B16)


def middle_call(outs, dh, dy, x1, bulk, gains):
    tokens = dy.shape[0]
    rows = min(MIDDLE_ROWS, tokens)
    block = lambda w: pl.BlockSpec((rows, w), lambda i: (i, 0))
    return pl.pallas_call(
        functools.partial(middle_body, len(outs)),
        grid=(tokens // rows,),
        in_specs=[block(o.shape[1]) for o in outs] + [block(D)] * 3 + [bulk_block(8), vector(1)],
        out_specs=[
            block(D),
            block(D),
            pl.BlockSpec((D, D), lambda i: (0, 0)),
            pl.BlockSpec((8, D), lambda i: (0, 0)),
        ],
        out_shape=[shape((tokens, D), F32), shape((tokens, D), B16), shape((D, D), B16), shape((8, D), F32)],
        scratch_shapes=[pltpu.VMEM((D, D), F32)],
        compiler_params=params(),
        cost_estimate=cost(4 * tokens * D * D, 20 * tokens * D),
        name="middle",
    )(*outs, dh, dy, x1, bulk, gains)


def attend_back_body(rows, q_ref, k_ref, v_ref, do_ref, o_ref, lse_ref, seg_ref, out_ref, mask, sums):
    make_mask(seg_ref, mask)
    sums[...] = jnp.zeros_like(sums)

    def block(r):
        for h in range(2):
            cols = slice(h * HD, (h + 1) * HD)
            k = k_ref[0, :, cols]
            q = q_ref[0, r, cols] * jnp.asarray(score_scale, B16)
            do = do_ref[r, cols]
            centre = jnp.sum(do.astype(F32) * o_ref[r, cols].astype(F32), axis=1, keepdims=True)
            s = mm(q, k, 1, 1) + mask[r, :]
            p = jnp.exp(s - lse_ref[0, h : h + 1, r].T)
            da = mm(do, v_ref[0, :, cols], 1, 1)
            ds = (p * (da - centre)).astype(B16)
            sums[2 * h + 1] += mm(do.T, p.astype(B16), 1, 0)
            sums[2 * h] += mm(q.T, ds, 1, 0)
            out_ref[0, r, cols] = (mm(ds, k, 1, 0) * score_scale).astype(B16)

    each_block(q_ref.shape[1], rows, block)
    for h in range(2):
        cols = slice(h * HD, (h + 1) * HD)
        out_ref[1, :, cols] = sums[2 * h].T.astype(B16)
        out_ref[2, :, cols] = sums[2 * h + 1].T.astype(B16)


def attend_back_call(qkv, do, o, lse, seg, first_pair):
    _, tokens, width = qkv.shape
    pairs = width // 128
    head = lambda j: pl.BlockSpec((1, tokens, 128), lambda i: (j, 0, i))
    return pl.pallas_call(
        functools.partial(attend_back_body, min(512, tokens)),
        grid=(pairs,),
        in_specs=[
            head(0),
            head(1),
            head(2),
            pl.BlockSpec((tokens, 128), lambda i: (0, i + first_pair)),
            pl.BlockSpec((tokens, 128), lambda i: (0, i)),
            pl.BlockSpec((1, 2, tokens), lambda i: (i, 0, 0)),
            pl.BlockSpec((1, tokens), lambda i: (0, 0)),
        ],
        out_specs=pl.BlockSpec((3, tokens, 128), lambda i: (0, 0, i)),
        out_shape=shape((3, tokens, width), B16),
        scratch_shapes=[pltpu.VMEM((tokens, tokens), F32), pltpu.VMEM((4, HD, tokens), F32)],
        compiler_params=params(),
        cost_estimate=cost(pairs * 40 * 128 * tokens * tokens, 16 * tokens * width, pairs * 2 * tokens * tokens),
        name="attend_back",
    )(qkv, qkv, qkv, do, o, lse, seg)


def weight_body(tab, h_ref, d_ref, din, dmid, dc1, dc2, own, send, dw, line, rows):
    step = pl.program_id(0)

    @pl.when(step == 0)
    def _():
        line[:, :D] = din[0:1, :]
        line[:, D : 2 * D] = dmid[0:1, :]
        for at, piece in ((2, din[1:2, :]), (3, din[2:3, :]), (4, din[3:4, :]), (5, dmid[2:3, :]), (6, dmid[1:2, :])):
            line[:, at * D : (at + 1) * D] = piece
        line[:, 7 * D : 7 * D + FF] = dc1[...]
        line[:, 7 * D + FF :] = dc2[...]
        rows[...] = jnp.zeros_like(rows)
        gains, biases = 2 * D // N16, (6 * D + FF) // N16
        for c in range(N16):
            rows[c : c + 1, :gains] = line[:, c * gains : (c + 1) * gains]
            rows[c : c + 1, gains : gains + biases] = line[:, 2 * D + c * biases : 2 * D + (c + 1) * biases]

    width = d_ref.shape[2]
    dw[...] = mm(h_ref[...], d_ref[0], 0, 0).astype(B16)
    core = tab[8]
    for t, here, there in places(tab, ROWS):
        own[t, :ROWS, :] = dw[here, :]
        send[t, :ROWS, :] = dw[there, :]
    for t in range(NZ * NX):
        base = tab[t] * 2
        for out, row in ((own, base + core), (send, base + 1 - core)):
            picked = rows[pl.ds(row, 1), pl.ds(pl.multiple_of(step * width, 128), width)]
            out[t, ROWS:, :] = jnp.broadcast_to(picked, (SPARE, width)).astype(B16)


def weight_call(tab, h1, dqkv, din, dmid, dc1, dc2):
    _, tokens, width = dqkv.shape
    piece = pl.BlockSpec((8, ROWS + SPARE, width), lambda j, t: (0, 0, j))
    pieces = shape((8, ROWS + SPARE, 3 * width), B16)
    whole = lambda v: pl.BlockSpec(v.shape, lambda j, t: (0, 0))
    return pl.pallas_call(
        weight_body,
        grid_spec=pltpu.PrefetchScalarGridSpec(
            num_scalar_prefetch=1,
            grid=(3,),
            in_specs=[
                pl.BlockSpec((tokens, D), lambda j, t: (0, 0)),
                pl.BlockSpec((1, tokens, width), lambda j, t: (j, 0, 0)),
            ]
            + [whole(v) for v in (din, dmid, dc1, dc2)],
            out_specs=[piece, piece],
            scratch_shapes=[
                pltpu.VMEM((D, width), B16),
                pltpu.VMEM((1, 8 * D + FF), F32),
                pltpu.VMEM((N16, 3 * width), F32),
            ],
        ),
        out_shape=[pieces, pieces],
        compiler_params=params(),
        cost_estimate=cost(6 * tokens * D * width, 12 * tokens * width),
        name="qkv_weight",
    )(tab, h1, dqkv, din, dmid, dc1, dc2)


def joint_body(h_ref, d_ref, o_ref, dw):
    width = d_ref.shape[2]
    dw[:, :width] = mm(h_ref[...], d_ref[0], 0, 0).astype(B16)
    dw[:, width:] = o_ref[...]


def joint_call(h1, dqkv, dwo):
    _, tokens, width = dqkv.shape
    side = D // 3
    return pl.pallas_call(
        joint_body,
        grid=(3,),
        in_specs=[
            pl.BlockSpec((tokens, D), lambda j: (0, 0)),
            pl.BlockSpec((1, tokens, width), lambda j: (j, 0, 0)),
            pl.BlockSpec((D, side), lambda j: (0, j)),
        ],
        out_specs=pl.BlockSpec((D, width + side), lambda j: (0, j)),
        out_shape=shape((D, 3 * (width + side)), B16),
        compiler_params=params(),
        cost_estimate=cost(6 * tokens * D * width, 12 * tokens * width),
        name="joint_weight",
    )(h1, dqkv, dwo)


def split_joint(total):
    side = D // 3
    parts = jnp.split(total, 3, axis=1)
    width = parts[0].shape[1] - side
    return jnp.concatenate([p[:, :width] for p in parts], axis=1), jnp.concatenate([p[:, width:] for p in parts], axis=1)


def input_body(tab, da_ref, db_ref, x_ref, dx_ref, a0, a1, a2, a3, b0, b1, b2, b3, gain, *refs):
    out_ref, dvec, wa, wb = refs[-4:]
    step = pl.program_id(0)

    @pl.when(step == 0)
    def _():
        assemble(tab, (a0, a1, a2, a3), wa)
        assemble(tab, (b0, b1, b2, b3), wb)
        dvec[...] = jnp.zeros_like(dvec)

    dh, at = None, 0
    for d_ref, w in ((da_ref, wa), (db_ref, wb)):
        width = d_ref.shape[2]
        for j in range(3):
            term = mm(d_ref[j], w[:, j * width : (j + 1) * width], 1, 1)
            dh = term if dh is None else dh + term
        for j, row in ((0, 2), (2, 3)):
            dvec[row : row + 1, at : at + width] += jnp.sum(d_ref[j].astype(F32), axis=0, keepdims=True)
        at += width
    grad, dgain, dshift = layer_norm_back(x_ref[...].astype(F32), gain[...], dh)
    out_ref[...] = dx_ref[...] + grad
    dvec[0:1, :] += dgain
    dvec[1:2, :] += dshift


def input_call(tab, da, db, x, dx, parts_a, parts_b, gain):
    tokens = x.shape[0]
    rows = tokens // 4
    wa, wb = da.shape[2], db.shape[2]
    grads = lambda w: pl.BlockSpec((3, rows, w), lambda i, t: (0, i, 0))
    block = pl.BlockSpec((rows, D), lambda i, t: (i, 0))
    piece = lambda w: pl.BlockSpec((NZ, ROWS, 3 * w), lambda i, t: (0, 0, 0), pipeline_mode=pl.Buffered(1))
    return pl.pallas_call(
        input_body,
        grid_spec=pltpu.PrefetchScalarGridSpec(
            num_scalar_prefetch=1,
            grid=(4,),
            in_specs=[grads(wa), grads(wb), block, block]
            + [piece(wa)] * 4
            + [piece(wb)] * 4
            + [vector(0)],
            out_specs=[block, pl.BlockSpec((8, D), lambda i, t: (0, 0))],
            scratch_shapes=[pltpu.VMEM((D, 3 * wa), B16), pltpu.VMEM((D, 3 * wb), B16)],
        ),
        out_shape=[shape((tokens, D), F32), shape((8, D), F32)],
        compiler_params=params(),
        cost_estimate=cost(6 * tokens * D * D, 20 * tokens * D),
        name="input_grad",
    )(tab, da, db, x, dx, *parts_a, *parts_b, gain)


def small_params():
    return pltpu.CompilerParams(vmem_limit_bytes=40 * 1024 * 1024)


def add(a, b):
    return a + b


def stack_body(*refs):
    for i, ref in enumerate(refs[:-1]):
        refs[-1][i] = ref[...]


def stack(parts):
    return pl.pallas_call(
        stack_body,
        out_shape=shape((len(parts), *parts[0].shape), parts[0].dtype),
        compiler_params=small_params(),
        cost_estimate=cost(0, 16 * parts[0].size),
        name="stack",
    )(*parts)


def split_body(grid, a, b, keep, send):
    if grid:
        keep[0] = add(a[0, 0], b[0, 0])
        send[0] = add(a[1, 0], b[1, 0])
    else:
        keep[...] = add(a[0], b[0])
        send[...] = add(a[1], b[1])


def add_split(own, received, grid=True):
    _, r, w = own.shape
    both = pl.BlockSpec((NX, 1, r, w), lambda i: (0, i, 0, 0))
    one = pl.BlockSpec((1, r, w), lambda i: (i, 0, 0))
    how = dict(grid=(NZ,), in_specs=[both, both], out_specs=[one, one], compiler_params=params())
    return pl.pallas_call(
        functools.partial(split_body, grid),
        out_shape=[shape((NZ, r, w), B16)] * 2,
        cost_estimate=cost(8 * r * w, 48 * r * w),
        name="add_split",
        **(how if grid else dict(compiler_params=small_params())),
    )(own.reshape(NX, NZ, r, w), received.reshape(NX, NZ, r, w))


def halves_body(tab, a0, b0, a1, b1, keep, send):
    keep[...] = add(a0[...], b0[...])
    send[...] = add(a1[...], b1[...])


def add_halves(tab, own, received):
    n, r, w = own.shape
    mine = pl.BlockSpec((2, r, w // 2), lambda i, t: (i, 0, t[9]))
    other = pl.BlockSpec((2, r, w // 2), lambda i, t: (i, 0, 1 - t[9]))
    one = pl.BlockSpec((2, r, w // 2), lambda i, t: (i, 0, 0))
    return pl.pallas_call(
        halves_body,
        grid_spec=pltpu.PrefetchScalarGridSpec(
            num_scalar_prefetch=1, grid=(n // 2,), in_specs=[mine, mine, other, other], out_specs=[one, one]
        ),
        out_shape=[shape((n, r, w // 2), B16)] * 2,
        compiler_params=params(),
        cost_estimate=cost(8 * r * w, 48 * r * w),
        name="add_halves",
    )(tab, own, received, own, received)


def vectors_body(tab, p0, p1, p2, p3, gains, biases, rows):
    parts = (p0, p1, p2, p3)
    core = tab[8]
    for t in range(NZ * NX):
        rx, rz = divmod(t, NZ)
        base = tab[t] * 2
        rows[pl.ds(base + core, 1), :] = parts[rx][rz, 0:1, :].astype(F32)
        rows[pl.ds(base + 1 - core, 1), :] = parts[2 + rx][rz, 0:1, :].astype(F32)
    at = 0
    for out in (gains, biases):
        n = out.shape[1] // N16
        for c in range(N16):
            out[:, c * n : (c + 1) * n] = rows[c : c + 1, at : at + n]
        at += n


def read_vectors(tab, parts, ngain, nbias):
    width = parts[0].shape[2]
    part = pl.BlockSpec((NZ, SPARE, width), lambda i, t: (0, ROWS // SPARE, 0))
    whole = lambda n: pl.BlockSpec((1, N16 * n), lambda i, t: (0, 0))
    return pl.pallas_call(
        vectors_body,
        grid_spec=pltpu.PrefetchScalarGridSpec(
            num_scalar_prefetch=1,
            grid=(1,),
            in_specs=[part] * 4,
            out_specs=[whole(ngain), whole(nbias)],
            scratch_shapes=[pltpu.VMEM((N16, width), F32)],
        ),
        out_shape=[shape((1, N16 * ngain), F32), shape((1, N16 * nbias), F32)],
        name="vectors",
    )(tab, *parts)


def parts_body(a, b, *outs):
    for i, out in enumerate(outs):
        out[...] = add(a[i], b[i])


def add_parts(keep, received):
    n, r, w = keep.shape
    return pl.pallas_call(
        parts_body,
        out_shape=[shape((r, w), B16)] * n,
        compiler_params=small_params(),
        cost_estimate=cost(4 * r * w, 24 * r * w),
        name="add_parts",
    )(keep, received)


def four_body(a, b, c, d, out):
    out[...] = ((a[...].astype(F32) + b[...].astype(F32)) + (c[...].astype(F32) + d[...].astype(F32))).astype(B16)


def add_four(parts):
    return pl.pallas_call(
        four_body,
        out_shape=shape(parts[0].shape, B16),
        compiler_params=small_params(),
        cost_estimate=cost(4 * parts[0].size, 10 * parts[0].size),
        name="add_four",
    )(*parts)


def tie(*trees):
    flat, tree = jax.tree.flatten(trees)
    return jax.tree.unflatten(tree, lax.optimization_barrier(flat))


def flip(value, axis, size, by):
    return lax.ppermute(value, axis, [(i, i ^ by) for i in range(size)])


def along_z(value):
    return [flip(value, "z", NZ, by) for by in range(1, NZ)]


def swap_z(parts):
    return [flip(parts[by], "z", NZ, by) for by in range(1, NZ)]


def along_x(value):
    return flip(value, "x", NX, 1)


def across(value):
    return flip(value, "core", 2, 1)


def along_rep(value):
    return flip(value, "rep", 2, 1)


def bounds_of():
    out, at = [], 0
    for heads in FWD_GROUPS:
        out.append((at * HD, (at + heads) * HD))
        at += heads
    return out


def qkv_shards(w_qkv):
    shard = w_qkv.reshape(-1, 3 * D)
    return [jnp.concatenate([shard[:, part * D + a : part * D + b] for part in range(3)], axis=1) for a, b in bounds_of()]


def column_blocks(w):
    return [w[:, j * D : (j + 1) * D] for j in range(w.shape[1] // D)]


def gather_vectors(gains, biases):
    count = 1
    for axis in FSDP:
        count *= lax.axis_size(axis)
    vec = jnp.concatenate([gains, biases])
    vec = lax.all_to_all(
        jnp.broadcast_to(vec[None], (count, vec.shape[0])), FSDP, split_axis=0, concat_axis=0, tiled=True
    ).astype(F32)
    n = gains.shape[0]
    return vec[:, :n].reshape(1, -1), vec[:, n:].reshape(1, -1)


def reduce_small(dgains, dbiases):
    count, reps = 1, lax.axis_size("rep")
    for axis in FSDP:
        count *= lax.axis_size(axis)
    small = jnp.concatenate([dgains.reshape(count, -1), dbiases.reshape(count, -1)], axis=1)
    small = jnp.broadcast_to(small[:, None], (count, reps, small.shape[1])).reshape(count * reps, -1)
    small = lax.all_to_all(small, FSDP + ("rep",), split_axis=0, concat_axis=0, tiled=True)
    small = jnp.sum(small, axis=0)
    n = dgains.shape[0] // count
    return small[:n], small[n:]


def small_gradients(din, dmid, dc1, dc2):
    dgains = jnp.concatenate([din[0], dmid[0]])
    dbiases = jnp.concatenate([din[1], din[2], din[3], dmid[2], dmid[1], dc1[0], dc2[0]])
    return dgains, dbiases


def join_qkv(grads):
    widths = [b - a for a, b in bounds_of()]
    return jnp.concatenate(
        [g[:, part * w : (part + 1) * w] for part in range(3) for g, w in zip(grads, widths)], axis=1
    ).reshape(-1)


def shards(tokens, w_qkv, w_out, w_fc1, w_fc2, gains, biases, segment, cotangent):
    mz, mx, core = lax.axis_index("z"), lax.axis_index("x"), lax.axis_index("core")
    rep = lax.axis_index("rep")
    tab = jnp.stack(
        [((mz ^ rz) * NX + (mx ^ rx)).astype(jnp.int32) for rx in range(NX) for rz in range(NZ)]
        + [core.astype(jnp.int32), rep.astype(jnp.int32)]
    )
    seg = segment.reshape(1, -1)
    pairs = [(b - a) // 128 for a, b in bounds_of()]
    starts = [a for a, _ in bounds_of()]
    s0, s1 = qkv_shards(w_qkv)
    vec = jnp.concatenate([gains, biases]).reshape(1, -1)
    s0 = jnp.concatenate([s0, jnp.pad(vec, ((0, SPARE - 1), (0, s0.shape[1] - vec.shape[1])))])
    bulk = jnp.concatenate([w_fc2.reshape(ROWS2, D), *column_blocks(w_fc1.reshape(ROWS, FF)), w_out.reshape(ROWS, D)])
    bulk = lax.dynamic_slice_in_dim(bulk, rep * (BULK // 2), BULK // 2)
    bulk = lax.all_gather(bulk, FSDP + ("rep",), axis=0, tiled=False).reshape(N16, BULK, D)

    z0 = along_z(s0)
    z0, s1 = tie(z0, s1)
    a0 = stack([s0, *z0])
    x0, c0 = along_x(a0), across(a0)
    z1 = along_z(s1)
    x0, c0 = tie(x0, c0)
    w0 = (a0, x0, c0, across(x0))
    gain_all, bias_all = read_vectors(tab, w0, gains.shape[0], biases.shape[0])
    qkv0, h1 = qkv_call(True, starts[0], tab, tokens, w0, gain_all, bias_all)
    qkv0, z1 = tie(qkv0, z1)
    a1 = stack([s1, *z1])
    x1, c1 = along_x(a1), across(a1)
    o0, lse0 = attend_call(qkv0, seg)
    o0, x1, c1, h1 = tie(o0, x1, c1, h1)
    w1 = (a1, x1, c1, across(x1))
    (qkv1,) = qkv_call(False, starts[1], tab, h1, w1, gain_all, bias_all)
    o1, lse1 = attend_call(qkv1, seg)
    outs = [o0, o1]
    x1, h2, act, slope = up_call(outs, tokens, bulk, gain_all, bias_all)

    du, dw2, dc1, dc2 = down_call(act, slope, cotangent, bulk)
    r2 = lax.psum_scatter(dw2, FSDP, scatter_dimension=0, tiled=True)
    dh, own1, send1 = hidden_call(tab, h2, du, bulk)
    r1 = across(send1)
    dx1, do, dwo, dmid = middle_call(outs, dh, cotangent, x1, bulk, gain_all)
    do, r1 = tie(do, r1)
    keep, give = add_halves(tab, own1, r1)
    do, give = tie(do, give)
    r1 = along_rep(give)
    d1 = attend_back_call(qkv1, do, o1, lse1, seg, pairs[0])
    d1, r1 = tie(d1, r1)
    dwq = joint_call(h1, d1, dwo)
    rq = lax.psum_scatter(dwq, FSDP, scatter_dimension=0, tiled=True)
    keep, give = add_split(keep, r1)
    dwq, give, do = tie(dwq, give, do)
    r1 = along_x(give)
    d0 = attend_back_call(qkv0, do, o0, lse0, seg, 0)
    d0, r1 = tie(d0, r1)
    parts1 = add_parts(keep, r1)
    parts1, d0 = tie(parts1, d0)
    r1 = swap_z(parts1)
    grad_tokens, din = input_call(tab, d0, d1, tokens, dx1, w0, w1, gain_all)
    din, r1, r2 = tie(din, r1, r2)
    total1 = add_four([parts1[0], *r1])
    total1, din, r2 = tie(total1, din, r2)
    y1, y2 = along_rep(total1), along_rep(r2)
    own_p, send_p = weight_call(tab, h1, d0, din, dmid, dc1, dc2)
    send_p, y1, y2 = tie(send_p, y1, y2)
    rp = across(send_p)
    keepp, givep = add_split(own_p, rp, False)
    givep, act = tie(givep, act)
    rp = along_x(givep)
    output = finish_call(act, x1, bulk, bias_all, 0, 2)
    output, rp = tie(output, rp)
    partsp = add_parts(keepp, rp)
    partsp, output = tie(partsp, output)
    rp = swap_z(partsp)
    output = finish_call(act, x1, bulk, bias_all, 2, 2, (output,))
    output, rp, rq = tie(output, rp, rq)
    totalp = add_four([partsp[0], *rp])
    yp, yq = along_rep(totalp), along_rep(rq)
    gradp = totalp.astype(F32) + yp.astype(F32)
    small = gradp[ROWS, : gains.shape[0] + biases.shape[0]]
    gradq, grado = split_joint(rq.astype(F32) + yq.astype(F32))
    grad1 = jnp.where(rep == 0, jnp.concatenate([total1, y1], axis=1), jnp.concatenate([y1, total1], axis=1))
    return (
        output,
        grad_tokens,
        join_qkv([gradp[:ROWS], gradq]),
        grado.reshape(-1),
        grad1.astype(F32).reshape(-1),
        (r2.astype(F32) + y2.astype(F32)).reshape(-1),
        small[: gains.shape[0]],
        small[gains.shape[0] :],
    )


def gather_any(shard):
    whole = lax.all_gather(shard, FSDP, axis=0, tiled=True)
    blocks = whole.reshape(NZ, NX, 2, -1, whole.shape[1]).transpose(2, 1, 0, 3, 4)
    return blocks[0, 0], blocks[0, 1], blocks[1, 0], blocks[1, 1]


def sum_rows(whole):
    part = lax.psum_scatter(whole, FSDP, scatter_dimension=0, tiled=True)
    return lax.psum(part, "rep").astype(F32)


def reduce_any(own, send):
    blocks = jnp.stack([own, send]).reshape(2, NX, NZ, *own.shape[1:]).transpose(2, 1, 0, 3, 4)
    return sum_rows(blocks.reshape(-1, own.shape[2]))


def shards_any(tokens, w_qkv, w_out, w_fc1, w_fc2, gains, biases, segment, cotangent):
    tab = jnp.asarray([rz * NX + rx for rx in range(NX) for rz in range(NZ)] + [0], jnp.int32)
    seg = segment.reshape(1, -1)
    pairs = [(b - a) // 128 for a, b in bounds_of()]
    w0, w1 = [gather_any(s) for s in qkv_shards(w_qkv)]
    lower, wide, out = [
        lax.all_gather(w.reshape(-1, n), FSDP, axis=0, tiled=True) for w, n in ((w_fc2, D), (w_fc1, FF), (w_out, D))
    ]
    bulk = jnp.concatenate([b.reshape(N16, -1, D) for b in (lower, *column_blocks(wide), out)], axis=1)
    gain_all, bias_all = gather_vectors(gains, biases)
    starts = [a for a, _ in bounds_of()]
    qkv0, h1 = qkv_call(True, starts[0], tab, tokens, w0, gain_all, bias_all)
    (qkv1,) = qkv_call(False, starts[1], tab, h1, w1, gain_all, bias_all)
    o0, lse0 = attend_call(qkv0, seg)
    o1, lse1 = attend_call(qkv1, seg)
    outs = [o0, o1]
    x1, h2, act, slope = up_call(outs, tokens, bulk, gain_all, bias_all)
    output = finish_call(act, x1, bulk, bias_all, 0, 4)
    du, dw2, dc1, dc2 = down_call(act, slope, cotangent, bulk)
    dh, own1, send1 = hidden_call(tab, h2, du, bulk)
    dx1, do, dwo, dmid = middle_call(outs, dh, cotangent, x1, bulk, gain_all)
    d1 = attend_back_call(qkv1, do, o1, lse1, seg, pairs[0])
    d0 = attend_back_call(qkv0, do, o0, lse0, seg, 0)
    dwq = joint_call(h1, d1, dwo)
    grad_tokens, din = input_call(tab, d0, d1, tokens, dx1, w0, w1, gain_all)
    own_p, send_p = [v[:, :ROWS] for v in weight_call(tab, h1, d0, din, dmid, dc1, dc2)]
    gradq, grado = split_joint(sum_rows(dwq))
    return (
        output,
        grad_tokens,
        join_qkv([reduce_any(own_p, send_p), gradq]),
        grado.reshape(-1),
        reduce_any(own1, send1).reshape(-1),
        sum_rows(dw2).reshape(-1),
        *reduce_small(*small_gradients(din, dmid, dc1, dc2)),
    )


def solution(mesh):
    count, reps = mesh.shape["fsdp"], mesh.shape["rep"]
    inner = Mesh(mesh.devices.reshape(count // 4, 2, 2, reps), FSDP + ("rep",))
    rows = P(FSDP + ("rep",), None)
    flat = P(FSDP)
    return jax.shard_map(
        shards if (count, reps) == (2 * NZ * NX, 2) else shards_any,
        mesh=inner,
        in_specs=(rows, flat, flat, flat, flat, flat, flat, P(FSDP + ("rep",)), rows),
        out_specs=(rows, rows, flat, flat, flat, flat, flat, flat),
        check_vma=False,
    )
```

```python
import functools

import jax
import jax.numpy as jnp
from jax import lax
from jax.experimental import pallas as pl
from jax.experimental.pallas import tpu as pltpu
from jax.sharding import Mesh
from jax.sharding import PartitionSpec as P

D = 768
H = 12
HD = 64
FF = 3072
B16 = jnp.bfloat16
F32 = jnp.float32

epsilon_norm = 1e-06
score_scale = 0.125
masked_low = -1e30

FWD_GROUPS = (4, 8)
NZ, NX = 4, 2
ROWS = D // 16
ROWS2 = FF // 16
FSDP = ("z", "x", "core")


def mm(a, b, ca, cb):
    return lax.dot_general(a, b, (((ca,), (cb,)), ((), ())), preferred_element_type=F32)


def params(mib=56):
    return pltpu.CompilerParams(
        dimension_semantics=("arbitrary",), vmem_limit_bytes=mib * 1024 * 1024
    )


def cost(flops, nbytes, trans=0):
    return pl.CostEstimate(flops=int(flops), bytes_accessed=int(nbytes), transcendentals=int(trans))


def shape(dims, dtype):
    return jax.ShapeDtypeStruct(dims, dtype)


def layer_norm(values, gain, shift):
    center = values - jnp.mean(values, axis=-1, keepdims=True)
    spread = jnp.mean(center * center, axis=-1, keepdims=True)
    return center * lax.rsqrt(spread + epsilon_norm) * gain + shift


def layer_norm_back(values, gain, grad):
    center = values - jnp.mean(values, axis=-1, keepdims=True)
    spread = jnp.mean(center * center, axis=-1, keepdims=True)
    inverse = lax.rsqrt(spread + epsilon_norm)
    hat = center * inverse
    grad_hat = grad * gain
    grad_values = inverse * (
        grad_hat
        - jnp.mean(grad_hat, axis=-1, keepdims=True)
        - hat * jnp.mean(grad_hat * hat, axis=-1, keepdims=True)
    )
    return grad_values, jnp.sum(grad * hat, axis=0, keepdims=True), jnp.sum(grad, axis=0, keepdims=True)


def normal(u):
    bell = jnp.exp(u * u * -0.5)
    t = 1.0 / (1.0 + 0.2316418882663604 * jnp.abs(u))
    top = 0.5307027145
    for c in (-0.7265760135, 0.7107068705, -0.142248368, 0.127414796):
        top = top * t + c
    tail = top * t * bell
    return jnp.where(u < 0.0, tail, 1.0 - tail), bell * 0.3989422804014327


def places(tab, rows):
    core = tab[8]
    for t in range(NZ * NX):
        base = tab[t] * 2
        yield (
            t,
            pl.ds(pl.multiple_of((base + core) * rows, 16), rows),
            pl.ds(pl.multiple_of((base + 1 - core) * rows, 16), rows),
        )


def assemble(tab, parts, dest):
    for t, here, there in places(tab, ROWS):
        rx, rz = divmod(t, NZ)
        dest[here, :] = parts[rx][rz]
        dest[there, :] = parts[2 + rx][rz]


def scatter(tab, source, own, send):
    for t, here, there in places(tab, ROWS):
        own[t] = source[here, :]
        send[t] = source[there, :]


def vector(j):
    return pl.BlockSpec((1, D), lambda *_: (0, j))


def qkv_body(first, at, tab, x_ref, p0, p1, p2, p3, gain, biases, *rest):
    step = pl.program_id(0)
    if first:
        out_ref, h_ref, w_s = rest

        @pl.when(step == 0)
        def _():
            def block(r):
                h_ref[r, :] = layer_norm(x_ref[r, :].astype(F32), gain[...], biases[:, :D]).astype(B16)

            each_block(x_ref.shape[0], 32, block)

        h = h_ref
    else:
        out_ref, w_s = rest
        h = x_ref
    assemble(tab, (p0, p1, p2, p3), w_s)
    bias = [biases[:, part * D + at : part * D + at + w_s.shape[1]] for part in (1, 2)]
    bias = jnp.where(step == 0, bias[0], jnp.where(step == 2, bias[1], 0.0))
    out_ref[0] = (mm(h[...], w_s[...], 1, 0) + bias).astype(B16)


def qkv_call(first, at, tab, x, parts, gains, biases):
    tokens = x.shape[0]
    width = parts[0].shape[2] // 3
    full = pl.BlockSpec((tokens, D), lambda j, t: (0, 0))
    piece = pl.BlockSpec((NZ, ROWS, width), lambda j, t: (0, 0, j))
    outs = [shape((3, tokens, width), B16)]
    out_specs = [pl.BlockSpec((1, tokens, width), lambda j, t: (j, 0, 0))]
    if first:
        outs.append(shape((tokens, D), B16))
        out_specs.append(full)
    return pl.pallas_call(
        functools.partial(qkv_body, first, at),
        grid_spec=pltpu.PrefetchScalarGridSpec(
            num_scalar_prefetch=1,
            grid=(3,),
            in_specs=[full, piece, piece, piece, piece, vector(0), pl.BlockSpec(biases.shape, lambda j, t: (0, 0))],
            out_specs=out_specs,
            scratch_shapes=[pltpu.VMEM((D, width), B16)],
        ),
        out_shape=outs,
        compiler_params=params(),
        cost_estimate=cost(6 * tokens * D * width, 8 * tokens * D),
        name="qkv_first" if first else "qkv_next",
    )(tab, x, *parts, gains, biases)


def each_block(count, rows, run, unroll=False):
    rows = min(rows, count)
    if unroll:
        for b in range(count // rows):
            run(slice(b * rows, (b + 1) * rows))
        return

    def step(b, carry):
        run(pl.ds(pl.multiple_of(b * rows, rows), rows))
        return carry

    lax.fori_loop(0, count // rows, step, 0)


def make_mask(seg_ref, mask):
    @pl.when(pl.program_id(0) == 0)
    def _():
        row = seg_ref[...].astype(F32)

        def block(r):
            mask[r, :] = jnp.where(seg_ref[:, r].astype(F32).T == row, 0.0, masked_low)

        each_block(seg_ref.shape[1], 128, block)


def attend_body(rows, unroll, q_ref, k_ref, v_ref, seg_ref, o_ref, lse_ref, mask):
    make_mask(seg_ref, mask)

    def block(r):
        for h in range(2):
            cols = slice(h * HD, (h + 1) * HD)
            q = q_ref[0, r, cols] * jnp.asarray(score_scale, B16)
            s = mm(q, k_ref[0, :, cols], 1, 1) + mask[r, :]
            top = jnp.max(s, axis=-1, keepdims=True)
            p = jnp.exp(s - top)
            total = jnp.sum(p, axis=-1, keepdims=True)
            o_ref[r, cols] = (mm(p.astype(B16), v_ref[0, :, cols], 1, 0) * (1.0 / total)).astype(B16)
            lse_ref[0, h : h + 1, r] = (top + jnp.log(total)).T

    each_block(q_ref.shape[1], rows, block, unroll)


def attend_call(qkv, seg, rows, unroll=False, start=0, pairs=None):
    _, tokens, width = qkv.shape
    pairs = pairs or width // 128
    width = pairs * 128
    head = lambda j: pl.BlockSpec((1, tokens, 128), lambda i: (j, 0, i + start))
    return pl.pallas_call(
        functools.partial(attend_body, min(rows, tokens), unroll),
        grid=(pairs,),
        in_specs=[head(0), head(1), head(2), pl.BlockSpec((1, tokens), lambda i: (0, 0))],
        out_specs=[
            pl.BlockSpec((tokens, 128), lambda i: (0, i)),
            pl.BlockSpec((1, 2, tokens), lambda i: (i, 0, 0)),
        ],
        out_shape=[shape((tokens, width), B16), shape((pairs, 2, tokens), F32)],
        scratch_shapes=[pltpu.VMEM((tokens, tokens), F32)],
        compiler_params=params(),
        cost_estimate=cost(pairs * 16 * 128 * tokens * tokens, 8 * tokens * width, pairs * 2 * tokens * tokens),
        name="attend",
    )(qkv, qkv, qkv, seg)


BULK = ROWS2 + 4 * ROWS + ROWS
N16 = 16
SPARE = 16
MIDDLE_ROWS = 256


def up_body(count, *refs):
    outs, (x_ref, wo_ref, wa, wb, wc, wd, gain, biases) = refs[:count], refs[count : count + 8]
    x1_ref, h2_ref, act_ref, slope_ref, w_s = refs[count + 8 :]
    tile = w_s.shape[2]

    @pl.when(pl.program_id(0) == 0)
    def _():
        for f in range(FF // tile):
            w_s[f] = (wa, wb, wc, wd)[f // 2][:, :, (f % 2) * tile : (f % 2 + 1) * tile].reshape(D, tile)

    x1 = x_ref[...].astype(F32) + biases[:, 3 * D : 4 * D]
    wo = wo_ref[...].reshape(D, D)
    at = 0
    for o in outs:
        x1 = x1 + mm(o[...], wo[at : at + o.shape[1], :], 1, 0)
        at += o.shape[1]
    x1_ref[...] = x1
    h2_ref[...] = layer_norm(x1, gain[...], biases[:, 4 * D : 5 * D]).astype(B16)

    def pair(g, carry):
        for f in (2 * g, 2 * g + 1):
            cols = pl.ds(pl.multiple_of(f * tile, 128), tile)
            u = mm(h2_ref[...], w_s[f], 1, 0) + biases[:, pl.ds(pl.multiple_of(5 * D + f * tile, 128), tile)]
            cdf, density = normal(u)
            act_ref[:, cols] = (u * cdf).astype(B16)
            slope_ref[:, cols] = (cdf + u * density).astype(B16)
        return carry

    lax.fori_loop(0, FF // tile // 2, pair, 0)


def bulk_block(j):
    return pl.BlockSpec((N16, ROWS, D), lambda i: (0, j, 0), pipeline_mode=pl.Buffered(1))


def up_call(outs, x, bulk, gains, biases):
    tokens = x.shape[0]
    rows = min(256, tokens)
    block = lambda w: pl.BlockSpec((rows, w), lambda i: (i, 0))
    return pl.pallas_call(
        functools.partial(up_body, len(outs)),
        grid=(tokens // rows,),
        in_specs=[block(o.shape[1]) for o in outs]
        + [block(D)]
        + [bulk_block(j) for j in (8, 4, 5, 6, 7)]
        + [vector(1), pl.BlockSpec(biases.shape, lambda i: (0, 0))],
        out_specs=[block(D), block(D), block(FF), block(FF)],
        out_shape=[shape((tokens, D), F32), shape((tokens, D), B16), shape((tokens, FF), B16), shape((tokens, FF), B16)],
        scratch_shapes=[pltpu.VMEM((8, D, FF // 8), B16)],
        compiler_params=params(),
        cost_estimate=cost(2 * tokens * D * (D + FF), 30 * tokens * D, tokens * FF),
        name="up",
    )(*outs, x, bulk, bulk, bulk, bulk, bulk, gains, biases)


def down_body(act_ref, slope_ref, dy_ref, w_ref, du_ref, dw_ref, dc1, dc2):
    @pl.when(pl.program_id(0) == 0)
    def _():
        dc2[...] = jnp.sum(dy_ref[...].astype(F32), axis=0, keepdims=True)

    dc1[...] = jnp.zeros_like(dc1)

    def block(r):
        du = (mm(dy_ref[r, :], w_ref[...].reshape(D, D), 1, 1) * slope_ref[r, :].astype(F32)).astype(B16)
        du_ref[r, :] = du
        dc1[...] += jnp.sum(du.astype(F32), axis=0, keepdims=True)

    each_block(dy_ref.shape[0], 512, block, True)
    dw_ref[...] = mm(act_ref[...], dy_ref[...], 0, 0).astype(B16)


def down_call(act, slope, dy, bulk):
    tokens = dy.shape[0]
    ff = pl.BlockSpec((tokens, D), lambda i: (0, i))
    return pl.pallas_call(
        down_body,
        grid=(FF // D,),
        in_specs=[
            ff,
            ff,
            pl.BlockSpec((tokens, D), lambda i: (0, 0)),
            pl.BlockSpec((N16 // 4, ROWS2, D), lambda i: (i, 0, 0)),
        ],
        out_specs=[
            ff,
            pl.BlockSpec((D, D), lambda i: (i, 0)),
            vector_step(),
            pl.BlockSpec((1, D), lambda i: (0, 0)),
        ],
        out_shape=[shape((tokens, FF), B16), shape((FF, D), B16), shape((1, FF), F32), shape((1, D), F32)],
        compiler_params=params(),
        cost_estimate=cost(4 * tokens * D * FF, 30 * tokens * D),
        name="down",
    )(act, slope, dy, bulk)


def vector_step():
    return pl.BlockSpec((1, D), lambda i: (0, i))


def finish_body(act_ref, x1_ref, w_ref, c2, *refs):
    refs[-1][...] = (x1_ref[...] + c2[...] + mm(act_ref[...], w_ref[...].reshape(FF, D), 1, 0)).astype(B16)


def finish_call(act, x1, bulk, biases, start, steps, into=()):
    tokens = x1.shape[0]
    rows = tokens // 4
    block = lambda w: pl.BlockSpec((rows, w), lambda i: (i + start, 0))
    return pl.pallas_call(
        finish_body,
        grid=(steps,),
        in_specs=[
            block(FF),
            block(D),
            pl.BlockSpec((N16, ROWS2, D), lambda i: (0, 0, 0), pipeline_mode=pl.Buffered(1)),
            vector(9),
        ]
        + [pl.BlockSpec(memory_space=pl.ANY)] * len(into),
        out_specs=block(D),
        out_shape=shape((tokens, D), B16),
        input_output_aliases={4: 0} if into else {},
        compiler_params=params(),
        cost_estimate=cost(2 * steps * rows * D * FF, 20 * steps * rows * D),
        name="finish",
    )(act, x1, bulk, biases, *into)


def hidden_body(tab, h2_ref, du_ref, w_ref, acc, own, send, dw):
    @pl.when(pl.program_id(0) == 0)
    def _():
        acc[...] = jnp.zeros_like(acc)

    du = du_ref[...]
    dw[...] = mm(h2_ref[...], du, 0, 0).astype(B16)
    acc[...] += mm(du, w_ref[...].reshape(D, D), 1, 1)
    scatter(tab, dw, own, send)


def hidden_call(tab, h2, du, bulk):
    tokens = h2.shape[0]
    full = pl.BlockSpec((tokens, D), lambda i, t: (0, 0), pipeline_mode=pl.Buffered(1))
    piece = pl.BlockSpec((8, ROWS, D), lambda i, t: (0, 0, i))
    pieces = shape((8, ROWS, FF), B16)
    return pl.pallas_call(
        hidden_body,
        grid_spec=pltpu.PrefetchScalarGridSpec(
            num_scalar_prefetch=1,
            grid=(FF // D,),
            in_specs=[
                full,
                pl.BlockSpec((tokens, D), lambda i, t: (0, i)),
                pl.BlockSpec((N16, ROWS, D), lambda i, t: (0, 4 + i, 0)),
            ],
            out_specs=[pl.BlockSpec((tokens, D), lambda i, t: (0, 0)), piece, piece],
            scratch_shapes=[pltpu.VMEM((D, D), B16)],
        ),
        out_shape=[shape((tokens, D), F32), pieces, pieces],
        compiler_params=params(),
        cost_estimate=cost(4 * tokens * D * FF, 20 * tokens * D),
        name="hidden",
    )(tab, h2, du, bulk)


def middle_body(count, *refs):
    outs, (dh_ref, dy_ref, x1_ref, w_ref, gain) = refs[:count], refs[count : count + 5]
    dx_ref, do_ref, dw_ref, dvec, acc = refs[count + 5 :]
    step = pl.program_id(0)

    @pl.when(step == 0)
    def _():
        acc[...] = jnp.zeros_like(acc)
        dvec[...] = jnp.zeros_like(dvec)

    grad, dgain, dshift = layer_norm_back(x1_ref[...], gain[...], dh_ref[...])
    dx = dy_ref[...].astype(F32) + grad
    dx_ref[...] = dx
    da = dx.astype(B16)
    dvec[0:1, :] += dgain
    dvec[1:2, :] += dshift
    dvec[2:3, :] += jnp.sum(da.astype(F32), axis=0, keepdims=True)
    do_ref[...] = mm(da, w_ref[...].reshape(D, D), 1, 1).astype(B16)
    at = 0
    for o in outs:
        acc[at : at + o.shape[1], :] += mm(o[...], da, 0, 0)
        at += o.shape[1]

    @pl.when(step == pl.num_programs(0) - 1)
    def _():
        dw_ref[...] = acc[...].astype(B16)


def middle_call(outs, dh, dy, x1, bulk, gains):
    tokens = dy.shape[0]
    rows = min(MIDDLE_ROWS, tokens)
    block = lambda w: pl.BlockSpec((rows, w), lambda i: (i, 0))
    return pl.pallas_call(
        functools.partial(middle_body, len(outs)),
        grid=(tokens // rows,),
        in_specs=[block(o.shape[1]) for o in outs] + [block(D)] * 3 + [bulk_block(8), vector(1)],
        out_specs=[
            block(D),
            block(D),
            pl.BlockSpec((D, D), lambda i: (0, 0)),
            pl.BlockSpec((8, D), lambda i: (0, 0)),
        ],
        out_shape=[shape((tokens, D), F32), shape((tokens, D), B16), shape((D, D), B16), shape((8, D), F32)],
        scratch_shapes=[pltpu.VMEM((D, D), F32)],
        compiler_params=params(),
        cost_estimate=cost(4 * tokens * D * D, 20 * tokens * D),
        name="middle",
    )(*outs, dh, dy, x1, bulk, gains)


def attend_back_body(rows, q_ref, k_ref, v_ref, do_ref, o_ref, lse_ref, seg_ref, out_ref, mask, sums):
    make_mask(seg_ref, mask)
    sums[...] = jnp.zeros_like(sums)

    def block(r):
        for h in range(2):
            cols = slice(h * HD, (h + 1) * HD)
            k = k_ref[0, :, cols]
            q = q_ref[0, r, cols] * jnp.asarray(score_scale, B16)
            do = do_ref[r, cols]
            centre = jnp.sum(do.astype(F32) * o_ref[r, cols].astype(F32), axis=1, keepdims=True)
            s = mm(q, k, 1, 1) + mask[r, :]
            p = jnp.exp(s - lse_ref[0, h : h + 1, r].T)
            da = mm(do, v_ref[0, :, cols], 1, 1)
            ds = (p * (da - centre)).astype(B16)
            sums[2 * h + 1] += mm(do.T, p.astype(B16), 1, 0)
            sums[2 * h] += mm(q.T, ds, 1, 0)
            out_ref[0, r, cols] = (mm(ds, k, 1, 0) * score_scale).astype(B16)

    each_block(q_ref.shape[1], rows, block)
    for h in range(2):
        cols = slice(h * HD, (h + 1) * HD)
        out_ref[1, :, cols] = sums[2 * h].T.astype(B16)
        out_ref[2, :, cols] = sums[2 * h + 1].T.astype(B16)


def attend_back_call(qkv, do, o, lse, seg, first_pair):
    _, tokens, width = qkv.shape
    pairs = width // 128
    head = lambda j: pl.BlockSpec((1, tokens, 128), lambda i: (j, 0, i))
    return pl.pallas_call(
        functools.partial(attend_back_body, min(512, tokens)),
        grid=(pairs,),
        in_specs=[
            head(0),
            head(1),
            head(2),
            pl.BlockSpec((tokens, 128), lambda i: (0, i + first_pair)),
            pl.BlockSpec((tokens, 128), lambda i: (0, i)),
            pl.BlockSpec((1, 2, tokens), lambda i: (i, 0, 0)),
            pl.BlockSpec((1, tokens), lambda i: (0, 0)),
        ],
        out_specs=pl.BlockSpec((3, tokens, 128), lambda i: (0, 0, i)),
        out_shape=shape((3, tokens, width), B16),
        scratch_shapes=[pltpu.VMEM((tokens, tokens), F32), pltpu.VMEM((4, HD, tokens), F32)],
        compiler_params=params(),
        cost_estimate=cost(pairs * 40 * 128 * tokens * tokens, 16 * tokens * width, pairs * 2 * tokens * tokens),
        name="attend_back",
    )(qkv, qkv, qkv, do, o, lse, seg)


def weight_body(tab, h_ref, d_ref, din, dmid, dc1, dc2, own, send, dw, line, rows):
    step = pl.program_id(0)

    @pl.when(step == 0)
    def _():
        line[:, :D] = din[0:1, :]
        line[:, D : 2 * D] = dmid[0:1, :]
        for at, piece in ((2, din[1:2, :]), (3, din[2:3, :]), (4, din[3:4, :]), (5, dmid[2:3, :]), (6, dmid[1:2, :])):
            line[:, at * D : (at + 1) * D] = piece
        line[:, 7 * D : 7 * D + FF] = dc1[...]
        line[:, 7 * D + FF :] = dc2[...]
        rows[...] = jnp.zeros_like(rows)
        gains, biases = 2 * D // N16, (6 * D + FF) // N16
        for c in range(N16):
            rows[c : c + 1, :gains] = line[:, c * gains : (c + 1) * gains]
            rows[c : c + 1, gains : gains + biases] = line[:, 2 * D + c * biases : 2 * D + (c + 1) * biases]

    width = d_ref.shape[2]
    dw[...] = mm(h_ref[...], d_ref[0], 0, 0).astype(B16)
    core = tab[8]
    for t, here, there in places(tab, ROWS):
        own[t, :ROWS, :] = dw[here, :]
        send[t, :ROWS, :] = dw[there, :]
    for t in range(NZ * NX):
        base = tab[t] * 2
        for out, row in ((own, base + core), (send, base + 1 - core)):
            picked = rows[pl.ds(row, 1), pl.ds(pl.multiple_of(step * width, 128), width)]
            out[t, ROWS:, :] = jnp.broadcast_to(picked, (SPARE, width)).astype(B16)


def weight_call(tab, h1, dqkv, din, dmid, dc1, dc2):
    _, tokens, width = dqkv.shape
    piece = pl.BlockSpec((8, ROWS + SPARE, width), lambda j, t: (0, 0, j))
    pieces = shape((8, ROWS + SPARE, 3 * width), B16)
    whole = lambda v: pl.BlockSpec(v.shape, lambda j, t: (0, 0))
    return pl.pallas_call(
        weight_body,
        grid_spec=pltpu.PrefetchScalarGridSpec(
            num_scalar_prefetch=1,
            grid=(3,),
            in_specs=[
                pl.BlockSpec((tokens, D), lambda j, t: (0, 0)),
                pl.BlockSpec((1, tokens, width), lambda j, t: (j, 0, 0)),
            ]
            + [whole(v) for v in (din, dmid, dc1, dc2)],
            out_specs=[piece, piece],
            scratch_shapes=[
                pltpu.VMEM((D, width), B16),
                pltpu.VMEM((1, 8 * D + FF), F32),
                pltpu.VMEM((N16, 3 * width), F32),
            ],
        ),
        out_shape=[pieces, pieces],
        compiler_params=params(),
        cost_estimate=cost(6 * tokens * D * width, 12 * tokens * width),
        name="qkv_weight",
    )(tab, h1, dqkv, din, dmid, dc1, dc2)


def joint_body(h_ref, d_ref, o_ref, dw):
    width = d_ref.shape[2]
    dw[:, :width] = mm(h_ref[...], d_ref[0], 0, 0).astype(B16)
    dw[:, width:] = o_ref[...]


def joint_call(h1, dqkv, dwo):
    _, tokens, width = dqkv.shape
    side = D // 3
    return pl.pallas_call(
        joint_body,
        grid=(3,),
        in_specs=[
            pl.BlockSpec((tokens, D), lambda j: (0, 0)),
            pl.BlockSpec((1, tokens, width), lambda j: (j, 0, 0)),
            pl.BlockSpec((D, side), lambda j: (0, j)),
        ],
        out_specs=pl.BlockSpec((D, width + side), lambda j: (0, j)),
        out_shape=shape((D, 3 * (width + side)), B16),
        compiler_params=params(),
        cost_estimate=cost(6 * tokens * D * width, 12 * tokens * width),
        name="joint_weight",
    )(h1, dqkv, dwo)


def split_joint(total):
    side = D // 3
    parts = jnp.split(total, 3, axis=1)
    width = parts[0].shape[1] - side
    return jnp.concatenate([p[:, :width] for p in parts], axis=1), jnp.concatenate([p[:, width:] for p in parts], axis=1)


def input_body(tab, da_ref, db_ref, x_ref, dx_ref, a0, a1, a2, a3, b0, b1, b2, b3, gain, *refs):
    out_ref, dvec, wa, wb = refs[-4:]
    step = pl.program_id(0)

    @pl.when(step == 0)
    def _():
        assemble(tab, (a0, a1, a2, a3), wa)
        assemble(tab, (b0, b1, b2, b3), wb)
        dvec[...] = jnp.zeros_like(dvec)

    dh, at = None, 0
    for d_ref, w in ((da_ref, wa), (db_ref, wb)):
        width = d_ref.shape[2]
        for j in range(3):
            term = mm(d_ref[j], w[:, j * width : (j + 1) * width], 1, 1)
            dh = term if dh is None else dh + term
        for j, row in ((0, 2), (2, 3)):
            dvec[row : row + 1, at : at + width] += jnp.sum(d_ref[j].astype(F32), axis=0, keepdims=True)
        at += width
    grad, dgain, dshift = layer_norm_back(x_ref[...].astype(F32), gain[...], dh)
    out_ref[...] = dx_ref[...] + grad
    dvec[0:1, :] += dgain
    dvec[1:2, :] += dshift


def input_call(tab, da, db, x, dx, parts_a, parts_b, gain):
    tokens = x.shape[0]
    rows = tokens // 4
    wa, wb = da.shape[2], db.shape[2]
    grads = lambda w: pl.BlockSpec((3, rows, w), lambda i, t: (0, i, 0))
    block = pl.BlockSpec((rows, D), lambda i, t: (i, 0))
    piece = lambda w: pl.BlockSpec((NZ, ROWS, 3 * w), lambda i, t: (0, 0, 0), pipeline_mode=pl.Buffered(1))
    return pl.pallas_call(
        input_body,
        grid_spec=pltpu.PrefetchScalarGridSpec(
            num_scalar_prefetch=1,
            grid=(4,),
            in_specs=[grads(wa), grads(wb), block, block]
            + [piece(wa)] * 4
            + [piece(wb)] * 4
            + [vector(0)],
            out_specs=[block, pl.BlockSpec((8, D), lambda i, t: (0, 0))],
            scratch_shapes=[pltpu.VMEM((D, 3 * wa), B16), pltpu.VMEM((D, 3 * wb), B16)],
        ),
        out_shape=[shape((tokens, D), F32), shape((8, D), F32)],
        compiler_params=params(),
        cost_estimate=cost(6 * tokens * D * D, 20 * tokens * D),
        name="input_grad",
    )(tab, da, db, x, dx, *parts_a, *parts_b, gain)


def small_params():
    return pltpu.CompilerParams(vmem_limit_bytes=40 * 1024 * 1024)


def add(a, b):
    return a + b


def stack_body(*refs):
    for i, ref in enumerate(refs[:-1]):
        refs[-1][i] = ref[...]


def stack(parts):
    return pl.pallas_call(
        stack_body,
        out_shape=shape((len(parts), *parts[0].shape), parts[0].dtype),
        compiler_params=small_params(),
        cost_estimate=cost(0, 16 * parts[0].size),
        name="stack",
    )(*parts)


def split_body(grid, a, b, keep, send):
    if grid:
        keep[0] = add(a[0, 0], b[0, 0])
        send[0] = add(a[1, 0], b[1, 0])
    else:
        keep[...] = add(a[0], b[0])
        send[...] = add(a[1], b[1])


def add_split(own, received, grid=True):
    _, r, w = own.shape
    both = pl.BlockSpec((NX, 1, r, w), lambda i: (0, i, 0, 0))
    one = pl.BlockSpec((1, r, w), lambda i: (i, 0, 0))
    how = dict(grid=(NZ,), in_specs=[both, both], out_specs=[one, one], compiler_params=params())
    return pl.pallas_call(
        functools.partial(split_body, grid),
        out_shape=[shape((NZ, r, w), B16)] * 2,
        cost_estimate=cost(8 * r * w, 48 * r * w),
        name="add_split",
        **(how if grid else dict(compiler_params=small_params())),
    )(own.reshape(NX, NZ, r, w), received.reshape(NX, NZ, r, w))


def halves_body(tab, a0, b0, a1, b1, keep, send):
    keep[...] = add(a0[...], b0[...])
    send[...] = add(a1[...], b1[...])


def add_halves(tab, own, received):
    n, r, w = own.shape
    mine = pl.BlockSpec((2, r, w // 2), lambda i, t: (i, 0, t[9]))
    other = pl.BlockSpec((2, r, w // 2), lambda i, t: (i, 0, 1 - t[9]))
    one = pl.BlockSpec((2, r, w // 2), lambda i, t: (i, 0, 0))
    return pl.pallas_call(
        halves_body,
        grid_spec=pltpu.PrefetchScalarGridSpec(
            num_scalar_prefetch=1, grid=(n // 2,), in_specs=[mine, mine, other, other], out_specs=[one, one]
        ),
        out_shape=[shape((n, r, w // 2), B16)] * 2,
        compiler_params=params(),
        cost_estimate=cost(8 * r * w, 48 * r * w),
        name="add_halves",
    )(tab, own, received, own, received)


def vectors_body(tab, p0, p1, p2, p3, gains, biases, rows):
    parts = (p0, p1, p2, p3)
    core = tab[8]
    for t in range(NZ * NX):
        rx, rz = divmod(t, NZ)
        base = tab[t] * 2
        rows[pl.ds(base + core, 1), :] = parts[rx][rz, 0:1, :].astype(F32)
        rows[pl.ds(base + 1 - core, 1), :] = parts[2 + rx][rz, 0:1, :].astype(F32)
    at = 0
    for out in (gains, biases):
        n = out.shape[1] // N16
        for c in range(N16):
            out[:, c * n : (c + 1) * n] = rows[c : c + 1, at : at + n]
        at += n


def read_vectors(tab, parts, ngain, nbias):
    width = parts[0].shape[2]
    part = pl.BlockSpec((NZ, SPARE, width), lambda i, t: (0, ROWS // SPARE, 0))
    whole = lambda n: pl.BlockSpec((1, N16 * n), lambda i, t: (0, 0))
    return pl.pallas_call(
        vectors_body,
        grid_spec=pltpu.PrefetchScalarGridSpec(
            num_scalar_prefetch=1,
            grid=(1,),
            in_specs=[part] * 4,
            out_specs=[whole(ngain), whole(nbias)],
            scratch_shapes=[pltpu.VMEM((N16, width), F32)],
        ),
        out_shape=[shape((1, N16 * ngain), F32), shape((1, N16 * nbias), F32)],
        name="vectors",
    )(tab, *parts)


def parts_body(a, b, *outs):
    for i, out in enumerate(outs):
        out[...] = add(a[i], b[i])


def add_parts(keep, received):
    n, r, w = keep.shape
    return pl.pallas_call(
        parts_body,
        out_shape=[shape((r, w), B16)] * n,
        compiler_params=small_params(),
        cost_estimate=cost(4 * r * w, 24 * r * w),
        name="add_parts",
    )(keep, received)


def four_body(a, b, c, d, out):
    out[...] = ((a[...].astype(F32) + b[...].astype(F32)) + (c[...].astype(F32) + d[...].astype(F32))).astype(B16)


def add_four(parts):
    return pl.pallas_call(
        four_body,
        out_shape=shape(parts[0].shape, B16),
        compiler_params=small_params(),
        cost_estimate=cost(4 * parts[0].size, 10 * parts[0].size),
        name="add_four",
    )(*parts)


def tie(*trees):
    flat, tree = jax.tree.flatten(trees)
    return jax.tree.unflatten(tree, lax.optimization_barrier(flat))


def flip(value, axis, size, by):
    return lax.ppermute(value, axis, [(i, i ^ by) for i in range(size)])


def along_z(value):
    return [flip(value, "z", NZ, by) for by in range(1, NZ)]


def swap_z(parts):
    return [flip(parts[by], "z", NZ, by) for by in range(1, NZ)]


def along_x(value):
    return flip(value, "x", NX, 1)


def across(value):
    return flip(value, "core", 2, 1)


def along_rep(value):
    return flip(value, "rep", 2, 1)


def bounds_of():
    out, at = [], 0
    for heads in FWD_GROUPS:
        out.append((at * HD, (at + heads) * HD))
        at += heads
    return out


def qkv_shards(w_qkv):
    shard = w_qkv.reshape(-1, 3 * D)
    return [jnp.concatenate([shard[:, part * D + a : part * D + b] for part in range(3)], axis=1) for a, b in bounds_of()]


def column_blocks(w):
    return [w[:, j * D : (j + 1) * D] for j in range(w.shape[1] // D)]


def gather_vectors(gains, biases):
    count = 1
    for axis in FSDP:
        count *= lax.axis_size(axis)
    vec = jnp.concatenate([gains, biases])
    vec = lax.all_to_all(
        jnp.broadcast_to(vec[None], (count, vec.shape[0])), FSDP, split_axis=0, concat_axis=0, tiled=True
    ).astype(F32)
    n = gains.shape[0]
    return vec[:, :n].reshape(1, -1), vec[:, n:].reshape(1, -1)


def reduce_small(dgains, dbiases):
    count, reps = 1, lax.axis_size("rep")
    for axis in FSDP:
        count *= lax.axis_size(axis)
    small = jnp.concatenate([dgains.reshape(count, -1), dbiases.reshape(count, -1)], axis=1)
    small = jnp.broadcast_to(small[:, None], (count, reps, small.shape[1])).reshape(count * reps, -1)
    small = lax.all_to_all(small, FSDP + ("rep",), split_axis=0, concat_axis=0, tiled=True)
    small = jnp.sum(small, axis=0)
    n = dgains.shape[0] // count
    return small[:n], small[n:]


def small_gradients(din, dmid, dc1, dc2):
    dgains = jnp.concatenate([din[0], dmid[0]])
    dbiases = jnp.concatenate([din[1], din[2], din[3], dmid[2], dmid[1], dc1[0], dc2[0]])
    return dgains, dbiases


def join_qkv(grads):
    widths = [b - a for a, b in bounds_of()]
    return jnp.concatenate(
        [g[:, part * w : (part + 1) * w] for part in range(3) for g, w in zip(grads, widths)], axis=1
    ).reshape(-1)


def shards(tokens, w_qkv, w_out, w_fc1, w_fc2, gains, biases, segment, cotangent):
    mz, mx, core = lax.axis_index("z"), lax.axis_index("x"), lax.axis_index("core")
    rep = lax.axis_index("rep")
    tab = jnp.stack(
        [((mz ^ rz) * NX + (mx ^ rx)).astype(jnp.int32) for rx in range(NX) for rz in range(NZ)]
        + [core.astype(jnp.int32), rep.astype(jnp.int32)]
    )
    seg = segment.reshape(1, -1)
    pairs = [(b - a) // 128 for a, b in bounds_of()]
    starts = [a for a, _ in bounds_of()]
    s0, s1 = qkv_shards(w_qkv)
    vec = jnp.concatenate([gains, biases]).reshape(1, -1)
    s0 = jnp.concatenate([s0, jnp.pad(vec, ((0, SPARE - 1), (0, s0.shape[1] - vec.shape[1])))])
    bulk = jnp.concatenate([w_fc2.reshape(ROWS2, D), *column_blocks(w_fc1.reshape(ROWS, FF)), w_out.reshape(ROWS, D)])
    bulk = lax.dynamic_slice_in_dim(bulk, rep * (BULK // 2), BULK // 2)
    bulk = lax.all_gather(bulk, FSDP + ("rep",), axis=0, tiled=False).reshape(N16, BULK, D)

    z0 = along_z(s0)
    z0, s1 = tie(z0, s1)
    a0 = stack([s0, *z0])
    x0, c0 = along_x(a0), across(a0)
    z1 = along_z(s1)
    x0, c0 = tie(x0, c0)
    w0 = (a0, x0, c0, across(x0))
    gain_all, bias_all = read_vectors(tab, w0, gains.shape[0], biases.shape[0])
    qkv0, h1 = qkv_call(True, starts[0], tab, tokens, w0, gain_all, bias_all)
    qkv0, z1 = tie(qkv0, z1)
    a1 = stack([s1, *z1])
    x1, c1 = along_x(a1), across(a1)
    o0, lse0 = attend_call(qkv0, seg, 128)
    o0, x1, c1, h1 = tie(o0, x1, c1, h1)
    w1 = (a1, x1, c1, across(x1))
    (qkv1,) = qkv_call(False, starts[1], tab, h1, w1, gain_all, bias_all)
    o1, lse1 = attend_call(qkv1, seg, 512, True)
    outs = [o0, o1]
    x1, h2, act, slope = up_call(outs, tokens, bulk, gain_all, bias_all)

    du, dw2, dc1, dc2 = down_call(act, slope, cotangent, bulk)
    r2 = lax.psum_scatter(dw2, FSDP, scatter_dimension=0, tiled=True)
    dh, own1, send1 = hidden_call(tab, h2, du, bulk)
    r1 = across(send1)
    dx1, do, dwo, dmid = middle_call(outs, dh, cotangent, x1, bulk, gain_all)
    do, r1 = tie(do, r1)
    keep, give = add_halves(tab, own1, r1)
    do, give = tie(do, give)
    r1 = along_rep(give)
    d1 = attend_back_call(qkv1, do, o1, lse1, seg, pairs[0])
    d1, r1 = tie(d1, r1)
    dwq = joint_call(h1, d1, dwo)
    rq = lax.psum_scatter(dwq, FSDP, scatter_dimension=0, tiled=True)
    keep, give = add_split(keep, r1)
    dwq, give, do = tie(dwq, give, do)
    r1 = along_x(give)
    d0 = attend_back_call(qkv0, do, o0, lse0, seg, 0)
    d0, r1 = tie(d0, r1)
    parts1 = add_parts(keep, r1)
    parts1, d0 = tie(parts1, d0)
    r1 = swap_z(parts1)
    grad_tokens, din = input_call(tab, d0, d1, tokens, dx1, w0, w1, gain_all)
    din, r1, r2 = tie(din, r1, r2)
    total1 = add_four([parts1[0], *r1])
    total1, din, r2 = tie(total1, din, r2)
    y1, y2 = along_rep(total1), along_rep(r2)
    own_p, send_p = weight_call(tab, h1, d0, din, dmid, dc1, dc2)
    send_p, y1, y2 = tie(send_p, y1, y2)
    rp = across(send_p)
    keepp, givep = add_split(own_p, rp, False)
    givep, act = tie(givep, act)
    rp = along_x(givep)
    output = finish_call(act, x1, bulk, bias_all, 0, 2)
    output, rp = tie(output, rp)
    partsp = add_parts(keepp, rp)
    partsp, output = tie(partsp, output)
    rp = swap_z(partsp)
    output = finish_call(act, x1, bulk, bias_all, 2, 2, (output,))
    output, rp, rq = tie(output, rp, rq)
    totalp = add_four([partsp[0], *rp])
    yp, yq = along_rep(totalp), along_rep(rq)
    gradp = totalp.astype(F32) + yp.astype(F32)
    small = gradp[ROWS, : gains.shape[0] + biases.shape[0]]
    gradq, grado = split_joint(rq.astype(F32) + yq.astype(F32))
    grad1 = jnp.where(rep == 0, jnp.concatenate([total1, y1], axis=1), jnp.concatenate([y1, total1], axis=1))
    return (
        output,
        grad_tokens,
        join_qkv([gradp[:ROWS], gradq]),
        grado.reshape(-1),
        grad1.astype(F32).reshape(-1),
        (r2.astype(F32) + y2.astype(F32)).reshape(-1),
        small[: gains.shape[0]],
        small[gains.shape[0] :],
    )


def gather_any(shard):
    whole = lax.all_gather(shard, FSDP, axis=0, tiled=True)
    blocks = whole.reshape(NZ, NX, 2, -1, whole.shape[1]).transpose(2, 1, 0, 3, 4)
    return blocks[0, 0], blocks[0, 1], blocks[1, 0], blocks[1, 1]


def sum_rows(whole):
    part = lax.psum_scatter(whole, FSDP, scatter_dimension=0, tiled=True)
    return lax.psum(part, "rep").astype(F32)


def reduce_any(own, send):
    blocks = jnp.stack([own, send]).reshape(2, NX, NZ, *own.shape[1:]).transpose(2, 1, 0, 3, 4)
    return sum_rows(blocks.reshape(-1, own.shape[2]))


def shards_any(tokens, w_qkv, w_out, w_fc1, w_fc2, gains, biases, segment, cotangent):
    tab = jnp.asarray([rz * NX + rx for rx in range(NX) for rz in range(NZ)] + [0], jnp.int32)
    seg = segment.reshape(1, -1)
    pairs = [(b - a) // 128 for a, b in bounds_of()]
    w0, w1 = [gather_any(s) for s in qkv_shards(w_qkv)]
    lower, wide, out = [
        lax.all_gather(w.reshape(-1, n), FSDP, axis=0, tiled=True) for w, n in ((w_fc2, D), (w_fc1, FF), (w_out, D))
    ]
    bulk = jnp.concatenate([b.reshape(N16, -1, D) for b in (lower, *column_blocks(wide), out)], axis=1)
    gain_all, bias_all = gather_vectors(gains, biases)
    starts = [a for a, _ in bounds_of()]
    qkv0, h1 = qkv_call(True, starts[0], tab, tokens, w0, gain_all, bias_all)
    (qkv1,) = qkv_call(False, starts[1], tab, h1, w1, gain_all, bias_all)
    o0, lse0 = attend_call(qkv0, seg, 128)
    o1, lse1 = attend_call(qkv1, seg, 512, True)
    outs = [o0, o1]
    x1, h2, act, slope = up_call(outs, tokens, bulk, gain_all, bias_all)
    output = finish_call(act, x1, bulk, bias_all, 0, 4)
    du, dw2, dc1, dc2 = down_call(act, slope, cotangent, bulk)
    dh, own1, send1 = hidden_call(tab, h2, du, bulk)
    dx1, do, dwo, dmid = middle_call(outs, dh, cotangent, x1, bulk, gain_all)
    d1 = attend_back_call(qkv1, do, o1, lse1, seg, pairs[0])
    d0 = attend_back_call(qkv0, do, o0, lse0, seg, 0)
    dwq = joint_call(h1, d1, dwo)
    grad_tokens, din = input_call(tab, d0, d1, tokens, dx1, w0, w1, gain_all)
    own_p, send_p = [v[:, :ROWS] for v in weight_call(tab, h1, d0, din, dmid, dc1, dc2)]
    gradq, grado = split_joint(sum_rows(dwq))
    return (
        output,
        grad_tokens,
        join_qkv([reduce_any(own_p, send_p), gradq]),
        grado.reshape(-1),
        reduce_any(own1, send1).reshape(-1),
        sum_rows(dw2).reshape(-1),
        *reduce_small(*small_gradients(din, dmid, dc1, dc2)),
    )


def solution(mesh):
    count, reps = mesh.shape["fsdp"], mesh.shape["rep"]
    inner = Mesh(mesh.devices.reshape(count // 4, 2, 2, reps), FSDP + ("rep",))
    rows = P(FSDP + ("rep",), None)
    flat = P(FSDP)
    return jax.shard_map(
        shards if (count, reps) == (2 * NZ * NX, 2) else shards_any,
        mesh=inner,
        in_specs=(rows, flat, flat, flat, flat, flat, flat, P(FSDP + ("rep",)), rows),
        out_specs=(rows, rows, flat, flat, flat, flat, flat, flat),
        check_vma=False,
    )
```
